32 devices in a mesh: group: 4 (over z), patch: 8 (over y, x, core).
Axes of the slice: x: 2, y: 2, z: 4, core: 2. Of those that a mesh axis runs over, the one named last changes fastest.
Arguments:
- volume: float32 [4096, 8, 1024], P(('group', 'patch')), may hold values from 0.02 to 18, as said below
- block_place: int32 [4096], P(('group', 'patch')), may hold values from 0 to 4095, as said below
- measured: float32 [2, 512, 384], P(None, 'patch'), may hold values from 0.5 to 5.5
- live_rays: int32 [2, 512], replicated, may hold values from 24 to 48
Outputs:
- final_volume: float32 [4096, 8, 1024], P(('group', 'patch'))
- last_residual: float32 [4, 128, 384], P('group', 'patch')
The draws below stay inside these ranges and needn't reach their ends.
Inputs may be any that keep to these rules, and one draw needn't show every extreme that they name: block_place lists the block positions of the 64 x 64 grid in the order of a Hilbert curve over that grid, begun at a drawn point of the curve (continuing from its end to its start) and turned or mirrored by one of the grid's eight symmetries; each position appears once. `volume`: positive.
All inputs are finite; a program needn't handle non-finite values.
Results may differ from the reference program's by a relative error of at most 0.0007.
Values may be sent and summed in bfloat16 or wider, within the bound.
A program may use at most 192 MiB of HBM per device.

```python
import math
import jax
import jax.numpy as jnp
from jax import lax

NSL = 8
IMG_BLK = 64
BLK_SIDE = 32
RAYS_TILE = 48
NTILE = 64
ANG_SUB = 8
SUBSETS = 2
NBLK = 4096
ROWS = 512
N_GROUP = 4
N_PATCH = 8


def draw_volume(key, part):
    scale_key, texture_key = jax.random.split(jax.random.fold_in(key, 17))
    brightness = jnp.exp(jax.random.uniform(scale_key, (NBLK, 1, 1), jnp.float32, -2.3, 2.3))
    texture = jax.random.uniform(texture_key, (NBLK, NSL, BLK_SIDE * BLK_SIDE), jnp.float32, 0.5, 1.5)
    return brightness * texture


def draw_block_place(key, part):
    symmetry_key, start_key = jax.random.split(jax.random.fold_in(key, 29))
    symmetry = jax.random.randint(symmetry_key, (3,), 0, 2, jnp.int32)
    start = jax.random.randint(start_key, (), 0, NBLK, jnp.int32)
    walk = (jnp.arange(NBLK, dtype=jnp.int32) + start) % NBLK
    column = jnp.zeros((NBLK,), jnp.int32)
    row_pos = jnp.zeros((NBLK,), jnp.int32)
    level = 1
    while level < IMG_BLK:
        right_bit = walk // 2 % 2
        upper_bit = (walk + right_bit) % 2
        upper_bit = jnp.where(right_bit == 1, 1 - walk % 2, walk % 2)
        flipped = (upper_bit == 0) & (right_bit == 1)
        column = jnp.where(flipped, level - 1 - column, column)
        row_pos = jnp.where(flipped, level - 1 - row_pos, row_pos)
        turned = upper_bit == 0
        column, row_pos = (jnp.where(turned, row_pos, column), jnp.where(turned, column, row_pos))
        column = column + level * right_bit
        row_pos = row_pos + level * upper_bit
        walk = walk // 4
        level = level * 2
    column = jnp.where(symmetry[0] == 1, IMG_BLK - 1 - column, column)
    row_pos = jnp.where(symmetry[1] == 1, IMG_BLK - 1 - row_pos, row_pos)
    column, row_pos = (jnp.where(symmetry[2] == 1, row_pos, column), jnp.where(symmetry[2] == 1, column, row_pos))
    return (row_pos * IMG_BLK + column).astype(jnp.int32)


def with_ends(values, key, smallest, largest):
    spot = [jax.random.randint(jax.random.fold_in(key, axis), (), 0, length) for axis, length in enumerate(values.shape)]
    longest = values.shape.index(max(values.shape))
    neighbour = spot[:longest] + [(spot[longest] + 1) % values.shape[longest]] + spot[longest + 1:]
    return values.at[tuple(spot)].set(smallest).at[tuple(neighbour)].set(largest)


def levels(stream_key, dims, shards, low, top_value):
    def one(position, parts):
        steps = jax.random.uniform(jax.random.fold_in(jax.random.fold_in(stream_key, 6), position), (parts,), jnp.float32, low / len(shards), top_value / len(shards))
        return jnp.repeat(jnp.exp(steps), dims[position] // parts).reshape((-1,) + (1,) * (len(dims) - position - 1))

    factor_of = one(*shards[0])
    for cut in shards[1:]:
        factor_of = factor_of * one(*cut)
    return factor_of


def setup_inputs(seed: int = 0) -> dict:
    splits = jax.random.split(jax.random.key(seed), 5)
    volume = draw_volume(jax.random.fold_in(splits[4], 71), 0)
    block_place = draw_block_place(jax.random.fold_in(splits[4], 71), 0)
    measured = jnp.clip(0.5 + 5.0 * jax.random.uniform(splits[2], (SUBSETS, ROWS, RAYS_TILE * NSL), jnp.float32) ** levels(splits[2], (SUBSETS, ROWS, RAYS_TILE * NSL), ((1, 8),), -0.2, 0.2), 0.5, 5.5)
    live_rays = with_ends(jax.random.randint(splits[3], (SUBSETS, ROWS), 24, 49), jax.random.fold_in(splits[3], 1), 24, 48).astype(jnp.int32)
    return {"volume": volume, "block_place": block_place, "measured": measured, "live_rays": live_rays}


spread = 1.5
relax = 0.9


def footprint_tiles(place, angle_value):
    cosine = jnp.cos(angle_value)
    sine_value = jnp.sin(angle_value)
    half_image = IMG_BLK * BLK_SIDE * 0.5
    half_detector = NTILE * RAYS_TILE * 0.5
    block_col = (place % IMG_BLK).astype(jnp.float32) * BLK_SIDE - half_image
    block_row = (place // IMG_BLK).astype(jnp.float32) * BLK_SIDE - half_image
    centre = (block_col + BLK_SIDE * 0.5) * cosine + (block_row + BLK_SIDE * 0.5) * sine_value
    first_tile = jnp.floor((centre + half_detector - RAYS_TILE * 0.5) / RAYS_TILE).astype(jnp.int32)
    voxel = jnp.arange(BLK_SIDE * BLK_SIDE, dtype=jnp.int32)
    offset_col = (voxel % BLK_SIDE).astype(jnp.float32) + 0.5
    offset_row = (voxel // BLK_SIDE).astype(jnp.float32) + 0.5
    along = (block_col[:, None] + offset_col[None, :]) * cosine + (block_row[:, None] + offset_row[None, :]) * sine_value
    ray_ids = first_tile[:, None] * RAYS_TILE + jnp.arange(2 * RAYS_TILE, dtype=jnp.int32)[None, :]
    detector = ray_ids.astype(jnp.float32) + 0.5 - half_detector
    scaled = (along[:, None, :] - detector[:, :, None]) / spread
    bump = jnp.maximum(1.0 - scaled * scaled, 0.0)
    return first_tile, (bump * bump).astype(jnp.bfloat16)


def angle_of(angle, subset):
    return jnp.asarray(math.pi * (angle * SUBSETS + subset) / (ANG_SUB * SUBSETS), jnp.float32)


def tile_rows(angle, first_tile):
    return (angle * NTILE + first_tile[:, None] + jnp.arange(2, dtype=jnp.int32)[None, :]).reshape(-1)


def forward(rounded, place, subset):
    blocks, slices = rounded.shape[0], rounded.shape[1]
    projection = jnp.zeros((ANG_SUB * NTILE, RAYS_TILE * slices), jnp.float32)
    ray_sum = jnp.zeros((ANG_SUB * NTILE, RAYS_TILE), jnp.float32)
    col_sum = jnp.zeros((blocks, BLK_SIDE * BLK_SIDE), jnp.float32)
    for angle in range(ANG_SUB):
        first_tile, footprint = footprint_tiles(place, angle_of(angle, subset))
        row_ids = tile_rows(angle, first_tile)
        contrib = jnp.einsum("brv,bsv->brs", footprint.astype(jnp.float32), rounded.astype(jnp.float32))
        projection = projection.at[row_ids].add(contrib.reshape(2 * blocks, RAYS_TILE * slices))
        ray_part = jnp.sum(footprint.astype(jnp.float32), axis=2)
        ray_sum = ray_sum.at[row_ids].add(ray_part.reshape(2 * blocks, RAYS_TILE))
        col_sum = col_sum + jnp.sum(footprint.astype(jnp.float32), axis=1)
    return projection, ray_sum, col_sum


def backward(residual_b, place, subset):
    blocks = place.shape[0]
    slices = residual_b.shape[1] // RAYS_TILE
    total = jnp.zeros((blocks, slices, BLK_SIDE * BLK_SIDE), jnp.float32)
    for angle in range(ANG_SUB):
        first_tile, footprint = footprint_tiles(place, angle_of(angle, subset))
        picked = residual_b[tile_rows(angle, first_tile)].reshape(blocks, 2 * RAYS_TILE, slices)
        total = total + jnp.einsum("brv,brs->bsv", footprint.astype(jnp.float32), picked.astype(jnp.float32))
    return total


def residual_of(projection, ray_sum, measured_rows, live_count):
    count = projection.shape[0]
    live = (jnp.arange(RAYS_TILE, dtype=jnp.int32)[None, :] < live_count[:, None]).astype(jnp.float32)
    level = projection.reshape(count, RAYS_TILE, -1) / jnp.maximum(ray_sum, 1.0)[:, :, None]
    differ = (measured_rows.reshape(count, RAYS_TILE, -1) - level) * live[:, :, None]
    return differ.reshape(count, -1)


def reference(volume, block_place, measured, live_rays):
    estimate = volume
    slices = volume.shape[1]
    width = RAYS_TILE * slices
    batches = NBLK // 64
    place_groups = block_place.reshape(batches, 64)
    residual = jnp.zeros((ANG_SUB * NTILE, width), jnp.float32)
    for subset in range(SUBSETS):
        rounded = estimate.astype(jnp.bfloat16).reshape(batches, 64, slices, BLK_SIDE * BLK_SIDE)

        def forward_step(totals, member):
            projection, ray_sum, col_sum = forward(member[0], member[1], subset)
            return (totals[0] + projection, totals[1] + ray_sum), col_sum

        start = (jnp.zeros((ANG_SUB * NTILE, width), jnp.float32), jnp.zeros((ANG_SUB * NTILE, RAYS_TILE), jnp.float32))
        totals, col_sums = lax.scan(forward_step, start, (rounded, place_groups))
        col_sum = col_sums.reshape(NBLK, BLK_SIDE * BLK_SIDE)
        residual = residual_of(totals[0], totals[1], measured[subset], live_rays[subset])
        residual_b = residual.astype(jnp.bfloat16)
        backprojected = lax.map(lambda place: backward(residual_b, place, subset), place_groups)
        backprojected = backprojected.reshape(NBLK, slices, BLK_SIDE * BLK_SIDE)
        estimate = jnp.maximum(estimate + relax * backprojected / col_sum[:, None, :], 0.0)
    share_rows = ANG_SUB * NTILE // (N_GROUP * N_PATCH)
    last_residual = residual.reshape(N_PATCH, N_GROUP, share_rows, width).transpose(1, 0, 2, 3)
    return estimate, last_residual.reshape(N_GROUP, N_PATCH * share_rows, width)
```

```python
import math

import jax
import jax.numpy as jnp
import numpy as np
from jax import lax
from jax.experimental import pallas as pl
from jax.experimental.pallas import tpu as pltpu
from jax.sharding import PartitionSpec as P

IMG_BLK = 64
BLK_SIDE = 32
RAYS_TILE = 48
NTILE = 64
ANG_SUB = 8
SUBSETS = 2

spread = 1.5
relax = 0.9

SUB = 8
NQ = (BLK_SIDE // SUB) ** 2
R = 16
VOX = BLK_SIDE * BLK_SIDE
RAYS = NTILE * RAYS_TILE
LANES = 128
PAD = 32
SPAN = 128
TALL = RAYS + SPAN
VMEM_LIMIT = 60 * 1024 * 1024


def angles(subset):
    return [math.pi * (a * SUBSETS + subset) / (ANG_SUB * SUBSETS) for a in range(ANG_SUB)]


def geometry(subset):
    v = np.arange(VOX)
    col = (v % BLK_SIDE) + 0.5 - BLK_SIDE / 2
    row = (v // BLK_SIDE) + 0.5 - BLK_SIDE / 2
    q_of = (v // BLK_SIDE // SUB) * (BLK_SIDE // SUB) + (v % BLK_SIDE) // SUB
    base = np.zeros((ANG_SUB, VOX), np.float64)
    first = np.zeros((ANG_SUB, NQ), np.int64)
    for a, theta in enumerate(angles(subset)):
        off = col * math.cos(theta) + row * math.sin(theta)
        for q in range(NQ):
            mine = q_of == q
            first[a, q] = math.floor(off[mine].min() - spread)
            base[a, mine] = off[mine] - first[a, q]
    return base.astype(np.float32), first.astype(np.int32)


def fill_grid(base_ref, e_scr):
    ray = lax.broadcasted_iota(jnp.int32, (R, VOX), 0).astype(jnp.float32)
    for a in range(ANG_SUB):
        e_scr[a * R:(a + 1) * R, :] = (base_ref[a:a + 1, :] - ray) * (1.0 / spread)


def footprint(t):
    t = t.astype(jnp.bfloat16)
    bump = jnp.maximum(1.0 - t * t, 0.0)
    return bump * bump


TILES = RAYS // SPAN


def list_tiles(win_ref, tiles):
    def step(i, n):
        hit = win_ref[i]
        tiles[n] = i
        return n + hit

    n = lax.fori_loop(0, ANG_SUB * TILES, step, 0, unroll=16)
    tiles[n] = tiles[jnp.maximum(n - 1, 0)]
    return (n + 1) // 2


def over_tiles(tiles, half_count, body):
    def pair(i, c):
        for j in range(2):
            at = tiles[2 * i + j]
            body(at // TILES, lax.rem(at, TILES))
        return c

    lax.fori_loop(0, half_count, pair, 0)


def aligned(x, m):
    return pl.multiple_of(x, m)


def forward_kernel(nb, lo_ref, win_ref, first_ref, vol_ref, frac_ref, grid_ref, out_ref, fold_scr, acc, tiles):
    step = pl.program_id(0)

    @pl.when(step == 0)
    def _():
        zero = jnp.zeros((2 * SPAN, LANES), jnp.float32)

        tiles[ANG_SUB * TILES + 1] = list_tiles(win_ref, tiles)

        def clear(a, i):
            acc[pl.ds(aligned(a * TALL + i * SPAN, SPAN), 2 * SPAN), :] = zero

        over_tiles(tiles, tiles[ANG_SUB * TILES + 1], clear)

    width = SUB * BLK_SIDE
    group = BLK_SIDE // SUB
    slices = vol_ref.shape[1]
    col_group = (lax.broadcasted_iota(jnp.int32, (group * slices, width), 1) % BLK_SIDE) // SUB
    mine = col_group == lax.broadcasted_iota(jnp.int32, (group * slices, width), 0) // slices
    for i in range(nb):
        b = step * nb + i
        parts = []
        for g in range(group):
            at = slice(g * width, (g + 1) * width)
            f = footprint(grid_ref[at, :] + frac_ref[i:i + 1, :])
            wide = jnp.where(mine, jnp.tile(vol_ref[i, :, at], (group, 1)), 0.0)
            parts.append(jnp.dot(wide.astype(jnp.bfloat16), f, preferred_element_type=jnp.float32))
        part = jnp.transpose(jnp.concatenate(parts, axis=0))
        for a in range(ANG_SUB):
            at = pl.ds(a * TALL + PAD + lo_ref[b, a], R)
            acc[at, :] += part[a * R:(a + 1) * R, :]

    @pl.when(step == pl.num_programs(0) - 1)
    def _():
        out_ref[...] = jnp.zeros_like(out_ref)
        span = SPAN
        lane_q = lax.broadcasted_iota(jnp.int32, (span, LANES), 1) // 8
        line_q = lax.broadcasted_iota(jnp.int32, (span // 16, LANES), 1) // 8

        def merge(a, i):
            k = i * span
            total = jnp.zeros((span, LANES), jnp.float32)
            for q in range(NQ):
                src = a * TALL + PAD + k - first_ref[a, q]
                total = jnp.where(lane_q == q, acc[pl.ds(src, span), :], total)
            for s in (64, 32, 16, 8):
                total = total + pltpu.roll(total, s, 1)
            fold_scr[...] = total
            out = fold_scr[pl.ds(0, span // 16, stride=16), :]
            for r in range(1, 16):
                out = jnp.where(line_q == r, fold_scr[pl.ds(r, span // 16, stride=16), :], out)
            out_ref[pl.ds(aligned(a * (RAYS // 16) + i * 8, 8), 8), :] = out

        over_tiles(tiles, tiles[ANG_SUB * TILES + 1], merge)


def backward_kernel(nb, lo_ref, frac_ref, win_ref, first_ref, vol_ref, base_ref, res_ref, out_ref,
                    e_scr, rb, dd, tiles):
    step = pl.program_id(0)

    @pl.when(step == 0)
    def _():
        fill_grid(base_ref, e_scr)
        span = SPAN
        lane_q = lax.broadcasted_iota(jnp.int32, (span, LANES), 1) // 8
        row_j = lax.broadcasted_iota(jnp.int32, (span, LANES), 0) % 16
        pick = lane_q == row_j
        fold = jnp.where(
            lax.broadcasted_iota(jnp.int32, (LANES, LANES), 0) % 8
            == lax.broadcasted_iota(jnp.int32, (LANES, LANES), 1) % 8, 1.0, 0.0).astype(jnp.bfloat16)

        count = list_tiles(win_ref, tiles)

        def widen(a, i):
            rows = res_ref[pl.ds(aligned(a * (RAYS // 16) + i * 8, 8), 8), :]
            wide = jnp.broadcast_to(rows[:, None, :], (8, 16, LANES)).reshape(span, LANES)
            wide = jnp.where(pick, wide, 0.0).astype(jnp.bfloat16)
            rb[pl.ds(aligned(a * TALL + PAD + i * span, 8), span), :] = jnp.dot(
                wide, fold, preferred_element_type=jnp.float32)

        def shift(a, i):
            k = i * span
            total = jnp.zeros((span, LANES), jnp.float32)
            for q in range(NQ):
                src = a * TALL + PAD + k + first_ref[a, q]
                total = jnp.where(lane_q == q, rb[pl.ds(src, span), :], total)
            dd[pl.ds(aligned(a * RAYS + k, span), span), :] = total

        over_tiles(tiles, count, widen)
        over_tiles(tiles, count, shift)

    width = SUB * BLK_SIDE
    group = BLK_SIDE // SUB
    lane = lax.broadcasted_iota(jnp.int32, (8, width), 1)
    col_group = (lane % BLK_SIDE) // SUB

    for i in range(nb):
        b = step * nb + i
        rows = jnp.concatenate(
            [dd[pl.ds(a * RAYS + lo_ref[b, a], R), :] for a in range(ANG_SUB)], axis=0)
        turned = jnp.transpose(rows)
        ones = jnp.ones((8, ANG_SUB * R), jnp.float32)
        for g in range(group):
            lhs = jnp.concatenate([turned[g * 32:(g + 1) * 32], ones], axis=0).astype(jnp.bfloat16)
            at = slice(g * width, (g + 1) * width)
            f = jnp.concatenate(
                [footprint(e_scr[a * R:(a + 1) * R, at] + frac_ref[b, a]) for a in range(ANG_SUB)], axis=0)
            part = jnp.dot(lhs, f, preferred_element_type=jnp.float32)
            back = part[0:8]
            for j in range(1, group):
                back = jnp.where(col_group == j, part[j * 8:(j + 1) * 8], back)
            col_sum = part[32:40]
            out_ref[i, :, at] = jnp.maximum(vol_ref[i, :, at] + relax * back / col_sum, 0.0)


def ray_sum_kernel(c_ref, s_ref, k_ref, out_ref):
    side = IMG_BLK * BLK_SIDE
    half = side * 0.5
    for u in range(c_ref.shape[0]):
        cs = c_ref[u] * (1.0 / spread)
        sn = s_ref[u] * (1.0 / spread)
        inv = 1.0 / cs
        ray = k_ref[u] * (1.0 / spread)

        def row(i, total):
            y = i.astype(jnp.float32) + (0.5 - half)
            w = ray - y * sn
            mid = jnp.clip(jnp.floor(w * inv) + 0.5, 2.5 - half, half - 2.5)
            t0 = mid * cs - w
            for t in (t0 - 2 * cs, t0 - cs, t0, t0 + cs, t0 + 2 * cs):
                bump = jnp.maximum(1.0 - t * t, 0.0)
                total = total + bump * bump
            return total

        out_ref[u] = lax.fori_loop(0, side, row, jnp.zeros(out_ref.shape[1:], jnp.float32), unroll=8)


def exchange_kernel(part_ref, mine_ref, on_ref, rs_ref, full_ref, own_ref,
                    half, inbox, sums, stage, gathered, send_sem, recv_sem,
                    pair_send, pair_recv, out_send, out_recv, back_send, back_recv):
    g, p = lax.axis_index("group"), lax.axis_index("patch")
    groups, pairs = inbox.shape[1], inbox.shape[0]
    n = groups * pairs
    parity, column = lax.rem(p, 2), p // 2
    me = column * groups + g
    partner = (g, column * 2 + 1 - parity)
    mesh_id = pl.DeviceIdType.MESH

    def peer(d):
        at = lax.rem(me + d, n)
        return at // groups, lax.rem(at, groups)

    barrier = pltpu.get_barrier_semaphore()
    pl.semaphore_signal(barrier, inc=1, device_id=partner, device_id_type=mesh_id)

    def greet(d, c):
        pc, pg = peer(d)
        pl.semaphore_signal(barrier, inc=1, device_id=(pg, pc * 2 + parity), device_id_type=mesh_id)
        return c

    lax.fori_loop(1, n, greet, 0)
    pl.semaphore_wait(barrier, n)

    swap = pltpu.make_async_remote_copy(
        src_ref=part_ref.at[:, 1 - parity], dst_ref=half, send_sem=pair_send, recv_sem=pair_recv,
        device_id=partner, device_id_type=mesh_id)
    swap.start()
    swap.wait()
    for i in range(pairs):
        sums[i] = part_ref[i, parity] + half[i]

    def to_owner(d):
        pc, pg = peer(d)
        return pltpu.make_async_remote_copy(
            src_ref=sums.at[pc, pg], dst_ref=inbox.at[column, g], send_sem=send_sem.at[d],
            recv_sem=recv_sem.at[d], device_id=(pg, pc * 2 + parity), device_id_type=mesh_id)

    def go(d, c):
        to_owner(d).start()
        return c

    def done(d, c):
        to_owner(d).wait()
        return c

    lax.fori_loop(1, n, go, 0)
    inbox[column, g] = sums[column, g]
    lax.fori_loop(1, n, done, 0)
    total = jnp.zeros(mine_ref.shape, jnp.float32)
    for i in range(pairs):
        for j in range(groups):
            total = total + inbox[i, j]
    residual = (mine_ref[...] - total / rs_ref[...]) * on_ref[...]
    own_ref[...] = residual
    stage[...] = residual.astype(jnp.bfloat16)

    def to_all(d):
        pc, pg = peer(d)
        return pltpu.make_async_remote_copy(
            src_ref=stage, dst_ref=gathered.at[column, parity, g], send_sem=out_send.at[d],
            recv_sem=out_recv.at[d], device_id=(pg, pc * 2 + parity), device_id_type=mesh_id)

    def go_all(d, c):
        to_all(d).start()
        return c

    def done_all(d, c):
        to_all(d).wait()
        return c

    lax.fori_loop(1, n, go_all, 0)
    gathered[column, parity, g] = stage[...]
    lax.fori_loop(1, n, done_all, 0)
    share = pltpu.make_async_remote_copy(
        src_ref=gathered.at[:, parity], dst_ref=gathered.at[:, parity], send_sem=back_send,
        recv_sem=back_recv, device_id=partner, device_id_type=mesh_id)
    share.start()
    share.wait()
    for i in range(pairs):
        full_ref[i] = gathered[i].astype(jnp.float32)


def exchange(partial, mine, on, rs, groups, patches):
    lines = mine.shape[0]
    pairs = patches // 2
    shape = (pairs, 2, groups, lines, LANES)
    n = pairs * groups
    dma = pltpu.SemaphoreType.DMA
    vmem = pl.BlockSpec(memory_space=pltpu.VMEM)
    full, own = pl.pallas_call(
        exchange_kernel,
        in_specs=[vmem] * 4,
        out_specs=[vmem] * 2,
        out_shape=[jax.ShapeDtypeStruct(shape, jnp.float32),
                   jax.ShapeDtypeStruct((lines, LANES), jnp.float32)],
        scratch_shapes=[pltpu.VMEM((pairs, groups, lines, LANES), jnp.float32),
                        pltpu.VMEM((pairs, groups, lines, LANES), jnp.float32),
                        pltpu.VMEM((pairs, groups, lines, LANES), jnp.float32),
                        pltpu.VMEM((lines, LANES), jnp.bfloat16),
                        pltpu.VMEM(shape, jnp.bfloat16),
                        dma((n,)), dma((n,)), dma, dma, dma((n,)), dma((n,)), dma, dma],
        compiler_params=pltpu.CompilerParams(collective_id=0, has_side_effects=True),
        name="exchange",
    )(partial.reshape(shape), mine, on, rs)
    return full.reshape(partial.shape), own


def smem():
    return pl.BlockSpec(memory_space=pltpu.SMEM)


def forward(volume, lo, frac, win, base, first):
    blocks, slices, _ = volume.shape
    nb = 8
    lines = ANG_SUB * RAYS // 16
    grid = (np.repeat(base, R, axis=0) - np.tile(np.arange(R), ANG_SUB)[:, None]) * (1.0 / spread)
    return pl.pallas_call(
        lambda *refs: forward_kernel(nb, *refs),
        grid=(blocks // nb,),
        in_specs=[smem(), smem(), smem(),
                  pl.BlockSpec((nb, slices, VOX), lambda i: (i, 0, 0)),
                  pl.BlockSpec((nb, LANES), lambda i: (i, 0)),
                  pl.BlockSpec((VOX, LANES), lambda i: (0, 0))],
        out_specs=pl.BlockSpec((lines, LANES), lambda i: (0, 0)),
        out_shape=jax.ShapeDtypeStruct((lines, LANES), jnp.float32),
        scratch_shapes=[pltpu.VMEM((SPAN, LANES), jnp.float32),
                        pltpu.VMEM((ANG_SUB * TALL, LANES), jnp.float32),
                        pltpu.SMEM((ANG_SUB * TILES + 2,), jnp.int32)],
        compiler_params=pltpu.CompilerParams(vmem_limit_bytes=VMEM_LIMIT),
        name="forward",
    )(lo, win, first, volume, jnp.repeat(frac, R, axis=1), grid.T.astype(np.float32))


def backward(volume, residual, lo, frac, win, base, first):
    blocks, slices, _ = volume.shape
    nb = 8
    return pl.pallas_call(
        lambda *refs: backward_kernel(nb, *refs),
        grid=(blocks // nb,),
        in_specs=[smem(), smem(), smem(), smem(),
                  pl.BlockSpec((nb, slices, VOX), lambda i: (i, 0, 0)),
                  pl.BlockSpec((ANG_SUB, VOX), lambda i: (0, 0)),
                  pl.BlockSpec(residual.shape, lambda i: (0, 0))],
        out_specs=pl.BlockSpec((nb, slices, VOX), lambda i: (i, 0, 0)),
        out_shape=jax.ShapeDtypeStruct(volume.shape, jnp.float32),
        scratch_shapes=[pltpu.VMEM((ANG_SUB * R, VOX), jnp.float32),
                        pltpu.VMEM((ANG_SUB * TALL, LANES), jnp.float32),
                        pltpu.VMEM((ANG_SUB * RAYS, LANES), jnp.float32),
                        pltpu.SMEM((ANG_SUB * TILES + 2,), jnp.int32)],
        compiler_params=pltpu.CompilerParams(vmem_limit_bytes=VMEM_LIMIT),
        name="backward",
    )(lo, frac, win, first, volume, base, residual)


def own_ray_sums(first_row, rows):
    count = rows * RAYS_TILE
    padded = -(-count // 1024) * 1024
    idx = jnp.minimum(jnp.arange(padded, dtype=jnp.int32), count - 1)
    row = first_row + idx // RAYS_TILE
    ray = ((row % NTILE) * RAYS_TILE + idx % RAYS_TILE).astype(jnp.float32) + (0.5 - RAYS * 0.5)
    angle = row // NTILE
    big, small = [], []
    for subset in range(SUBSETS):
        th = angles(subset)
        pairs = [sorted((math.cos(t), math.sin(t)), key=abs) for t in th]
        sign = jnp.zeros((padded,), jnp.float32)
        b, s = sign, sign
        for a in range(ANG_SUB):
            b = jnp.where(angle == a, np.float32(pairs[a][1]), b)
            s = jnp.where(angle == a, np.float32(pairs[a][0]), s)
        big.append(b)
        small.append(s)
    shape = (SUBSETS, padded // LANES, LANES)
    big = jnp.stack(big).reshape(shape)
    small = jnp.stack(small).reshape(shape)
    rays = jnp.broadcast_to(ray.reshape(1, padded // LANES, LANES), shape)
    sums = pl.pallas_call(
        ray_sum_kernel,
        out_shape=jax.ShapeDtypeStruct(shape, jnp.float32),
        name="raysum",
    )(big, small, rays)
    return sums.reshape(SUBSETS, padded)[:, :count]


def placing(place, subset):
    half = IMG_BLK * BLK_SIDE * 0.5
    x = (place % IMG_BLK).astype(jnp.float32) * BLK_SIDE + (BLK_SIDE * 0.5 - half)
    y = (place // IMG_BLK).astype(jnp.float32) * BLK_SIDE + (BLK_SIDE * 0.5 - half)
    cosine = np.cos(np.array(angles(subset))).astype(np.float32)
    sine = np.sin(np.array(angles(subset))).astype(np.float32)
    z = x[:, None] * cosine + y[:, None] * sine + (RAYS * 0.5 - 0.5)
    low = jnp.floor(z)
    lo = low.astype(jnp.int32)
    tile = jnp.arange(TILES, dtype=jnp.int32)
    touched = jnp.any(((lo - PAD) // SPAN)[:, :, None] == tile, axis=0)
    touched |= jnp.any(((lo + R + PAD) // SPAN)[:, :, None] == tile, axis=0)
    win = touched.reshape(-1).astype(jnp.int32)
    return lo, (z - low) * (1.0 / spread), win


def shards(volume, block_place, measured, live_rays):
    groups = lax.axis_size("group")
    patches = lax.axis_size("patch")
    group_index = lax.axis_index("group")
    patch_index = lax.axis_index("patch")
    slices = volume.shape[1]
    slab_rows = ANG_SUB * NTILE // patches
    rows = slab_rows // groups
    first_row = patch_index * slab_rows + group_index * rows
    lines = rows * RAYS_TILE * slices // LANES
    per = LANES // slices
    sums = own_ray_sums(first_row, rows)
    estimate = volume
    own_residual = None
    for subset in range(SUBSETS):
        base, first = geometry(subset)
        lo, frac, win = placing(block_place, subset)
        partial = forward(estimate, lo, frac, win, base, first)
        mine = lax.dynamic_slice_in_dim(measured[subset], group_index * rows, rows, 0)
        live = lax.dynamic_slice_in_dim(live_rays[subset], first_row, rows, 0)
        on = jnp.arange(RAYS_TILE, dtype=jnp.int32)[None, :] < live[:, None]
        on = jnp.broadcast_to(on[:, :, None], (rows, RAYS_TILE, slices)).reshape(lines, LANES)
        rs = jnp.maximum(sums[subset], 1.0).reshape(lines, per, 1)
        rs = jnp.broadcast_to(rs, (lines, per, slices)).reshape(lines, LANES)
        full, own = exchange(partial, mine.reshape(lines, LANES), on.astype(jnp.float32), rs, groups, patches)
        own_residual = own.reshape(rows, RAYS_TILE * slices)
        estimate = backward(estimate, full, lo, frac, win, base, first)
    return (estimate, own_residual[None])


def solution(mesh):
    return jax.shard_map(
        shards,
        mesh=mesh,
        in_specs=(
            P(("group", "patch"), None, None),
            P(("group", "patch")),
            P(None, "patch", None),
            P(),
        ),
        out_specs=(P(("group", "patch"), None, None), P("group", "patch", None)),
        check_vma=False,
    )
```

```python
import math

import jax
import jax.numpy as jnp
import numpy as np
from jax import lax
from jax.experimental import pallas as pl
from jax.experimental.pallas import tpu as pltpu
from jax.sharding import PartitionSpec as P

IMG_BLK = 64
BLK_SIDE = 32
RAYS_TILE = 48
NTILE = 64
ANG_SUB = 8
SUBSETS = 2

spread = 1.5
relax = 0.9

SUB = 8
NQ = (BLK_SIDE // SUB) ** 2
R = 16
VOX = BLK_SIDE * BLK_SIDE
RAYS = NTILE * RAYS_TILE
LANES = 128
PAD = 32
SPAN = 128
TALL = RAYS + SPAN
VMEM_LIMIT = 60 * 1024 * 1024


def angles(subset):
    return [math.pi * (a * SUBSETS + subset) / (ANG_SUB * SUBSETS) for a in range(ANG_SUB)]


def geometry(subset):
    v = np.arange(VOX)
    col = (v % BLK_SIDE) + 0.5 - BLK_SIDE / 2
    row = (v // BLK_SIDE) + 0.5 - BLK_SIDE / 2
    q_of = (v // BLK_SIDE // SUB) * (BLK_SIDE // SUB) + (v % BLK_SIDE) // SUB
    base = np.zeros((ANG_SUB, VOX), np.float64)
    first = np.zeros((ANG_SUB, NQ), np.int64)
    for a, theta in enumerate(angles(subset)):
        off = col * math.cos(theta) + row * math.sin(theta)
        for q in range(NQ):
            mine = q_of == q
            first[a, q] = math.floor(off[mine].min() - spread)
            base[a, mine] = off[mine] - first[a, q]
    return base.astype(np.float32), first.astype(np.int32)


def fill_grid(base_ref, e_scr):
    ray = lax.broadcasted_iota(jnp.int32, (R, VOX), 0).astype(jnp.float32)
    for a in range(ANG_SUB):
        e_scr[a * R:(a + 1) * R, :] = (base_ref[a:a + 1, :] - ray) * (1.0 / spread)


def footprint(t):
    t = t.astype(jnp.bfloat16)
    bump = jnp.maximum(1.0 - t * t, 0.0)
    return bump * bump


TILES = RAYS // SPAN


def list_tiles(subset, win_ref, tiles):
    def angle(a, n):
        for i in range(TILES):
            hit = win_ref[subset, a, i]
            tiles[n] = a * TILES + i
            n = n + hit
        return n

    n = lax.fori_loop(0, ANG_SUB, angle, 0)
    tiles[n] = tiles[jnp.maximum(n - 1, 0)]
    return (n + 1) // 2


def over_tiles(tiles, half_count, body):
    def pair(i, c):
        for j in range(2):
            at = tiles[2 * i + j]
            body(at // TILES, lax.rem(at, TILES), j)
        return c

    lax.fori_loop(0, half_count, pair, 0)


def aligned(x, m):
    return pl.multiple_of(x, m)


def forward_kernel(nb, subset, lo_ref, frac_ref, win_ref, first_ref, vol_ref, grid_ref, out_ref,
                   fold_scr, acc, tiles):
    step = pl.program_id(0)

    @pl.when(step == 0)
    def _():
        zero = jnp.zeros((2 * SPAN, LANES), jnp.float32)

        tiles[ANG_SUB * TILES + 1] = list_tiles(subset, win_ref, tiles)

        def clear(a, i, j):
            acc[pl.ds(aligned(a * TALL + i * SPAN, SPAN), 2 * SPAN), :] = zero

        over_tiles(tiles, tiles[ANG_SUB * TILES + 1], clear)

    width = SUB * BLK_SIDE
    group = BLK_SIDE // SUB
    slices = vol_ref.shape[1]
    col_group = (lax.broadcasted_iota(jnp.int32, (group * slices, width), 1) % BLK_SIDE) // SUB
    mine = col_group == lax.broadcasted_iota(jnp.int32, (group * slices, width), 0) // slices
    angle = lax.broadcasted_iota(jnp.int32, (1, LANES), 1) // R
    for i in range(nb):
        b = step * nb + i
        frac = jnp.zeros((1, LANES), jnp.float32)
        for a in range(ANG_SUB):
            frac = jnp.where(angle == a, frac_ref[subset, a, b], frac)
        parts = []
        for g in range(group):
            at = slice(g * width, (g + 1) * width)
            f = footprint(grid_ref[at, :] + frac)
            wide = jnp.where(mine, jnp.tile(vol_ref[i, :, at], (group, 1)), 0.0)
            parts.append(jnp.dot(wide.astype(jnp.bfloat16), f, preferred_element_type=jnp.float32))
        part = jnp.transpose(jnp.concatenate(parts, axis=0))
        for a in range(ANG_SUB):
            at = pl.ds(a * TALL + PAD + lo_ref[subset, a, b], R)
            acc[at, :] += part[a * R:(a + 1) * R, :]

    @pl.when(step == pl.num_programs(0) - 1)
    def _():
        out_ref[...] = jnp.zeros_like(out_ref)
        span = SPAN
        lane_q = lax.broadcasted_iota(jnp.int32, (span, LANES), 1) // 8
        line_q = lax.broadcasted_iota(jnp.int32, (span // 16, LANES), 1) // 8

        def merge(a, i, j):
            k = i * span
            total = jnp.zeros((span, LANES), jnp.float32)
            for q in range(NQ):
                src = a * TALL + PAD + k - first_ref[a, q]
                total = jnp.where(lane_q == q, acc[pl.ds(src, span), :], total)
            fold_scr[j] = total
            rows = [fold_scr[j, pl.ds(r, span // 16, stride=16), :] for r in range(16)]
            for half in (8, 4, 2, 1):
                low = line_q % (2 * half) < half
                rows = [jnp.where(low, rows[r] + pltpu.roll(rows[r], LANES - half * 8, 1),
                                  rows[r + half] + pltpu.roll(rows[r + half], half * 8, 1))
                        for r in range(half)]
            out_ref[pl.ds(aligned(a * (RAYS // 16) + i * 8, 8), 8), :] = rows[0]

        over_tiles(tiles, tiles[ANG_SUB * TILES + 1], merge)


def backward_kernel(nb, subset, lo_ref, frac_ref, win_ref, first_ref, vol_ref, base_ref, res_ref, out_ref,
                    e_scr, rb, dd, tiles):
    step = pl.program_id(0)

    @pl.when(step == 0)
    def _():
        fill_grid(base_ref, e_scr)
        span = SPAN
        lane_q = lax.broadcasted_iota(jnp.int32, (span, LANES), 1) // 8
        row_j = lax.broadcasted_iota(jnp.int32, (span, LANES), 0) % 16
        pick = lane_q == row_j
        fold = jnp.where(
            lax.broadcasted_iota(jnp.int32, (LANES, LANES), 0) % 8
            == lax.broadcasted_iota(jnp.int32, (LANES, LANES), 1) % 8, 1.0, 0.0).astype(jnp.bfloat16)

        count = list_tiles(subset, win_ref, tiles)

        def widen(a, i, j):
            rows = res_ref[pl.ds(aligned(a * (RAYS // 16) + i * 8, 8), 8), :]
            wide = jnp.broadcast_to(rows[:, None, :], (8, 16, LANES)).reshape(span, LANES)
            wide = jnp.where(pick, wide, 0.0).astype(jnp.bfloat16)
            rb[pl.ds(aligned(a * TALL + PAD + i * span, 8), span), :] = jnp.dot(
                wide, fold, preferred_element_type=jnp.float32)

        def shift(a, i, j):
            k = i * span
            total = jnp.zeros((span, LANES), jnp.float32)
            for q in range(NQ):
                src = a * TALL + PAD + k + first_ref[a, q]
                total = jnp.where(lane_q == q, rb[pl.ds(src, span), :], total)
            dd[pl.ds(aligned(a * RAYS + k, span), span), :] = total

        over_tiles(tiles, count, widen)
        over_tiles(tiles, count, shift)

    width = SUB * BLK_SIDE
    group = BLK_SIDE // SUB
    lane = lax.broadcasted_iota(jnp.int32, (8, width), 1)
    col_group = (lane % BLK_SIDE) // SUB

    for i in range(nb):
        b = step * nb + i
        rows = jnp.concatenate(
            [dd[pl.ds(a * RAYS + lo_ref[subset, a, b], R), :] for a in range(ANG_SUB)], axis=0)
        turned = jnp.transpose(rows)
        ones = jnp.ones((8, ANG_SUB * R), jnp.float32)
        for g in range(group):
            lhs = jnp.concatenate([turned[g * 32:(g + 1) * 32], ones], axis=0).astype(jnp.bfloat16)
            at = slice(g * width, (g + 1) * width)
            f = jnp.concatenate(
                [footprint(e_scr[a * R:(a + 1) * R, at] + frac_ref[subset, a, b]) for a in range(ANG_SUB)], axis=0)
            part = jnp.dot(lhs, f, preferred_element_type=jnp.float32)
            back = part[0:8]
            for j in range(1, group):
                back = jnp.where(col_group == j, part[j * 8:(j + 1) * 8], back)
            col_sum = part[32:40]
            out_ref[i, :, at] = jnp.maximum(vol_ref[i, :, at] + relax * back / col_sum, 0.0)


def ray_sums(shape, big, small, inv, ray):
    side = IMG_BLK * BLK_SIDE
    half = side * 0.5
    count = side // 8
    part = lax.broadcasted_iota(jnp.int32, shape, 1) % 8
    start = (part * count).astype(jnp.float32) + (0.5 - half)
    start = ray - start * small

    def row(i, total):
        w = start - i.astype(jnp.float32) * small
        mid = jnp.clip(jnp.floor(w * inv) + 0.5, 2.5 - half, half - 2.5)
        t0 = mid * big - w
        for t in (t0 - 2 * big, t0 - big, t0, t0 + big, t0 + 2 * big):
            bump = jnp.maximum(1.0 - t * t, 0.0)
            total = total + bump * bump
        return total

    total = lax.fori_loop(0, count, row, jnp.zeros(shape, jnp.float32), unroll=4)
    for d in (1, 2, 4):
        total = total + jnp.where(part // d % 2 == 0, pltpu.roll(total, LANES - d, 1), pltpu.roll(total, d, 1))
    return total


def exchange_kernel(subset, part_ref, live_ref, table_ref, meas_ref, full_ref, own_ref,
                    half, inbox, sums, lines_scr, halves, meas, stage, gathered,
                    meas_sem, pair_send, pair_recv, send_sem, recv_sem, rs_send, rs_recv,
                    out_send, out_recv, back_send, back_recv):
    g, p = lax.axis_index("group"), lax.axis_index("patch")
    pairs, groups = inbox.shape[0], inbox.shape[1]
    n = groups * pairs
    lines = stage.shape[0]
    rows = own_ref.shape[0]
    parity, column = lax.rem(p, 2), p // 2
    partner = (g, column * 2 + 1 - parity)
    mesh_id = pl.DeviceIdType.MESH

    def peer(d):
        return lax.rem(column + d // groups, pairs), lax.rem(g + lax.rem(d, groups), groups)

    def source(d):
        return (lax.rem(column + pairs - d // groups, pairs),
                lax.rem(g + groups - lax.rem(d, groups), groups))

    barrier = pltpu.get_barrier_semaphore()
    pl.semaphore_signal(barrier, inc=1, device_id=partner, device_id_type=mesh_id)

    def greet(d, c):
        pc, pg = peer(d)
        pl.semaphore_signal(barrier, inc=1, device_id=(pg, pc * 2 + parity), device_id_type=mesh_id)
        return c

    lax.fori_loop(1, n, greet, 0)
    read = pltpu.make_async_copy(meas_ref.at[subset, pl.ds(g * rows, rows)], meas, meas_sem)
    read.start()
    pl.semaphore_wait(barrier, n)

    def swap(d):
        pc = lax.rem(column + d, pairs)
        return pltpu.make_async_remote_copy(
            src_ref=part_ref.at[pc, 1 - parity], dst_ref=half.at[pc], send_sem=pair_send.at[d],
            recv_sem=pair_recv.at[d], device_id=partner, device_id_type=mesh_id)

    def to_owner(d):
        pc, pg = peer(d)
        return pltpu.make_async_remote_copy(
            src_ref=sums.at[pc, pg], dst_ref=inbox.at[column, g], send_sem=send_sem.at[d],
            recv_sem=recv_sem.at[d], device_id=(pg, pc * 2 + parity), device_id_type=mesh_id)

    def go_swap(d, c):
        swap(d).start()
        return c

    def go_column(i, c):
        pc = lax.rem(column + i, pairs)
        swap(i).wait_recv()
        sums[pc] = part_ref[pc, parity] + half[pc]

        def go(d, c):
            to_owner(d).start()
            return c

        return lax.fori_loop(jnp.maximum(i * groups, 1), (i + 1) * groups, go, c)

    lax.fori_loop(0, pairs, go_swap, 0)
    lax.fori_loop(0, pairs, go_column, 0)

    first_row = (p * groups + g) * rows
    mine = p // pairs
    line = lax.broadcasted_iota(jnp.int32, halves.shape[1:], 0)
    lane = lax.broadcasted_iota(jnp.int32, halves.shape[1:], 1)
    ray = lax.rem(first_row, NTILE) * RAYS_TILE + mine * (lines * 8) + line * 16 + lane // 8
    ray = (ray.astype(jnp.float32) + (0.5 - RAYS * 0.5)) * (1.0 / spread)
    a = first_row // NTILE
    halves[mine] = ray_sums(
        halves.shape[1:], table_ref[subset, 0, a], table_ref[subset, 1, a], table_ref[subset, 2, a], ray)
    trade = pltpu.make_async_remote_copy(
        src_ref=halves.at[mine], dst_ref=halves.at[mine], send_sem=rs_send, recv_sem=rs_recv,
        device_id=(g, lax.rem(p + pairs, 2 * pairs)), device_id_type=mesh_id)
    trade.start()

    def got(d, c):
        to_owner(d).wait_recv()
        return c

    inbox[column, g] = sums[column, g]
    lax.fori_loop(1, n, got, 0)
    total = jnp.zeros(stage.shape, jnp.float32)
    for i in range(pairs):
        for j in range(groups):
            total = total + inbox[i, j]
    lines_scr[...] = total
    read.wait()
    trade.wait()
    at = lax.broadcasted_iota(jnp.int32, (rows, LANES), 0)
    live = jnp.zeros((rows, LANES), jnp.int32)
    for r in range(rows):
        live = jnp.where(at == r, live_ref[subset, first_row + r], live)
    ray = lax.broadcasted_iota(jnp.int32, (rows, LANES), 1) // 8
    wide = lines // rows
    residuals = []
    for c in range(wide):
        sums_c = jnp.concatenate(
            [halves[h, pl.ds(c, rows // 2, stride=wide), :] for h in range(2)], axis=0)
        level = lines_scr[pl.ds(c, rows, stride=wide), :] / jnp.maximum(sums_c, 1.0)
        differ = meas[:, c * LANES:(c + 1) * LANES] - level
        residual = jnp.where(ray + c * 16 < live, differ, 0.0)
        own_ref[:, c * LANES:(c + 1) * LANES] = residual
        residuals.append(residual)
    for c in range(wide):
        lines_scr[pl.ds(c, rows, stride=wide), :] = residuals[c]
    stage[...] = lines_scr[...].astype(jnp.bfloat16)

    def to_all(d):
        pc, pg = peer(d)
        return pltpu.make_async_remote_copy(
            src_ref=stage, dst_ref=gathered.at[column, parity, g], send_sem=out_send.at[d],
            recv_sem=out_recv.at[d], device_id=(pg, pc * 2 + parity), device_id_type=mesh_id)

    def share(d):
        pc, pg = source(d)
        return pltpu.make_async_remote_copy(
            src_ref=gathered.at[pc, parity, pg], dst_ref=gathered.at[pc, parity, pg], send_sem=back_send.at[d],
            recv_sem=back_recv.at[d], device_id=partner, device_id_type=mesh_id)

    def go_all(d, c):
        to_all(d).start()
        return c

    def pass_on(d, c):
        to_all(d).wait_recv()
        share(d).start()
        return c

    def finish(d, c):
        share(d).wait()
        return c

    def sent(d, c):
        to_owner(d).wait_send()
        to_all(d).wait_send()
        return c

    def swapped(d, c):
        swap(d).wait_send()
        return c

    lax.fori_loop(1, n, go_all, 0)
    gathered[column, parity, g] = stage[...]
    share(0).start()
    lax.fori_loop(1, n, pass_on, 0)
    lax.fori_loop(0, n, finish, 0)
    lax.fori_loop(1, n, sent, 0)
    lax.fori_loop(0, pairs, swapped, 0)
    for i in range(pairs):
        full_ref[i] = gathered[i].astype(jnp.float32)


def exchange(subset, partial, live, table, measured, rows, groups, patches):
    pairs = patches // 2
    lines = rows * measured.shape[2] // LANES
    shape = (pairs, 2, groups, lines, LANES)
    n = pairs * groups
    dma = pltpu.SemaphoreType.DMA
    vmem = pl.BlockSpec(memory_space=pltpu.VMEM)
    full, own = pl.pallas_call(
        lambda *refs: exchange_kernel(subset, *refs),
        in_specs=[vmem, smem(), smem(), pl.BlockSpec(memory_space=pl.ANY)],
        out_specs=[vmem] * 2,
        out_shape=[jax.ShapeDtypeStruct(shape, jnp.float32),
                   jax.ShapeDtypeStruct((rows, measured.shape[2]), jnp.float32)],
        scratch_shapes=[pltpu.VMEM((pairs, groups, lines, LANES), jnp.float32),
                        pltpu.VMEM((pairs, groups, lines, LANES), jnp.float32),
                        pltpu.VMEM((pairs, groups, lines, LANES), jnp.float32),
                        pltpu.VMEM((lines, LANES), jnp.float32),
                        pltpu.VMEM((2, lines // 2, LANES), jnp.float32),
                        pltpu.VMEM((rows, measured.shape[2]), jnp.float32),
                        pltpu.VMEM((lines, LANES), jnp.bfloat16),
                        pltpu.VMEM(shape, jnp.bfloat16),
                        dma, dma((pairs,)), dma((pairs,)), dma((n,)), dma((n,)), dma, dma,
                        dma((n,)), dma((n,)), dma((n,)), dma((n,))],
        compiler_params=pltpu.CompilerParams(collective_id=subset, has_side_effects=True),
        name="exchange",
    )(partial.reshape(shape), live, table, measured)
    return full.reshape(partial.shape), own


def smem():
    return pl.BlockSpec(memory_space=pltpu.SMEM)


def forward(subset, volume, lo, frac, win, base, first):
    blocks, slices, _ = volume.shape
    nb = 8
    lines = ANG_SUB * RAYS // 16
    grid = (np.repeat(base, R, axis=0) - np.tile(np.arange(R), ANG_SUB)[:, None]) * (1.0 / spread)
    return pl.pallas_call(
        lambda *refs: forward_kernel(nb, subset, *refs),
        grid=(blocks // nb,),
        in_specs=[smem(), smem(), smem(), smem(),
                  pl.BlockSpec((nb, slices, VOX), lambda i: (i, 0, 0)),
                  pl.BlockSpec((VOX, LANES), lambda i: (0, 0))],
        out_specs=pl.BlockSpec((lines, LANES), lambda i: (0, 0)),
        out_shape=jax.ShapeDtypeStruct((lines, LANES), jnp.float32),
        scratch_shapes=[pltpu.VMEM((2, SPAN, LANES), jnp.float32),
                        pltpu.VMEM((ANG_SUB * TALL, LANES), jnp.float32),
                        pltpu.SMEM((ANG_SUB * TILES + 2,), jnp.int32)],
        compiler_params=pltpu.CompilerParams(vmem_limit_bytes=VMEM_LIMIT),
        name="forward",
    )(lo, frac, win, first, volume, grid.T.astype(np.float32))


def backward(subset, volume, residual, lo, frac, win, base, first):
    blocks, slices, _ = volume.shape
    nb = 8
    return pl.pallas_call(
        lambda *refs: backward_kernel(nb, subset, *refs),
        grid=(blocks // nb,),
        in_specs=[smem(), smem(), smem(), smem(),
                  pl.BlockSpec((nb, slices, VOX), lambda i: (i, 0, 0)),
                  pl.BlockSpec((ANG_SUB, VOX), lambda i: (0, 0)),
                  pl.BlockSpec(residual.shape, lambda i: (0, 0))],
        out_specs=pl.BlockSpec((nb, slices, VOX), lambda i: (i, 0, 0)),
        out_shape=jax.ShapeDtypeStruct(volume.shape, jnp.float32),
        scratch_shapes=[pltpu.VMEM((ANG_SUB * R, VOX), jnp.float32),
                        pltpu.VMEM((ANG_SUB * TALL, LANES), jnp.float32),
                        pltpu.VMEM((ANG_SUB * RAYS, LANES), jnp.float32),
                        pltpu.SMEM((ANG_SUB * TILES + 2,), jnp.int32)],
        compiler_params=pltpu.CompilerParams(vmem_limit_bytes=VMEM_LIMIT),
        name="backward",
    )(lo, frac, win, first, volume, base, residual)


def ray_table():
    table = np.zeros((SUBSETS, 3, ANG_SUB), np.float64)
    for subset in range(SUBSETS):
        for a, t in enumerate(angles(subset)):
            small, big = sorted((abs(math.cos(t)), abs(math.sin(t))))
            table[subset, :, a] = big / spread, small / spread, spread / big
    return table.astype(np.float32)


def placing(place):
    half = IMG_BLK * BLK_SIDE * 0.5
    x = (place % IMG_BLK).astype(jnp.float32) * BLK_SIDE + (BLK_SIDE * 0.5 - half)
    y = (place // IMG_BLK).astype(jnp.float32) * BLK_SIDE + (BLK_SIDE * 0.5 - half)
    theta = np.array([angles(subset) for subset in range(SUBSETS)])
    cosine = np.cos(theta).astype(np.float32)[:, :, None]
    sine = np.sin(theta).astype(np.float32)[:, :, None]
    z = x * cosine + y * sine + (RAYS * 0.5 - 0.5)
    low = jnp.floor(z)
    lo = low.astype(jnp.int32)
    tile = jnp.arange(TILES, dtype=jnp.int32)[:, None]
    near = ((lo - PAD) // SPAN)[:, :, None, :] == tile
    near |= ((lo + R + PAD) // SPAN)[:, :, None, :] == tile
    return lo, (z - low) * (1.0 / spread), jnp.any(near, axis=3).astype(jnp.int32)


def shards(volume, block_place, measured, live_rays):
    groups = lax.axis_size("group")
    patches = lax.axis_size("patch")
    rows = ANG_SUB * NTILE // patches // groups
    lo, frac, win = placing(block_place)
    table = ray_table()
    estimate = volume
    own = None
    for subset in range(SUBSETS):
        base, first = geometry(subset)
        partial = forward(subset, estimate, lo, frac, win, base, first)
        full, own = exchange(subset, partial, live_rays, table, measured, rows, groups, patches)
        estimate = backward(subset, estimate, full, lo, frac, win, base, first)
    return (estimate, own[None])


def solution(mesh):
    return jax.shard_map(
        shards,
        mesh=mesh,
        in_specs=(
            P(("group", "patch"), None, None),
            P(("group", "patch")),
            P(None, "patch", None),
            P(),
        ),
        out_specs=(P(("group", "patch"), None, None), P("group", "patch", None)),
        check_vma=False,
    )
```

```python
import math

import jax
import jax.numpy as jnp
import numpy as np
from jax import lax
from jax.experimental import pallas as pl
from jax.experimental.pallas import tpu as pltpu
from jax.sharding import PartitionSpec as P

IMG_BLK = 64
BLK_SIDE = 32
RAYS_TILE = 48
NTILE = 64
ANG_SUB = 8
SUBSETS = 2

spread = 1.5
relax = 0.9

SUB = 8
NQ = (BLK_SIDE // SUB) ** 2
R = 16
VOX = BLK_SIDE * BLK_SIDE
RAYS = NTILE * RAYS_TILE
LANES = 128
PAD = 32
SPAN = 128
TALL = RAYS + SPAN
VMEM_LIMIT = 60 * 1024 * 1024


def angles(subset):
    return [math.pi * (a * SUBSETS + subset) / (ANG_SUB * SUBSETS) for a in range(ANG_SUB)]


def geometry(subset):
    v = np.arange(VOX)
    col = (v % BLK_SIDE) + 0.5 - BLK_SIDE / 2
    row = (v // BLK_SIDE) + 0.5 - BLK_SIDE / 2
    q_of = (v // BLK_SIDE // SUB) * (BLK_SIDE // SUB) + (v % BLK_SIDE) // SUB
    base = np.zeros((ANG_SUB, VOX), np.float64)
    first = np.zeros((ANG_SUB, NQ), np.int64)
    for a, theta in enumerate(angles(subset)):
        off = col * math.cos(theta) + row * math.sin(theta)
        for q in range(NQ):
            mine = q_of == q
            first[a, q] = math.floor(off[mine].min() - spread)
            base[a, mine] = off[mine] - first[a, q]
    return base.astype(np.float32), first.astype(np.int32)


def fill_grid(base_ref, e_scr):
    ray = lax.broadcasted_iota(jnp.int32, (R, VOX), 0).astype(jnp.float32)
    for a in range(ANG_SUB):
        e_scr[a * R:(a + 1) * R, :] = (base_ref[a:a + 1, :] - ray) * (1.0 / spread)


def footprint(t):
    t = t.astype(jnp.bfloat16)
    bump = jnp.maximum(1.0 - t * t, 0.0)
    return bump * bump


TILES = RAYS // SPAN


WIDE = 4


def list_tiles(subset, win_ref, tiles, starts):
    def angle(a, n):
        starts[a] = n
        for i in range(TILES):
            hit = win_ref[0, (subset * ANG_SUB + a) * TILES + i]
            tiles[n] = a * TILES + i
            n = n + hit
        return n

    starts[ANG_SUB] = lax.fori_loop(0, ANG_SUB, angle, 0)


def over_tiles(tiles, starts, body):
    n = starts[ANG_SUB]

    def some(i, c):
        for j in range(WIDE):
            t = jnp.minimum(WIDE * i + j, n - 1)
            body(t, tiles[t])
        return c

    lax.fori_loop(0, (n + WIDE - 1) // WIDE, some, 0)


def over_angle(a, tiles, starts, body):
    def one(t, c):
        body(t, tiles[t] - a * TILES)
        return c

    lax.fori_loop(starts[a], starts[a + 1], one, 0)


def shifted(ref, base, offsets, lane_q):
    fine = [o % 8 for o in offsets]
    coarse = [o // 8 for o in offsets]
    low, high = min(coarse), max(coarse)

    def member(values, value):
        hits = [lane_q == q for q, v in enumerate(values) if v == value]
        mask = hits[0]
        for h in hits[1:]:
            mask = mask | h
        return mask

    rows = None
    for f in sorted(set(fine)):
        part = ref[pl.ds(base + 8 * low + f, SPAN + 8 * (high - low)), :]
        rows = part if rows is None else jnp.where(member(fine, f), part, rows)
    out = None
    for c in sorted(set(coarse)):
        part = rows[8 * (c - low):8 * (c - low) + SPAN]
        out = part if out is None else jnp.where(member(coarse, c), part, out)
    return out


def spread_lanes(x, lane_q):
    rows = [x]
    for half in (8, 4, 2, 1):
        low = lane_q % (2 * half) < half
        turned = [pltpu.roll(x, half * 8, 1) for x in rows]
        rows = ([jnp.where(low, x, y) for x, y in zip(rows, turned)]
                + [jnp.where(low, y, x) for x, y in zip(rows, turned)])
    return [rows[int(format(r, "04b")[::-1], 2)] for r in range(16)]


def sixteenth(base, r, tall):
    return pl.ds(base + 8 * r, 8) if tall else pl.ds(base + r, 8, stride=16)


def aligned(x, m):
    return pl.multiple_of(x, m)


def forward_kernel(nb, subset, first, tall, lo_ref, frac_ref, win_ref, vol_ref, grid_ref, out_ref,
                   tot, acc, tiles, starts):
    step = pl.program_id(0)

    @pl.when(step == 0)
    def _():
        zero = jnp.zeros((2 * SPAN, LANES), jnp.float32)

        list_tiles(subset, win_ref, tiles, starts)

        def clear(t, at):
            acc[pl.ds(aligned(at // TILES * TALL + lax.rem(at, TILES) * SPAN, SPAN), 2 * SPAN), :] = zero

        over_tiles(tiles, starts, clear)

    width = SUB * BLK_SIDE
    group = BLK_SIDE // SUB
    slices = vol_ref.shape[1]
    col_group = (lax.broadcasted_iota(jnp.int32, (group * slices, width), 1) % BLK_SIDE) // SUB
    mine = col_group == lax.broadcasted_iota(jnp.int32, (group * slices, width), 0) // slices
    angle = lax.broadcasted_iota(jnp.int32, (1, LANES), 1) // R
    for i in range(nb):
        b = step * nb + i
        frac = jnp.zeros((1, LANES), jnp.float32)
        for a in range(ANG_SUB):
            frac = jnp.where(angle == a, frac_ref[subset, a, b], frac)
        parts = []
        for g in range(group):
            at = slice(g * width, (g + 1) * width)
            f = footprint(grid_ref[at, :] + frac)
            wide = jnp.where(mine, jnp.tile(vol_ref[i, :, at], (group, 1)), 0.0)
            parts.append(jnp.dot(wide.astype(jnp.bfloat16), f, preferred_element_type=jnp.float32))
        part = jnp.transpose(jnp.concatenate(parts, axis=0))
        for a in range(ANG_SUB):
            at = pl.ds(a * TALL + PAD + lo_ref[subset, a, b], R)
            acc[at, :] += part[a * R:(a + 1) * R, :]

    @pl.when(step == pl.num_programs(0) - 1)
    def _():
        out_ref[...] = jnp.zeros_like(out_ref)
        lane_q = lax.broadcasted_iota(jnp.int32, (1, LANES), 1) // 8

        for a in range(ANG_SUB):
            def merge(t, i, a=a):
                base = aligned(a * TALL + PAD + i * SPAN, 32)
                tot[pl.ds(aligned(t * SPAN, SPAN), SPAN), :] = shifted(
                    acc, base, [-int(o) for o in first[a]], lane_q)

            over_angle(a, tiles, starts, merge)

        def fold(t, at):
            rows = [tot[sixteenth(aligned(t * SPAN, SPAN), r, tall), :] for r in range(16)]
            for half in (1, 2, 4, 8):
                low = lane_q % (2 * half) < half
                rows = [jnp.where(low, x, y) + pltpu.roll(jnp.where(low, y, x), half * 8, 1)
                        for x, y in zip(rows[0::2], rows[1::2])]
            out_ref[pl.ds(aligned(at * 8, 8), 8), :] = rows[0]

        over_tiles(tiles, starts, fold)


def backward_kernel(nb, subset, first, tall, lo_ref, frac_ref, win_ref, vol_ref, base_ref, res_ref, own_ref, out_ref, last_ref,
                    e_scr, rb, dd, tiles, starts):
    step = pl.program_id(0)

    @pl.when(step == 0)
    def _():
        fill_grid(base_ref, e_scr)
        lane_q = lax.broadcasted_iota(jnp.int32, (1, LANES), 1) // 8
        last_ref[...] = own_ref[...]
        list_tiles(subset, win_ref, tiles, starts)

        def widen(t, at):
            rows = spread_lanes(res_ref[pl.ds(aligned(at * 8, 8), 8), :], lane_q)
            base = aligned(at // TILES * TALL + PAD + lax.rem(at, TILES) * SPAN, 32)
            for r in range(16):
                rb[sixteenth(base, r, tall), :] = rows[r]

        over_tiles(tiles, starts, widen)

        for a in range(ANG_SUB):
            def shift(t, i, a=a):
                base = aligned(a * TALL + PAD + i * SPAN, 32)
                dd[pl.ds(aligned(a * RAYS + i * SPAN, SPAN), SPAN), :] = shifted(
                    rb, base, [int(o) for o in first[a]], lane_q)

            over_angle(a, tiles, starts, shift)

    width = SUB * BLK_SIDE
    group = BLK_SIDE // SUB
    lane = lax.broadcasted_iota(jnp.int32, (8, width), 1)
    col_group = (lane % BLK_SIDE) // SUB

    for i in range(nb):
        b = step * nb + i
        rows = jnp.concatenate(
            [dd[pl.ds(a * RAYS + lo_ref[subset, a, b], R), :] for a in range(ANG_SUB)], axis=0)
        turned = jnp.transpose(rows)
        ones = jnp.ones((8, ANG_SUB * R), jnp.float32)
        for g in range(group):
            lhs = jnp.concatenate([turned[g * 32:(g + 1) * 32], ones], axis=0).astype(jnp.bfloat16)
            at = slice(g * width, (g + 1) * width)
            f = jnp.concatenate(
                [footprint(e_scr[a * R:(a + 1) * R, at] + frac_ref[subset, a, b]) for a in range(ANG_SUB)], axis=0)
            part = jnp.dot(lhs, f, preferred_element_type=jnp.float32)
            back = part[0:8]
            for j in range(1, group):
                back = jnp.where(col_group == j, part[j * 8:(j + 1) * 8], back)
            col_sum = part[32:40]
            out_ref[i, :, at] = jnp.maximum(vol_ref[i, :, at] + relax * back / col_sum, 0.0)


def ray_sums(shape, big, small, inv, ray):
    side = IMG_BLK * BLK_SIDE
    half = side * 0.5
    count = side // 8
    part = lax.broadcasted_iota(jnp.int32, shape, 1) % 8
    start = (part * count).astype(jnp.float32) + (0.5 - half)
    start = ray - start * small

    def row(i, total):
        w = start - i.astype(jnp.float32) * small
        mid = jnp.clip(jnp.floor(w * inv) + 0.5, 2.5 - half, half - 2.5)
        t0 = mid * big - w
        for t in (t0 - 2 * big, t0 - big, t0, t0 + big, t0 + 2 * big):
            bump = jnp.maximum(1.0 - t * t, 0.0)
            total = total + bump * bump
        return total

    total = lax.fori_loop(0, count, row, jnp.zeros(shape, jnp.float32), unroll=4)
    for d in (1, 2, 4):
        total = total + jnp.where(part // d % 2 == 0, pltpu.roll(total, LANES - d, 1), pltpu.roll(total, d, 1))
    return total


def ray_at(line, lane, tall):
    if tall:
        return line // 8 * LANES + lane // 8 * 8 + line % 8
    return line * 16 + lane // 8


def exchange_kernel(subset, tall, part_ref, live_ref, table_ref, meas_ref, full_ref, own_ref,
                    half, inbox, sums, lines_scr, flat, halves, meas, stage, gathered,
                    meas_sem, pair_send, pair_recv, send_sem, recv_sem, rs_send, rs_recv,
                    out_send, out_recv, back_send, back_recv):
    g, p = lax.axis_index("group"), lax.axis_index("patch")
    pairs, groups = inbox.shape[0], inbox.shape[1]
    n = groups * pairs
    lines = stage.shape[0]
    rows = own_ref.shape[0]
    parity, column = lax.rem(p, 2), p // 2
    partner = (g, column * 2 + 1 - parity)
    mesh_id = pl.DeviceIdType.MESH

    def peer(d):
        return lax.rem(column + d // groups, pairs), lax.rem(g + lax.rem(d, groups), groups)

    def source(d):
        return (lax.rem(column + pairs - d // groups, pairs),
                lax.rem(g + groups - lax.rem(d, groups), groups))

    barrier = pltpu.get_barrier_semaphore()
    pl.semaphore_signal(barrier, inc=1, device_id=partner, device_id_type=mesh_id)

    def greet(d, c):
        pc, pg = peer(d)
        pl.semaphore_signal(barrier, inc=1, device_id=(pg, pc * 2 + parity), device_id_type=mesh_id)
        return c

    lax.fori_loop(1, n, greet, 0)
    read = pltpu.make_async_copy(meas_ref.at[subset, pl.ds(g * rows, rows)], meas, meas_sem)
    read.start()
    pl.semaphore_wait(barrier, n)

    def swap(d):
        pc = lax.rem(column + d, pairs)
        return pltpu.make_async_remote_copy(
            src_ref=part_ref.at[pc, 1 - parity], dst_ref=half.at[pc], send_sem=pair_send.at[d],
            recv_sem=pair_recv.at[d], device_id=partner, device_id_type=mesh_id)

    def to_owner(d):
        pc, pg = peer(d)
        return pltpu.make_async_remote_copy(
            src_ref=sums.at[pc, pg], dst_ref=inbox.at[column, g], send_sem=send_sem.at[d],
            recv_sem=recv_sem.at[d], device_id=(pg, pc * 2 + parity), device_id_type=mesh_id)

    def go_swap(d, c):
        swap(d).start()
        return c

    def go_column(i, c):
        pc = lax.rem(column + i, pairs)
        swap(i).wait_recv()
        sums[pc] = part_ref[pc, parity] + half[pc]

        def go(d, c):
            to_owner(d).start()
            return c

        return lax.fori_loop(jnp.maximum(i * groups, 1), (i + 1) * groups, go, c)

    lax.fori_loop(0, pairs, go_swap, 0)
    lax.fori_loop(0, pairs, go_column, 0)

    first_row = (p * groups + g) * rows
    mine = p // pairs
    line = lax.broadcasted_iota(jnp.int32, halves.shape[1:], 0)
    lane = lax.broadcasted_iota(jnp.int32, halves.shape[1:], 1)
    ray = lax.rem(first_row, NTILE) * RAYS_TILE + mine * (lines * 8) + ray_at(line, lane, tall)
    ray = (ray.astype(jnp.float32) + (0.5 - RAYS * 0.5)) * (1.0 / spread)
    a = first_row // NTILE
    halves[mine] = ray_sums(
        halves.shape[1:], table_ref[subset, 0, a], table_ref[subset, 1, a], table_ref[subset, 2, a], ray)
    trade = pltpu.make_async_remote_copy(
        src_ref=halves.at[mine], dst_ref=halves.at[mine], send_sem=rs_send, recv_sem=rs_recv,
        device_id=(g, lax.rem(p + pairs, 2 * pairs)), device_id_type=mesh_id)
    trade.start()

    def got(d, c):
        to_owner(d).wait_recv()
        return c

    read.wait()
    wide = lines // rows
    lane_q = lax.broadcasted_iota(jnp.int32, (1, LANES), 1) // 8

    def retile(forth):
        def one(i, c):
            at = pl.ds(aligned(i * 8, 8), 8)
            for r, x in enumerate(spread_lanes(lines_scr[at, :], lane_q)):
                flat[sixteenth(0, r, not forth), :] = x
            out = flat[sixteenth(0, 0, forth), :]
            for r in range(1, 16):
                out = jnp.where(lane_q == r, flat[sixteenth(0, r, forth), :], out)
            lines_scr[at, :] = out
            return c

        if tall:
            lax.fori_loop(0, lines // 8, one, 0)

    for c in range(wide):
        lines_scr[pl.ds(c, rows, stride=wide), :] = meas[:, c * LANES:(c + 1) * LANES]
    retile(True)

    inbox[column, g] = sums[column, g]
    lax.fori_loop(1, n, got, 0)
    total = jnp.zeros(stage.shape, jnp.float32)
    for i in range(pairs):
        for j in range(groups):
            total = total + inbox[i, j]
    ray = ray_at(lax.broadcasted_iota(jnp.int32, stage.shape, 0),
                 lax.broadcasted_iota(jnp.int32, stage.shape, 1), tall)
    row = ray // RAYS_TILE
    live = jnp.zeros(stage.shape, jnp.int32)
    for r in range(rows):
        live = jnp.where(row == r, live_ref[subset, first_row + r], live)
    trade.wait()
    sums_of = jnp.concatenate([halves[0], halves[1]], axis=0)
    differ = lines_scr[...] - total / jnp.maximum(sums_of, 1.0)
    residual = jnp.where(ray - row * RAYS_TILE < live, differ, 0.0)
    lines_scr[...] = residual
    stage[...] = residual.astype(jnp.bfloat16)

    def to_all(d):
        pc, pg = peer(d)
        return pltpu.make_async_remote_copy(
            src_ref=stage, dst_ref=gathered.at[column, parity, g], send_sem=out_send.at[d],
            recv_sem=out_recv.at[d], device_id=(pg, pc * 2 + parity), device_id_type=mesh_id)

    def share(d):
        pc, pg = source(d)
        return pltpu.make_async_remote_copy(
            src_ref=gathered.at[pc, parity, pg], dst_ref=gathered.at[pc, parity, pg], send_sem=back_send.at[d],
            recv_sem=back_recv.at[d], device_id=partner, device_id_type=mesh_id)

    def go_all(d, c):
        to_all(d).start()
        return c

    def pass_on(d, c):
        to_all(d).wait_recv()
        share(d).start()
        return c

    def finish(d, c):
        share(d).wait()
        return c

    def sent(d, c):
        to_owner(d).wait_send()
        to_all(d).wait_send()
        return c

    def swapped(d, c):
        swap(d).wait_send()
        return c

    lax.fori_loop(1, n, go_all, 0)
    gathered[column, parity, g] = stage[...]
    share(0).start()
    retile(False)
    for c in range(wide):
        own_ref[:, c * LANES:(c + 1) * LANES] = lines_scr[pl.ds(c, rows, stride=wide), :]
    lax.fori_loop(1, n, pass_on, 0)
    lax.fori_loop(0, n, finish, 0)
    lax.fori_loop(1, n, sent, 0)
    lax.fori_loop(0, pairs, swapped, 0)
    for i in range(pairs):
        full_ref[i] = gathered[i].astype(jnp.float32)


def exchange(subset, tall, partial, live, table, measured, rows, groups, patches):
    pairs = patches // 2
    lines = rows * measured.shape[2] // LANES
    shape = (pairs, 2, groups, lines, LANES)
    n = pairs * groups
    dma = pltpu.SemaphoreType.DMA
    vmem = pl.BlockSpec(memory_space=pltpu.VMEM)
    full, own = pl.pallas_call(
        lambda *refs: exchange_kernel(subset, tall, *refs),
        in_specs=[vmem, smem(), smem(), pl.BlockSpec(memory_space=pl.ANY)],
        out_specs=[vmem] * 2,
        out_shape=[jax.ShapeDtypeStruct(shape, jnp.float32),
                   jax.ShapeDtypeStruct((rows, measured.shape[2]), jnp.float32)],
        scratch_shapes=[pltpu.VMEM((pairs, groups, lines, LANES), jnp.float32),
                        pltpu.VMEM((pairs, groups, lines, LANES), jnp.float32),
                        pltpu.VMEM((pairs, groups, lines, LANES), jnp.float32),
                        pltpu.VMEM((lines, LANES), jnp.float32),
                        pltpu.VMEM((SPAN, LANES), jnp.float32),
                        pltpu.VMEM((2, lines // 2, LANES), jnp.float32),
                        pltpu.VMEM((rows, measured.shape[2]), jnp.float32),
                        pltpu.VMEM((lines, LANES), jnp.bfloat16),
                        pltpu.VMEM(shape, jnp.bfloat16),
                        dma, dma((pairs,)), dma((pairs,)), dma((n,)), dma((n,)), dma, dma,
                        dma((n,)), dma((n,)), dma((n,)), dma((n,))],
        compiler_params=pltpu.CompilerParams(collective_id=subset, has_side_effects=True),
        name="exchange",
    )(partial.reshape(shape), live, table, measured)
    return full.reshape(partial.shape), own


def smem():
    return pl.BlockSpec(memory_space=pltpu.SMEM)


def forward(subset, tall, volume, lo, frac, win, base, first):
    blocks, slices, _ = volume.shape
    nb = 8
    lines = ANG_SUB * RAYS // 16
    grid = (np.repeat(base, R, axis=0) - np.tile(np.arange(R), ANG_SUB)[:, None]) * (1.0 / spread)
    return pl.pallas_call(
        lambda *refs: forward_kernel(nb, subset, first, tall, *refs),
        grid=(blocks // nb,),
        in_specs=[smem(), smem(), smem(),
                  pl.BlockSpec((nb, slices, VOX), lambda i: (i, 0, 0)),
                  pl.BlockSpec((VOX, LANES), lambda i: (0, 0))],
        out_specs=pl.BlockSpec((lines, LANES), lambda i: (0, 0)),
        out_shape=jax.ShapeDtypeStruct((lines, LANES), jnp.float32),
        scratch_shapes=[pltpu.VMEM((ANG_SUB * RAYS, LANES), jnp.float32),
                        pltpu.VMEM((ANG_SUB * TALL, LANES), jnp.float32),
                        pltpu.SMEM((ANG_SUB * TILES + 1,), jnp.int32),
                        pltpu.SMEM((ANG_SUB + 1,), jnp.int32)],
        compiler_params=pltpu.CompilerParams(vmem_limit_bytes=VMEM_LIMIT),
        name="forward",
    )(lo, frac, win, volume, grid.T.astype(np.float32))


def backward(subset, tall, volume, residual, own, lo, frac, win, base, first):
    blocks, slices, _ = volume.shape
    nb = 8
    return pl.pallas_call(
        lambda *refs: backward_kernel(nb, subset, first, tall, *refs),
        grid=(blocks // nb,),
        in_specs=[smem(), smem(), smem(),
                  pl.BlockSpec((nb, slices, VOX), lambda i: (i, 0, 0)),
                  pl.BlockSpec((ANG_SUB, VOX), lambda i: (0, 0)),
                  pl.BlockSpec(residual.shape, lambda i: (0, 0)),
                  pl.BlockSpec(own.shape, lambda i: (0, 0))],
        out_specs=[pl.BlockSpec((nb, slices, VOX), lambda i: (i, 0, 0)),
                   pl.BlockSpec(own.shape, lambda i: (0, 0))],
        out_shape=[jax.ShapeDtypeStruct(volume.shape, jnp.float32),
                   jax.ShapeDtypeStruct(own.shape, jnp.float32)],
        scratch_shapes=[pltpu.VMEM((ANG_SUB * R, VOX), jnp.float32),
                        pltpu.VMEM((ANG_SUB * TALL, LANES), jnp.float32),
                        pltpu.VMEM((ANG_SUB * RAYS, LANES), jnp.float32),
                        pltpu.SMEM((ANG_SUB * TILES + 1,), jnp.int32),
                        pltpu.SMEM((ANG_SUB + 1,), jnp.int32)],
        compiler_params=pltpu.CompilerParams(vmem_limit_bytes=VMEM_LIMIT),
        name="backward",
    )(lo, frac, win, volume, base, residual, own)


def ray_table():
    table = np.zeros((SUBSETS, 3, ANG_SUB), np.float64)
    for subset in range(SUBSETS):
        for a, t in enumerate(angles(subset)):
            small, big = sorted((abs(math.cos(t)), abs(math.sin(t))))
            table[subset, :, a] = big / spread, small / spread, spread / big
    return table.astype(np.float32)


def placing_kernel(place_ref, lo_ref, frac_ref, win_ref):
    half = IMG_BLK * BLK_SIDE * 0.5
    shape = lo_ref.shape[1:]
    place = jnp.broadcast_to(place_ref[...], shape)
    x = (place % IMG_BLK).astype(jnp.float32) * BLK_SIDE + (BLK_SIDE * 0.5 - half)
    y = (place // IMG_BLK).astype(jnp.float32) * BLK_SIDE + (BLK_SIDE * 0.5 - half)
    angle = lax.broadcasted_iota(jnp.int32, shape, 0)
    tile = lax.broadcasted_iota(jnp.int32, (TILES, shape[1]), 0)
    near = []
    for subset in range(SUBSETS):
        cosine = sine = jnp.zeros(shape, jnp.float32)
        for a, theta in enumerate(angles(subset)):
            cosine = jnp.where(angle == a, np.float32(math.cos(theta)), cosine)
            sine = jnp.where(angle == a, np.float32(math.sin(theta)), sine)
        z = x * cosine + y * sine + (RAYS * 0.5 - 0.5)
        low = jnp.floor(z)
        lo = low.astype(jnp.int32)
        lo_ref[subset] = lo
        frac_ref[subset] = (z - low) * (1.0 / spread)
        ends = (lo - PAD) // SPAN, (lo + R + PAD) // SPAN
        for a in range(ANG_SUB):
            hit = (ends[0][a:a + 1] == tile) | (ends[1][a:a + 1] == tile)
            near.append(jnp.where(hit, 1.0, 0.0))
    count = lax.dot_general(jnp.ones((8, shape[1]), jnp.bfloat16), jnp.concatenate(near, axis=0).astype(jnp.bfloat16),
                            (((1,), (1,)), ((), ())), preferred_element_type=jnp.float32)
    win_ref[...] = jnp.where(count[0:1] > 0.0, 1, 0)


def placing(place):
    shape = (SUBSETS, ANG_SUB, place.shape[0])
    return pl.pallas_call(
        placing_kernel,
        out_shape=[jax.ShapeDtypeStruct(shape, jnp.int32), jax.ShapeDtypeStruct(shape, jnp.float32),
                   jax.ShapeDtypeStruct((1, SUBSETS * ANG_SUB * TILES), jnp.int32)],
        name="placing",
    )(place.reshape(1, -1))


def shards(volume, block_place, measured, live_rays):
    groups = lax.axis_size("group")
    patches = lax.axis_size("patch")
    rows = ANG_SUB * NTILE // patches // groups
    lo, frac, win = placing(block_place)
    table = ray_table()
    tall = rows * RAYS_TILE % (2 * LANES) == 0
    estimate = volume
    own = None
    for subset in range(SUBSETS):
        base, first = geometry(subset)
        partial = forward(subset, tall, estimate, lo, frac, win, base, first)
        full, own = exchange(subset, tall, partial, live_rays, table, measured, rows, groups, patches)
        estimate, own = backward(subset, tall, estimate, full, own, lo, frac, win, base, first)
    return (estimate, own[None])


def solution(mesh):
    return jax.shard_map(
        shards,
        mesh=mesh,
        in_specs=(
            P(("group", "patch"), None, None),
            P(("group", "patch")),
            P(None, "patch", None),
            P(),
        ),
        out_specs=(P(("group", "patch"), None, None), P("group", "patch", None)),
        check_vma=False,
    )
```

```python
import math

import jax
import jax.numpy as jnp
import numpy as np
from jax import lax
from jax.experimental import pallas as pl
from jax.experimental.pallas import tpu as pltpu
from jax.sharding import PartitionSpec as P

IMG_BLK = 64
BLK_SIDE = 32
RAYS_TILE = 48
NTILE = 64
ANG_SUB = 8
SUBSETS = 2

spread = 1.5
relax = 0.9

SUB = 8
NQ = (BLK_SIDE // SUB) ** 2
R = 16
VOX = BLK_SIDE * BLK_SIDE
RAYS = NTILE * RAYS_TILE
LANES = 128
PAD = 32
EARLY = 3
SPAN = 128
TALL = RAYS + SPAN
VMEM_LIMIT = 60 * 1024 * 1024


def angles(subset):
    return [math.pi * (a * SUBSETS + subset) / (ANG_SUB * SUBSETS) for a in range(ANG_SUB)]


def geometry(subset):
    v = np.arange(VOX)
    col = (v % BLK_SIDE) + 0.5 - BLK_SIDE / 2
    row = (v // BLK_SIDE) + 0.5 - BLK_SIDE / 2
    q_of = (v // BLK_SIDE // SUB) * (BLK_SIDE // SUB) + (v % BLK_SIDE) // SUB
    base = np.zeros((ANG_SUB, VOX), np.float64)
    first = np.zeros((ANG_SUB, NQ), np.int64)
    for a, theta in enumerate(angles(subset)):
        off = col * math.cos(theta) + row * math.sin(theta)
        for q in range(NQ):
            mine = q_of == q
            first[a, q] = math.floor(off[mine].min() - spread)
            base[a, mine] = off[mine] - first[a, q]
    return base.astype(np.float32), first.astype(np.int32)


def fill_grid(base_ref, e_scr):
    ray = lax.broadcasted_iota(jnp.int32, (R, VOX), 0).astype(jnp.float32)
    for a in range(ANG_SUB):
        e_scr[a * R:(a + 1) * R, :] = (base_ref[a:a + 1, :] - ray) * (1.0 / spread)


def footprint(t):
    t = t.astype(jnp.bfloat16)
    bump = jnp.maximum(1.0 - t * t, 0.0)
    return bump * bump


TILES = RAYS // SPAN


WIDE = 4


def list_tiles(subset, win_ref, tiles, starts):
    def angle(a, n):
        starts[a] = n
        for i in range(TILES):
            hit = win_ref[0, (subset * ANG_SUB + a) * TILES + i]
            tiles[n] = a * TILES + i
            n = n + hit
        return n

    starts[ANG_SUB] = lax.fori_loop(0, ANG_SUB, angle, 0)


def over_tiles(tiles, starts, body):
    n = starts[ANG_SUB]

    def some(i, c):
        for j in range(WIDE):
            t = jnp.minimum(WIDE * i + j, n - 1)
            body(t, tiles[t])
        return c

    lax.fori_loop(0, (n + WIDE - 1) // WIDE, some, 0)


def over_angle(a, tiles, starts, body):
    def one(t, c):
        body(t, tiles[t] - a * TILES)
        return c

    lax.fori_loop(starts[a], starts[a + 1], one, 0)


def shifted(ref, base, offsets, lane_q):
    fine = [o % 8 for o in offsets]
    coarse = [o // 8 for o in offsets]
    low, high = min(coarse), max(coarse)

    def member(values, value):
        hits = [lane_q == q for q, v in enumerate(values) if v == value]
        mask = hits[0]
        for h in hits[1:]:
            mask = mask | h
        return mask

    rows = None
    for f in sorted(set(fine)):
        part = ref[pl.ds(base + 8 * low + f, SPAN + 8 * (high - low)), :]
        rows = part if rows is None else jnp.where(member(fine, f), part, rows)
    out = None
    for c in sorted(set(coarse)):
        part = rows[8 * (c - low):8 * (c - low) + SPAN]
        out = part if out is None else jnp.where(member(coarse, c), part, out)
    return out


def spread_lanes(x, lane_q):
    rows = [x]
    for half in (8, 4, 2, 1):
        low = lane_q % (2 * half) < half
        turned = [pltpu.roll(x, half * 8, 1) for x in rows]
        rows = ([jnp.where(low, x, y) for x, y in zip(rows, turned)]
                + [jnp.where(low, y, x) for x, y in zip(rows, turned)])
    return [rows[int(format(r, "04b")[::-1], 2)] for r in range(16)]


def sixteenth(base, r, tall):
    return pl.ds(base + 8 * r, 8) if tall else pl.ds(base + r, 8, stride=16)


def aligned(x, m):
    return pl.multiple_of(x, m)


def forward_kernel(nb, subset, first, tall, lo_ref, frac_ref, win_ref, vol_ref, grid_ref, out_ref,
                   tot, acc, tiles, starts):
    step = pl.program_id(0)

    @pl.when(step == 0)
    def _():
        zero = jnp.zeros((2 * SPAN, LANES), jnp.float32)

        list_tiles(subset, win_ref, tiles, starts)

        def clear(t, at):
            acc[pl.ds(aligned(at // TILES * TALL + lax.rem(at, TILES) * SPAN, SPAN), 2 * SPAN), :] = zero

        over_tiles(tiles, starts, clear)

    width = SUB * BLK_SIDE
    group = BLK_SIDE // SUB
    slices = vol_ref.shape[1]
    col_group = (lax.broadcasted_iota(jnp.int32, (group * slices, width), 1) % BLK_SIDE) // SUB
    mine = col_group == lax.broadcasted_iota(jnp.int32, (group * slices, width), 0) // slices
    angle = lax.broadcasted_iota(jnp.int32, (1, LANES), 1) // R
    for i in range(nb):
        b = step * nb + i
        frac = jnp.zeros((1, LANES), jnp.float32)
        for a in range(ANG_SUB):
            frac = jnp.where(angle == a, frac_ref[subset, a, b], frac)
        parts = []
        for g in range(group):
            at = slice(g * width, (g + 1) * width)
            f = footprint(grid_ref[at, :] + frac)
            wide = jnp.where(mine, jnp.tile(vol_ref[i, :, at], (group, 1)), 0.0)
            parts.append(jnp.dot(wide.astype(jnp.bfloat16), f, preferred_element_type=jnp.float32))
        part = jnp.transpose(jnp.concatenate(parts, axis=0))
        for a in range(ANG_SUB):
            at = pl.ds(a * TALL + PAD + lo_ref[subset, a, b], R)
            acc[at, :] += part[a * R:(a + 1) * R, :]

    @pl.when(step == pl.num_programs(0) - 1)
    def _():
        out_ref[...] = jnp.zeros_like(out_ref)
        lane_q = lax.broadcasted_iota(jnp.int32, (1, LANES), 1) // 8

        for a in range(ANG_SUB):
            def merge(t, i, a=a):
                base = aligned(a * TALL + PAD + i * SPAN, 32)
                tot[pl.ds(aligned(t * SPAN, SPAN), SPAN), :] = shifted(
                    acc, base, [-int(o) for o in first[a]], lane_q)

            over_angle(a, tiles, starts, merge)

        def fold(t, at):
            rows = [tot[sixteenth(aligned(t * SPAN, SPAN), r, tall), :] for r in range(16)]
            for half in (1, 2, 4, 8):
                low = lane_q % (2 * half) < half
                rows = [jnp.where(low, x, y) + pltpu.roll(jnp.where(low, y, x), half * 8, 1)
                        for x, y in zip(rows[0::2], rows[1::2])]
            out_ref[pl.ds(aligned(at * 8, 8), 8), :] = rows[0]

        over_tiles(tiles, starts, fold)


def backward_kernel(nb, subset, first, tall, lo_ref, frac_ref, win_ref, vol_ref, base_ref, res_ref, own_ref, out_ref, last_ref,
                    e_scr, res, rb, dd, tiles, starts):
    step = pl.program_id(0)

    @pl.when(step == 0)
    def _():
        fill_grid(base_ref, e_scr)
        lane_q = lax.broadcasted_iota(jnp.int32, (1, LANES), 1) // 8
        last_ref[...] = own_ref[...]
        res[...] = res_ref[...].astype(jnp.float32)
        list_tiles(subset, win_ref, tiles, starts)

        def widen(t, at):
            rows = spread_lanes(res[pl.ds(aligned(at * 8, 8), 8), :], lane_q)
            base = aligned(at // TILES * TALL + PAD + lax.rem(at, TILES) * SPAN, 32)
            for r in range(16):
                rb[sixteenth(base, r, tall), :] = rows[r]

        over_tiles(tiles, starts, widen)

        for a in range(ANG_SUB):
            def shift(t, i, a=a):
                base = aligned(a * TALL + PAD + i * SPAN, 32)
                dd[pl.ds(aligned(a * RAYS + i * SPAN, SPAN), SPAN), :] = shifted(
                    rb, base, [int(o) for o in first[a]], lane_q)

            over_angle(a, tiles, starts, shift)

    width = SUB * BLK_SIDE
    group = BLK_SIDE // SUB
    lane = lax.broadcasted_iota(jnp.int32, (8, width), 1)
    col_group = (lane % BLK_SIDE) // SUB

    for i in range(nb):
        b = step * nb + i
        rows = jnp.concatenate(
            [dd[pl.ds(a * RAYS + lo_ref[subset, a, b], R), :] for a in range(ANG_SUB)], axis=0)
        turned = jnp.transpose(rows)
        ones = jnp.ones((8, ANG_SUB * R), jnp.float32)
        for g in range(group):
            lhs = jnp.concatenate([turned[g * 32:(g + 1) * 32], ones], axis=0).astype(jnp.bfloat16)
            at = slice(g * width, (g + 1) * width)
            f = jnp.concatenate(
                [footprint(e_scr[a * R:(a + 1) * R, at] + frac_ref[subset, a, b]) for a in range(ANG_SUB)], axis=0)
            part = jnp.dot(lhs, f, preferred_element_type=jnp.float32)
            back = part[0:8]
            for j in range(1, group):
                back = jnp.where(col_group == j, part[j * 8:(j + 1) * 8], back)
            col_sum = part[32:40]
            out_ref[i, :, at] = jnp.maximum(vol_ref[i, :, at] + relax * back / col_sum, 0.0)


def ray_sums(shape, big, small, inv, ray):
    side = IMG_BLK * BLK_SIDE
    half = side * 0.5
    count = side // 8
    part = lax.broadcasted_iota(jnp.int32, shape, 1) % 8
    start = (part * count).astype(jnp.float32) + (0.5 - half)
    start = ray - start * small

    def row(i, total):
        w = start - i.astype(jnp.float32) * small
        mid = jnp.clip(jnp.floor(w * inv) + 0.5, 2.5 - half, half - 2.5)
        t0 = mid * big - w
        for t in (t0 - 2 * big, t0 - big, t0, t0 + big, t0 + 2 * big):
            bump = jnp.maximum(1.0 - t * t, 0.0)
            total = total + bump * bump
        return total

    def fold(total):
        for d in (1, 2, 4):
            total = total + jnp.where(
                part // d % 2 == 0, pltpu.roll(total, LANES - d, 1), pltpu.roll(total, d, 1))
        return total

    early = count * EARLY // 8
    first = lax.fori_loop(0, early, row, jnp.zeros(shape, jnp.float32), unroll=4)
    return first, lambda total: fold(lax.fori_loop(early, count, row, total, unroll=4))


def ray_at(line, lane, tall):
    if tall:
        return line // 8 * LANES + lane // 8 * 8 + line % 8
    return line * 16 + lane // 8


def exchange_kernel(subset, tall, part_ref, live_ref, table_ref, meas_ref, gathered, own_ref,
                    keep, half, inbox, sums, lines_scr, flat, halves, meas, stage,
                    meas_sem, keep_sem, pair_send, pair_recv, send_sem, recv_sem, rs_send, rs_recv,
                    out_send, out_recv, back_send, back_recv):
    g, p = lax.axis_index("group"), lax.axis_index("patch")
    pairs, groups = inbox.shape[0], inbox.shape[1]
    n = groups * pairs
    lines = stage.shape[0]
    rows = own_ref.shape[0]
    parity, column = lax.rem(p, 2), p // 2
    partner = (g, column * 2 + 1 - parity)
    mesh_id = pl.DeviceIdType.MESH

    def peer(d):
        return lax.rem(column + d // groups, pairs), lax.rem(g + lax.rem(d, groups), groups)

    def source(d):
        return (lax.rem(column + pairs - d // groups, pairs),
                lax.rem(g + groups - lax.rem(d, groups), groups))

    barrier = pltpu.get_barrier_semaphore()
    pl.semaphore_signal(barrier, inc=1, device_id=partner, device_id_type=mesh_id)

    def greet(d, c):
        pc, pg = peer(d)
        pl.semaphore_signal(barrier, inc=1, device_id=(pg, pc * 2 + parity), device_id_type=mesh_id)
        return c

    lax.fori_loop(1, n, greet, 0)
    read = pltpu.make_async_copy(meas_ref.at[subset, pl.ds(g * rows, rows)], meas, meas_sem)
    read.start()
    kept = pltpu.make_async_copy(part_ref.at[:, parity], keep, keep_sem)
    kept.start()
    first_row = (p * groups + g) * rows
    mine = p // pairs
    line = lax.broadcasted_iota(jnp.int32, halves.shape[1:], 0)
    lane = lax.broadcasted_iota(jnp.int32, halves.shape[1:], 1)
    ray = lax.rem(first_row, NTILE) * RAYS_TILE + mine * (lines * 8) + ray_at(line, lane, tall)
    ray = (ray.astype(jnp.float32) + (0.5 - RAYS * 0.5)) * (1.0 / spread)
    a = first_row // NTILE
    early, rest = ray_sums(
        halves.shape[1:], table_ref[subset, 0, a], table_ref[subset, 1, a], table_ref[subset, 2, a], ray)
    pl.semaphore_wait(barrier, n)

    def swap(d):
        pc = lax.rem(column + d, pairs)
        return pltpu.make_async_remote_copy(
            src_ref=part_ref.at[pc, 1 - parity], dst_ref=half.at[pc], send_sem=pair_send.at[d],
            recv_sem=pair_recv.at[d], device_id=partner, device_id_type=mesh_id)

    def to_owner(d):
        pc, pg = peer(d)
        return pltpu.make_async_remote_copy(
            src_ref=sums.at[pc, pg], dst_ref=inbox.at[column, g], send_sem=send_sem.at[d],
            recv_sem=recv_sem.at[d], device_id=(pg, pc * 2 + parity), device_id_type=mesh_id)

    def go_swap(d, c):
        swap(d).start()
        return c

    def go_column(i, c):
        pc = lax.rem(column + i, pairs)
        swap(i).wait_recv()
        sums[pc] = (keep[pc] + half[pc]).astype(sums.dtype)

        def go(d, c):
            to_owner(d).start()
            return c

        return lax.fori_loop(jnp.maximum(i * groups, 1), (i + 1) * groups, go, c)

    lax.fori_loop(0, pairs, go_swap, 0)
    kept.wait()
    lax.fori_loop(0, pairs, go_column, 0)
    halves[mine] = rest(early)
    trade = pltpu.make_async_remote_copy(
        src_ref=halves.at[mine], dst_ref=halves.at[mine], send_sem=rs_send, recv_sem=rs_recv,
        device_id=(g, lax.rem(p + pairs, 2 * pairs)), device_id_type=mesh_id)
    trade.start()

    def got(d, c):
        to_owner(d).wait_recv()
        return c

    read.wait()
    wide = lines // rows
    lane_q = lax.broadcasted_iota(jnp.int32, (1, LANES), 1) // 8

    def retile(forth):
        def one(i, c):
            at = pl.ds(aligned(i * 8, 8), 8)
            for r, x in enumerate(spread_lanes(lines_scr[at, :], lane_q)):
                flat[sixteenth(0, r, not forth), :] = x
            out = flat[sixteenth(0, 0, forth), :]
            for r in range(1, 16):
                out = jnp.where(lane_q == r, flat[sixteenth(0, r, forth), :], out)
            lines_scr[at, :] = out
            return c

        if tall:
            lax.fori_loop(0, lines // 8, one, 0)

    for c in range(wide):
        lines_scr[pl.ds(c, rows, stride=wide), :] = meas[:, c * LANES:(c + 1) * LANES]
    retile(True)

    inbox[column, g] = sums[column, g]
    lax.fori_loop(1, n, got, 0)
    total = jnp.zeros(stage.shape, jnp.float32)
    for i in range(pairs):
        for j in range(groups):
            total = total + inbox[i, j].astype(jnp.float32)
    ray = ray_at(lax.broadcasted_iota(jnp.int32, stage.shape, 0),
                 lax.broadcasted_iota(jnp.int32, stage.shape, 1), tall)
    row = ray // RAYS_TILE
    live = jnp.zeros(stage.shape, jnp.int32)
    for r in range(rows):
        live = jnp.where(row == r, live_ref[subset, first_row + r], live)
    trade.wait()
    sums_of = jnp.concatenate([halves[0], halves[1]], axis=0)
    differ = lines_scr[...] - total / jnp.maximum(sums_of, 1.0)
    residual = jnp.where(ray - row * RAYS_TILE < live, differ, 0.0)
    lines_scr[...] = residual
    stage[...] = residual.astype(jnp.bfloat16)

    def to_all(d):
        pc, pg = peer(d)
        return pltpu.make_async_remote_copy(
            src_ref=stage, dst_ref=gathered.at[column, parity, g], send_sem=out_send.at[d],
            recv_sem=out_recv.at[d], device_id=(pg, pc * 2 + parity), device_id_type=mesh_id)

    def share(d):
        pc, pg = source(d)
        return pltpu.make_async_remote_copy(
            src_ref=gathered.at[pc, parity, pg], dst_ref=gathered.at[pc, parity, pg], send_sem=back_send.at[d],
            recv_sem=back_recv.at[d], device_id=partner, device_id_type=mesh_id)

    def go_all(d, c):
        to_all(d).start()
        return c

    def pass_on(d, c):
        to_all(d).wait_recv()
        share(d).start()
        return c

    def finish(d, c):
        share(d).wait()
        return c

    def sent(d, c):
        to_owner(d).wait_send()
        to_all(d).wait_send()
        return c

    def swapped(d, c):
        swap(d).wait_send()
        return c

    lax.fori_loop(1, n, go_all, 0)
    gathered[column, parity, g] = stage[...]
    share(0).start()
    retile(False)
    for c in range(wide):
        own_ref[:, c * LANES:(c + 1) * LANES] = lines_scr[pl.ds(c, rows, stride=wide), :]
    lax.fori_loop(1, n, pass_on, 0)
    lax.fori_loop(0, n, finish, 0)
    lax.fori_loop(1, n, sent, 0)
    lax.fori_loop(0, pairs, swapped, 0)


def exchange(subset, tall, partial, live, table, measured, rows, groups, patches):
    pairs = patches // 2
    lines = rows * measured.shape[2] // LANES
    shape = (pairs, 2, groups, lines, LANES)
    n = pairs * groups
    wire = jnp.bfloat16 if subset < SUBSETS - 1 else jnp.float32
    dma = pltpu.SemaphoreType.DMA
    vmem = pl.BlockSpec(memory_space=pltpu.VMEM)
    full, own = pl.pallas_call(
        lambda *refs: exchange_kernel(subset, tall, *refs),
        in_specs=[pl.BlockSpec(memory_space=pl.ANY), smem(), smem(), pl.BlockSpec(memory_space=pl.ANY)],
        out_specs=[vmem] * 2,
        out_shape=[jax.ShapeDtypeStruct(shape, jnp.bfloat16),
                   jax.ShapeDtypeStruct((rows, measured.shape[2]), jnp.float32)],
        scratch_shapes=[pltpu.VMEM((pairs, groups, lines, LANES), jnp.float32),
                        pltpu.VMEM((pairs, groups, lines, LANES), jnp.float32),
                        pltpu.VMEM((pairs, groups, lines, LANES), wire),
                        pltpu.VMEM((pairs, groups, lines, LANES), wire),
                        pltpu.VMEM((lines, LANES), jnp.float32),
                        pltpu.VMEM((SPAN, LANES), jnp.float32),
                        pltpu.VMEM((2, lines // 2, LANES), jnp.float32),
                        pltpu.VMEM((rows, measured.shape[2]), jnp.float32),
                        pltpu.VMEM((lines, LANES), jnp.bfloat16),
                        dma, dma, dma((pairs,)), dma((pairs,)), dma((n,)), dma((n,)), dma, dma,
                        dma((n,)), dma((n,)), dma((n,)), dma((n,))],
        compiler_params=pltpu.CompilerParams(collective_id=subset, has_side_effects=True),
        name="exchange",
    )(partial.reshape(shape), live, table, measured)
    return full.reshape(partial.shape), own


def smem():
    return pl.BlockSpec(memory_space=pltpu.SMEM)


def forward(subset, tall, volume, lo, frac, win, base, first):
    blocks, slices, _ = volume.shape
    nb = 8
    lines = ANG_SUB * RAYS // 16
    grid = (np.repeat(base, R, axis=0) - np.tile(np.arange(R), ANG_SUB)[:, None]) * (1.0 / spread)
    return pl.pallas_call(
        lambda *refs: forward_kernel(nb, subset, first, tall, *refs),
        grid=(blocks // nb,),
        in_specs=[smem(), smem(), smem(),
                  pl.BlockSpec((nb, slices, VOX), lambda i: (i, 0, 0)),
                  pl.BlockSpec((VOX, LANES), lambda i: (0, 0))],
        out_specs=pl.BlockSpec((lines, LANES), lambda i: (0, 0)),
        out_shape=jax.ShapeDtypeStruct((lines, LANES), jnp.float32),
        scratch_shapes=[pltpu.VMEM((ANG_SUB * RAYS, LANES), jnp.float32),
                        pltpu.VMEM((ANG_SUB * TALL, LANES), jnp.float32),
                        pltpu.SMEM((ANG_SUB * TILES + 1,), jnp.int32),
                        pltpu.SMEM((ANG_SUB + 1,), jnp.int32)],
        compiler_params=pltpu.CompilerParams(vmem_limit_bytes=VMEM_LIMIT),
        name="forward",
    )(lo, frac, win, volume, grid.T.astype(np.float32))


def backward(subset, tall, volume, residual, own, lo, frac, win, base, first):
    blocks, slices, _ = volume.shape
    nb = 8
    return pl.pallas_call(
        lambda *refs: backward_kernel(nb, subset, first, tall, *refs),
        grid=(blocks // nb,),
        in_specs=[smem(), smem(), smem(),
                  pl.BlockSpec((nb, slices, VOX), lambda i: (i, 0, 0)),
                  pl.BlockSpec((ANG_SUB, VOX), lambda i: (0, 0)),
                  pl.BlockSpec(residual.shape, lambda i: (0, 0)),
                  pl.BlockSpec(own.shape, lambda i: (0, 0))],
        out_specs=[pl.BlockSpec((nb, slices, VOX), lambda i: (i, 0, 0)),
                   pl.BlockSpec(own.shape, lambda i: (0, 0))],
        out_shape=[jax.ShapeDtypeStruct(volume.shape, jnp.float32),
                   jax.ShapeDtypeStruct(own.shape, jnp.float32)],
        scratch_shapes=[pltpu.VMEM((ANG_SUB * R, VOX), jnp.float32),
                        pltpu.VMEM(residual.shape, jnp.float32),
                        pltpu.VMEM((ANG_SUB * TALL, LANES), jnp.float32),
                        pltpu.VMEM((ANG_SUB * RAYS, LANES), jnp.float32),
                        pltpu.SMEM((ANG_SUB * TILES + 1,), jnp.int32),
                        pltpu.SMEM((ANG_SUB + 1,), jnp.int32)],
        compiler_params=pltpu.CompilerParams(vmem_limit_bytes=VMEM_LIMIT),
        name="backward",
    )(lo, frac, win, volume, base, residual, own)


def ray_table():
    table = np.zeros((SUBSETS, 3, ANG_SUB), np.float64)
    for subset in range(SUBSETS):
        for a, t in enumerate(angles(subset)):
            small, big = sorted((abs(math.cos(t)), abs(math.sin(t))))
            table[subset, :, a] = big / spread, small / spread, spread / big
    return table.astype(np.float32)


def placing_kernel(place_ref, lo_ref, frac_ref, win_ref):
    half = IMG_BLK * BLK_SIDE * 0.5
    shape = lo_ref.shape[1:]
    place = jnp.broadcast_to(place_ref[...], shape)
    x = (place % IMG_BLK).astype(jnp.float32) * BLK_SIDE + (BLK_SIDE * 0.5 - half)
    y = (place // IMG_BLK).astype(jnp.float32) * BLK_SIDE + (BLK_SIDE * 0.5 - half)
    angle = lax.broadcasted_iota(jnp.int32, shape, 0)
    tile = lax.broadcasted_iota(jnp.int32, (TILES, shape[1]), 0)
    near = []
    for subset in range(SUBSETS):
        cosine = sine = jnp.zeros(shape, jnp.float32)
        for a, theta in enumerate(angles(subset)):
            cosine = jnp.where(angle == a, np.float32(math.cos(theta)), cosine)
            sine = jnp.where(angle == a, np.float32(math.sin(theta)), sine)
        z = x * cosine + y * sine + (RAYS * 0.5 - 0.5)
        low = jnp.floor(z)
        lo = low.astype(jnp.int32)
        lo_ref[subset] = lo
        frac_ref[subset] = (z - low) * (1.0 / spread)
        ends = (lo - PAD) // SPAN, (lo + R + PAD) // SPAN
        for a in range(ANG_SUB):
            hit = (ends[0][a:a + 1] == tile) | (ends[1][a:a + 1] == tile)
            near.append(jnp.where(hit, 1.0, 0.0))
    count = lax.dot_general(jnp.ones((8, shape[1]), jnp.bfloat16), jnp.concatenate(near, axis=0).astype(jnp.bfloat16),
                            (((1,), (1,)), ((), ())), preferred_element_type=jnp.float32)
    win_ref[...] = jnp.where(count[0:1] > 0.0, 1, 0)


def placing(place):
    shape = (SUBSETS, ANG_SUB, place.shape[0])
    return pl.pallas_call(
        placing_kernel,
        out_shape=[jax.ShapeDtypeStruct(shape, jnp.int32), jax.ShapeDtypeStruct(shape, jnp.float32),
                   jax.ShapeDtypeStruct((1, SUBSETS * ANG_SUB * TILES), jnp.int32)],
        name="placing",
    )(place.reshape(1, -1))


def shards(volume, block_place, measured, live_rays):
    groups = lax.axis_size("group")
    patches = lax.axis_size("patch")
    rows = ANG_SUB * NTILE // patches // groups
    lo, frac, win = placing(block_place)
    table = ray_table()
    tall = rows * RAYS_TILE % (2 * LANES) == 0
    estimate = volume
    own = None
    for subset in range(SUBSETS):
        base, first = geometry(subset)
        partial = forward(subset, tall, estimate, lo, frac, win, base, first)
        full, own = exchange(subset, tall, partial, live_rays, table, measured, rows, groups, patches)
        estimate, own = backward(subset, tall, estimate, full, own, lo, frac, win, base, first)
    return (estimate, own[None])


def solution(mesh):
    return jax.shard_map(
        shards,
        mesh=mesh,
        in_specs=(
            P(("group", "patch"), None, None),
            P(("group", "patch")),
            P(None, "patch", None),
            P(),
        ),
        out_specs=(P(("group", "patch"), None, None), P("group", "patch", None)),
        check_vma=False,
    )
```

```python
import math

import jax
import jax.numpy as jnp
import numpy as np
from jax import lax
from jax.experimental import pallas as pl
from jax.experimental.pallas import tpu as pltpu
from jax.sharding import PartitionSpec as P

IMG_BLK = 64
BLK_SIDE = 32
RAYS_TILE = 48
NTILE = 64
ANG_SUB = 8
SUBSETS = 2

spread = 1.5
relax = 0.9

SUB = 8
NQ = (BLK_SIDE // SUB) ** 2
R = 16
VOX = BLK_SIDE * BLK_SIDE
RAYS = NTILE * RAYS_TILE
LANES = 128
PAD = 32
CHUNK = 32
DEPTH = 2
EARLY = 3
SPAN = 128
TALL = RAYS + SPAN
VMEM_LIMIT = 60 * 1024 * 1024


def angles(subset):
    return [math.pi * (a * SUBSETS + subset) / (ANG_SUB * SUBSETS) for a in range(ANG_SUB)]


def geometry(subset):
    v = np.arange(VOX)
    col = (v % BLK_SIDE) + 0.5 - BLK_SIDE / 2
    row = (v // BLK_SIDE) + 0.5 - BLK_SIDE / 2
    q_of = (v // BLK_SIDE // SUB) * (BLK_SIDE // SUB) + (v % BLK_SIDE) // SUB
    base = np.zeros((ANG_SUB, VOX), np.float64)
    first = np.zeros((ANG_SUB, NQ), np.int64)
    for a, theta in enumerate(angles(subset)):
        off = col * math.cos(theta) + row * math.sin(theta)
        for q in range(NQ):
            mine = q_of == q
            first[a, q] = math.floor(off[mine].min() - spread)
            base[a, mine] = off[mine] - first[a, q]
    return base.astype(np.float32), first.astype(np.int32)


def fill_grid(base_ref, e_scr):
    ray = lax.broadcasted_iota(jnp.int32, (R, VOX), 0).astype(jnp.float32)
    for a in range(ANG_SUB):
        e_scr[a * R:(a + 1) * R, :] = (base_ref[a:a + 1, :] - ray) * (1.0 / spread)


def footprint(t):
    t = t.astype(jnp.bfloat16)
    bump = jnp.maximum(1.0 - t * t, 0.0)
    return bump * bump


TILES = RAYS // SPAN


WIDE = 16


def list_tiles(subset, win_ref, tiles, starts):
    def angle(a, n):
        starts[a] = n
        for i in range(TILES):
            hit = win_ref[0, (subset * ANG_SUB + a) * TILES + i]
            tiles[n] = a * TILES + i
            n = n + hit
        return n

    starts[ANG_SUB] = lax.fori_loop(0, ANG_SUB, angle, 0)


def over_tiles(tiles, starts, body):
    n = starts[ANG_SUB]

    def some(i, c):
        for j in range(WIDE):
            t = jnp.minimum(WIDE * i + j, n - 1)
            body(t, tiles[t])
        return c

    lax.fori_loop(0, (n + WIDE - 1) // WIDE, some, 0)


def over_angle(a, tiles, starts, body):
    def one(t, c):
        body(t, tiles[t] - a * TILES)
        return c

    lax.fori_loop(starts[a], starts[a + 1], one, 0)


def shifted(ref, base, offsets, lane_q):
    fine = [o % 8 for o in offsets]
    coarse = [o // 8 for o in offsets]
    low, high = min(coarse), max(coarse)

    def member(values, value):
        hits = [lane_q == q for q, v in enumerate(values) if v == value]
        mask = hits[0]
        for h in hits[1:]:
            mask = mask | h
        return mask

    rows = None
    for f in sorted(set(fine)):
        part = ref[pl.ds(base + 8 * low + f, SPAN + 8 * (high - low)), :]
        rows = part if rows is None else jnp.where(member(fine, f), part, rows)
    out = None
    for c in sorted(set(coarse)):
        part = rows[8 * (c - low):8 * (c - low) + SPAN]
        out = part if out is None else jnp.where(member(coarse, c), part, out)
    return out


def spread_lanes(x, lane_q):
    rows = [x]
    for half in (8, 4, 2, 1):
        low = lane_q % (2 * half) < half
        turned = [pltpu.roll(x, half * 8, 1) for x in rows]
        rows = ([jnp.where(low, x, y) for x, y in zip(rows, turned)]
                + [jnp.where(low, y, x) for x, y in zip(rows, turned)])
    return [rows[int(format(r, "04b")[::-1], 2)] for r in range(16)]


def sixteenth(base, r, tall):
    return pl.ds(base + 8 * r, 8) if tall else pl.ds(base + r, 8, stride=16)


def aligned(x, m):
    return pl.multiple_of(x, m)


def chunk_of(ref, c):
    return ref.at[pl.ds(c * CHUNK, CHUNK)]


def forward_kernel(subset, first, tall, lo_ref, frac_ref, win_ref, vol_hbm, grid_hbm, out_ref,
                   vol_ref, grid_ref, tot, acc, tiles, starts, grid_sem, vol_sem):
    chunks = vol_ref.shape[0] // CHUNK

    def fetch(c):
        return pltpu.make_async_copy(chunk_of(vol_hbm, c), chunk_of(vol_ref, c), vol_sem.at[c])

    grid_copy = pltpu.make_async_copy(grid_hbm, grid_ref, grid_sem)
    grid_copy.start()
    for c in range(min(DEPTH, chunks)):
        fetch(c).start()

    zero = jnp.zeros((2 * SPAN, LANES), jnp.float32)
    list_tiles(subset, win_ref, tiles, starts)

    def clear(t, at):
        acc[pl.ds(aligned(at // TILES * TALL + lax.rem(at, TILES) * SPAN, SPAN), 2 * SPAN), :] = zero

    over_tiles(tiles, starts, clear)
    out_ref[...] = jnp.zeros_like(out_ref)
    grid_copy.wait()

    width = SUB * BLK_SIDE
    group = BLK_SIDE // SUB
    slices = vol_ref.shape[1]
    col_group = (lax.broadcasted_iota(jnp.int32, (group * slices, width), 1) % BLK_SIDE) // SUB
    mine = col_group == lax.broadcasted_iota(jnp.int32, (group * slices, width), 0) // slices
    angle = lax.broadcasted_iota(jnp.int32, (1, LANES), 1) // R
    def chunk(c, carry):
        fetch(c).wait()

        @pl.when(c + DEPTH < chunks)
        def _():
            fetch(c + DEPTH).start()

        for i in range(CHUNK):
            block(c * CHUNK + i)
        return carry

    def block(b):
        frac = jnp.zeros((1, LANES), jnp.float32)
        for a in range(ANG_SUB):
            frac = jnp.where(angle == a, frac_ref[subset, a, b], frac)
        parts = []
        for g in range(group):
            at = slice(g * width, (g + 1) * width)
            f = footprint(grid_ref[at, :] + frac)
            wide = jnp.where(mine, jnp.tile(vol_ref[b, :, at], (group, 1)), 0.0)
            parts.append(jnp.dot(wide.astype(jnp.bfloat16), f, preferred_element_type=jnp.float32))
        part = jnp.transpose(jnp.concatenate(parts, axis=0))
        for a in range(ANG_SUB):
            at = pl.ds(a * TALL + PAD + lo_ref[subset, a, b], R)
            acc[at, :] += part[a * R:(a + 1) * R, :]

    lax.fori_loop(0, chunks, chunk, 0)
    lane_q = lax.broadcasted_iota(jnp.int32, (1, LANES), 1) // 8

    for a in range(ANG_SUB):
        def merge(t, i, a=a):
            base = aligned(a * TALL + PAD + i * SPAN, 32)
            tot[pl.ds(aligned(t * SPAN, SPAN), SPAN), :] = shifted(
                acc, base, [-int(o) for o in first[a]], lane_q)

        over_angle(a, tiles, starts, merge)

    def fold(t, at):
        rows = [tot[sixteenth(aligned(t * SPAN, SPAN), r, tall), :] for r in range(16)]
        for half in (1, 2, 4, 8):
            low = lane_q % (2 * half) < half
            rows = [jnp.where(low, x, y) + pltpu.roll(jnp.where(low, y, x), half * 8, 1)
                    for x, y in zip(rows[0::2], rows[1::2])]
        out_ref[pl.ds(aligned(at * 8, 8), 8), :] = rows[0]

    over_tiles(tiles, starts, fold)


def backward_kernel(subset, first, tall, lo_ref, frac_ref, win_ref, vol_hbm, base_ref, res_ref, own_ref,
                    out_hbm, last_ref,
                    vol_ref, out_ref, e_scr, res, rb, dd, tiles, starts, vol_sem, out_sem):
    chunks = vol_ref.shape[0] // CHUNK

    def fetch(c):
        return pltpu.make_async_copy(chunk_of(vol_hbm, c), chunk_of(vol_ref, c), vol_sem.at[c])

    def emit(c):
        return pltpu.make_async_copy(chunk_of(out_ref, c), chunk_of(out_hbm, c), out_sem.at[c])

    for c in range(min(DEPTH, chunks)):
        fetch(c).start()
    fill_grid(base_ref, e_scr)
    lane_q = lax.broadcasted_iota(jnp.int32, (1, LANES), 1) // 8
    last_ref[...] = own_ref[...]
    res[...] = res_ref[...].astype(jnp.float32)
    list_tiles(subset, win_ref, tiles, starts)

    def widen(t, at):
        rows = spread_lanes(res[pl.ds(aligned(at * 8, 8), 8), :], lane_q)
        base = aligned(at // TILES * TALL + PAD + lax.rem(at, TILES) * SPAN, 32)
        for r in range(16):
            rb[sixteenth(base, r, tall), :] = rows[r]

    over_tiles(tiles, starts, widen)

    for a in range(ANG_SUB):
        def shift(t, i, a=a):
            base = aligned(a * TALL + PAD + i * SPAN, 32)
            dd[pl.ds(aligned(a * RAYS + i * SPAN, SPAN), SPAN), :] = shifted(
                rb, base, [int(o) for o in first[a]], lane_q)

        over_angle(a, tiles, starts, shift)

    width = SUB * BLK_SIDE
    group = BLK_SIDE // SUB
    lane = lax.broadcasted_iota(jnp.int32, (8, width), 1)
    col_group = (lane % BLK_SIDE) // SUB

    def block(b):
        rows = jnp.concatenate(
            [dd[pl.ds(a * RAYS + lo_ref[subset, a, b], R), :] for a in range(ANG_SUB)], axis=0)
        turned = jnp.transpose(rows)
        ones = jnp.ones((8, ANG_SUB * R), jnp.float32)
        for g in range(group):
            lhs = jnp.concatenate([turned[g * 32:(g + 1) * 32], ones], axis=0).astype(jnp.bfloat16)
            at = slice(g * width, (g + 1) * width)
            f = jnp.concatenate(
                [footprint(e_scr[a * R:(a + 1) * R, at] + frac_ref[subset, a, b]) for a in range(ANG_SUB)], axis=0)
            part = jnp.dot(lhs, f, preferred_element_type=jnp.float32)
            back = part[0:8]
            for j in range(1, group):
                back = jnp.where(col_group == j, part[j * 8:(j + 1) * 8], back)
            col_sum = part[32:40]
            out_ref[b, :, at] = jnp.maximum(vol_ref[b, :, at] + relax * back / col_sum, 0.0)

    def chunk(c, carry):
        fetch(c).wait()

        @pl.when(c + DEPTH < chunks)
        def _():
            fetch(c + DEPTH).start()

        for i in range(CHUNK):
            block(c * CHUNK + i)
        emit(c).start()
        return carry

    lax.fori_loop(0, chunks, chunk, 0)
    for c in range(chunks):
        emit(c).wait()


def ray_sums(shape, big, small, inv, ray):
    side = IMG_BLK * BLK_SIDE
    half = side * 0.5
    count = side // 8
    part = lax.broadcasted_iota(jnp.int32, shape, 1) % 8
    start = (part * count).astype(jnp.float32) + (0.5 - half)
    start = ray - start * small

    def row(i, total):
        w = start - i.astype(jnp.float32) * small
        mid = jnp.clip(jnp.floor(w * inv) + 0.5, 2.5 - half, half - 2.5)
        t0 = mid * big - w
        for t in (t0 - 2 * big, t0 - big, t0, t0 + big, t0 + 2 * big):
            bump = jnp.maximum(1.0 - t * t, 0.0)
            total = total + bump * bump
        return total

    def fold(total):
        for d in (1, 2, 4):
            total = total + jnp.where(
                part // d % 2 == 0, pltpu.roll(total, LANES - d, 1), pltpu.roll(total, d, 1))
        return total

    early = count * EARLY // 8
    first = lax.fori_loop(0, early, row, jnp.zeros(shape, jnp.float32), unroll=4)
    return first, lambda total: fold(lax.fori_loop(early, count, row, total, unroll=4))


def ray_at(line, lane, tall):
    if tall:
        return line // 8 * LANES + lane // 8 * 8 + line % 8
    return line * 16 + lane // 8


def exchange_kernel(subset, tall, part_ref, live_ref, table_ref, meas_ref, gathered, own_ref,
                    keep, half, inbox, sums, lines_scr, flat, halves, meas, stage,
                    meas_sem, keep_sem, pair_send, pair_recv, send_sem, recv_sem, rs_send, rs_recv,
                    out_send, out_recv, back_send, back_recv):
    g, p = lax.axis_index("group"), lax.axis_index("patch")
    pairs, groups = inbox.shape[0], inbox.shape[1]
    n = groups * pairs
    lines = stage.shape[0]
    rows = own_ref.shape[0]
    parity, column = lax.rem(p, 2), p // 2
    partner = (g, column * 2 + 1 - parity)
    mesh_id = pl.DeviceIdType.MESH

    def peer(d):
        return lax.rem(column + d // groups, pairs), lax.rem(g + lax.rem(d, groups), groups)

    def source(d):
        return (lax.rem(column + pairs - d // groups, pairs),
                lax.rem(g + groups - lax.rem(d, groups), groups))

    barrier = pltpu.get_barrier_semaphore()
    pl.semaphore_signal(barrier, inc=1, device_id=partner, device_id_type=mesh_id)

    def greet(d, c):
        pc, pg = peer(d)
        pl.semaphore_signal(barrier, inc=1, device_id=(pg, pc * 2 + parity), device_id_type=mesh_id)
        return c

    lax.fori_loop(1, n, greet, 0)
    read = pltpu.make_async_copy(meas_ref.at[subset, pl.ds(g * rows, rows)], meas, meas_sem)
    read.start()
    kept = pltpu.make_async_copy(part_ref.at[:, parity], keep, keep_sem)
    kept.start()
    first_row = (p * groups + g) * rows
    mine = p // pairs
    line = lax.broadcasted_iota(jnp.int32, halves.shape[1:], 0)
    lane = lax.broadcasted_iota(jnp.int32, halves.shape[1:], 1)
    ray = lax.rem(first_row, NTILE) * RAYS_TILE + mine * (lines * 8) + ray_at(line, lane, tall)
    ray = (ray.astype(jnp.float32) + (0.5 - RAYS * 0.5)) * (1.0 / spread)
    a = first_row // NTILE
    early, rest = ray_sums(
        halves.shape[1:], table_ref[subset, 0, a], table_ref[subset, 1, a], table_ref[subset, 2, a], ray)
    pl.semaphore_wait(barrier, n)

    def swap(d):
        pc = lax.rem(column + d, pairs)
        return pltpu.make_async_remote_copy(
            src_ref=part_ref.at[pc, 1 - parity], dst_ref=half.at[pc], send_sem=pair_send.at[d],
            recv_sem=pair_recv.at[d], device_id=partner, device_id_type=mesh_id)

    def to_owner(d):
        pc, pg = peer(d)
        return pltpu.make_async_remote_copy(
            src_ref=sums.at[pc, pg], dst_ref=inbox.at[column, g], send_sem=send_sem.at[d],
            recv_sem=recv_sem.at[d], device_id=(pg, pc * 2 + parity), device_id_type=mesh_id)

    def go_swap(d, c):
        swap(d).start()
        return c

    def go_column(i, c):
        pc = lax.rem(column + i, pairs)
        swap(i).wait_recv()
        sums[pc] = (keep[pc] + half[pc]).astype(sums.dtype)

        def go(d, c):
            to_owner(d).start()
            return c

        return lax.fori_loop(jnp.maximum(i * groups, 1), (i + 1) * groups, go, c)

    lax.fori_loop(0, pairs, go_swap, 0)
    kept.wait()
    lax.fori_loop(0, pairs, go_column, 0)
    halves[mine] = rest(early)
    trade = pltpu.make_async_remote_copy(
        src_ref=halves.at[mine], dst_ref=halves.at[mine], send_sem=rs_send, recv_sem=rs_recv,
        device_id=(g, lax.rem(p + pairs, 2 * pairs)), device_id_type=mesh_id)
    trade.start()

    def got(d, c):
        to_owner(d).wait_recv()
        return c

    read.wait()
    wide = lines // rows
    lane_q = lax.broadcasted_iota(jnp.int32, (1, LANES), 1) // 8

    def retile(forth):
        def one(i, c):
            at = pl.ds(aligned(i * 8, 8), 8)
            for r, x in enumerate(spread_lanes(lines_scr[at, :], lane_q)):
                flat[sixteenth(0, r, not forth), :] = x
            out = flat[sixteenth(0, 0, forth), :]
            for r in range(1, 16):
                out = jnp.where(lane_q == r, flat[sixteenth(0, r, forth), :], out)
            lines_scr[at, :] = out
            return c

        if tall:
            lax.fori_loop(0, lines // 8, one, 0)

    for c in range(wide):
        lines_scr[pl.ds(c, rows, stride=wide), :] = meas[:, c * LANES:(c + 1) * LANES]
    retile(True)

    inbox[column, g] = sums[column, g]
    lax.fori_loop(1, n, got, 0)
    total = jnp.zeros(stage.shape, jnp.float32)
    for i in range(pairs):
        for j in range(groups):
            total = total + inbox[i, j].astype(jnp.float32)
    ray = ray_at(lax.broadcasted_iota(jnp.int32, stage.shape, 0),
                 lax.broadcasted_iota(jnp.int32, stage.shape, 1), tall)
    row = ray // RAYS_TILE
    live = jnp.zeros(stage.shape, jnp.int32)
    for r in range(rows):
        live = jnp.where(row == r, live_ref[subset, first_row + r], live)
    trade.wait()
    sums_of = jnp.concatenate([halves[0], halves[1]], axis=0)
    differ = lines_scr[...] - total / jnp.maximum(sums_of, 1.0)
    residual = jnp.where(ray - row * RAYS_TILE < live, differ, 0.0)
    lines_scr[...] = residual
    stage[...] = residual.astype(jnp.bfloat16)

    def to_all(d):
        pc, pg = peer(d)
        return pltpu.make_async_remote_copy(
            src_ref=stage, dst_ref=gathered.at[column, parity, g], send_sem=out_send.at[d],
            recv_sem=out_recv.at[d], device_id=(pg, pc * 2 + parity), device_id_type=mesh_id)

    def share(d):
        pc, pg = source(d)
        return pltpu.make_async_remote_copy(
            src_ref=gathered.at[pc, parity, pg], dst_ref=gathered.at[pc, parity, pg], send_sem=back_send.at[d],
            recv_sem=back_recv.at[d], device_id=partner, device_id_type=mesh_id)

    def go_all(d, c):
        to_all(d).start()
        return c

    def pass_on(d, c):
        to_all(d).wait_recv()
        share(d).start()
        return c

    def finish(d, c):
        share(d).wait()
        return c

    def sent(d, c):
        to_owner(d).wait_send()
        to_all(d).wait_send()
        return c

    def swapped(d, c):
        swap(d).wait_send()
        return c

    lax.fori_loop(1, n, go_all, 0)
    gathered[column, parity, g] = stage[...]
    share(0).start()
    retile(False)
    for c in range(wide):
        own_ref[:, c * LANES:(c + 1) * LANES] = lines_scr[pl.ds(c, rows, stride=wide), :]
    lax.fori_loop(1, n, pass_on, 0)
    lax.fori_loop(0, n, finish, 0)
    lax.fori_loop(1, n, sent, 0)
    lax.fori_loop(0, pairs, swapped, 0)


def exchange(subset, tall, partial, live, table, measured, rows, groups, patches):
    pairs = patches // 2
    lines = rows * measured.shape[2] // LANES
    shape = (pairs, 2, groups, lines, LANES)
    n = pairs * groups
    wire = jnp.bfloat16 if subset < SUBSETS - 1 else jnp.float32
    dma = pltpu.SemaphoreType.DMA
    vmem = pl.BlockSpec(memory_space=pltpu.VMEM)
    full, own = pl.pallas_call(
        lambda *refs: exchange_kernel(subset, tall, *refs),
        in_specs=[pl.BlockSpec(memory_space=pl.ANY), smem(), smem(), pl.BlockSpec(memory_space=pl.ANY)],
        out_specs=[vmem] * 2,
        out_shape=[jax.ShapeDtypeStruct(shape, jnp.bfloat16),
                   jax.ShapeDtypeStruct((rows, measured.shape[2]), jnp.float32)],
        scratch_shapes=[pltpu.VMEM((pairs, groups, lines, LANES), jnp.float32),
                        pltpu.VMEM((pairs, groups, lines, LANES), jnp.float32),
                        pltpu.VMEM((pairs, groups, lines, LANES), wire),
                        pltpu.VMEM((pairs, groups, lines, LANES), wire),
                        pltpu.VMEM((lines, LANES), jnp.float32),
                        pltpu.VMEM((SPAN, LANES), jnp.float32),
                        pltpu.VMEM((2, lines // 2, LANES), jnp.float32),
                        pltpu.VMEM((rows, measured.shape[2]), jnp.float32),
                        pltpu.VMEM((lines, LANES), jnp.bfloat16),
                        dma, dma, dma((pairs,)), dma((pairs,)), dma((n,)), dma((n,)), dma, dma,
                        dma((n,)), dma((n,)), dma((n,)), dma((n,))],
        compiler_params=pltpu.CompilerParams(collective_id=subset, has_side_effects=True),
        name="exchange",
    )(partial.reshape(shape), live, table, measured)
    return full.reshape(partial.shape), own


def smem():
    return pl.BlockSpec(memory_space=pltpu.SMEM)


def forward(subset, tall, volume, lo, frac, win, base, first):
    blocks = volume.shape[0]
    lines = ANG_SUB * RAYS // 16
    grid = (np.repeat(base, R, axis=0) - np.tile(np.arange(R), ANG_SUB)[:, None]) * (1.0 / spread)
    vmem = pl.BlockSpec(memory_space=pltpu.VMEM)
    hbm = pl.BlockSpec(memory_space=pl.ANY)
    dma = pltpu.SemaphoreType.DMA
    return pl.pallas_call(
        lambda *refs: forward_kernel(subset, first, tall, *refs),
        in_specs=[smem(), smem(), smem(), hbm, hbm],
        out_specs=vmem,
        out_shape=jax.ShapeDtypeStruct((lines, LANES), jnp.float32),
        scratch_shapes=[pltpu.VMEM(volume.shape, jnp.float32),
                        pltpu.VMEM((VOX, LANES), jnp.float32),
                        pltpu.VMEM((ANG_SUB * RAYS, LANES), jnp.float32),
                        pltpu.VMEM((ANG_SUB * TALL, LANES), jnp.float32),
                        pltpu.SMEM((ANG_SUB * TILES + 1,), jnp.int32),
                        pltpu.SMEM((ANG_SUB + 1,), jnp.int32),
                        dma, dma((blocks // CHUNK,))],
        compiler_params=pltpu.CompilerParams(vmem_limit_bytes=VMEM_LIMIT),
        name="forward",
    )(lo, frac, win, volume, grid.T.astype(np.float32))


def backward(subset, tall, volume, residual, own, lo, frac, win, base, first):
    blocks = volume.shape[0]
    vmem = pl.BlockSpec(memory_space=pltpu.VMEM)
    hbm = pl.BlockSpec(memory_space=pl.ANY)
    dma = pltpu.SemaphoreType.DMA
    return pl.pallas_call(
        lambda *refs: backward_kernel(subset, first, tall, *refs),
        in_specs=[smem(), smem(), smem(), hbm, vmem, vmem, vmem],
        out_specs=[hbm, vmem],
        out_shape=[jax.ShapeDtypeStruct(volume.shape, jnp.float32),
                   jax.ShapeDtypeStruct(own.shape, jnp.float32)],
        scratch_shapes=[pltpu.VMEM(volume.shape, jnp.float32),
                        pltpu.VMEM(volume.shape, jnp.float32),
                        pltpu.VMEM((ANG_SUB * R, VOX), jnp.float32),
                        pltpu.VMEM(residual.shape, jnp.float32),
                        pltpu.VMEM((ANG_SUB * TALL, LANES), jnp.float32),
                        pltpu.VMEM((ANG_SUB * RAYS, LANES), jnp.float32),
                        pltpu.SMEM((ANG_SUB * TILES + 1,), jnp.int32),
                        pltpu.SMEM((ANG_SUB + 1,), jnp.int32),
                        dma((blocks // CHUNK,)), dma((blocks // CHUNK,))],
        compiler_params=pltpu.CompilerParams(vmem_limit_bytes=VMEM_LIMIT),
        name="backward",
    )(lo, frac, win, volume, base, residual, own)


def ray_table():
    table = np.zeros((SUBSETS, 3, ANG_SUB), np.float64)
    for subset in range(SUBSETS):
        for a, t in enumerate(angles(subset)):
            small, big = sorted((abs(math.cos(t)), abs(math.sin(t))))
            table[subset, :, a] = big / spread, small / spread, spread / big
    return table.astype(np.float32)


def placing_kernel(place_ref, lo_ref, frac_ref, win_ref):
    half = IMG_BLK * BLK_SIDE * 0.5
    shape = lo_ref.shape[1:]
    place = jnp.broadcast_to(place_ref[...], shape)
    x = (place % IMG_BLK).astype(jnp.float32) * BLK_SIDE + (BLK_SIDE * 0.5 - half)
    y = (place // IMG_BLK).astype(jnp.float32) * BLK_SIDE + (BLK_SIDE * 0.5 - half)
    angle = lax.broadcasted_iota(jnp.int32, shape, 0)
    tile = lax.broadcasted_iota(jnp.int32, (TILES, shape[1]), 0)
    near = []
    for subset in range(SUBSETS):
        cosine = sine = jnp.zeros(shape, jnp.float32)
        for a, theta in enumerate(angles(subset)):
            cosine = jnp.where(angle == a, np.float32(math.cos(theta)), cosine)
            sine = jnp.where(angle == a, np.float32(math.sin(theta)), sine)
        z = x * cosine + y * sine + (RAYS * 0.5 - 0.5)
        low = jnp.floor(z)
        lo = low.astype(jnp.int32)
        lo_ref[subset] = lo
        frac_ref[subset] = (z - low) * (1.0 / spread)
        ends = (lo - PAD) // SPAN, (lo + R + PAD) // SPAN
        for a in range(ANG_SUB):
            hit = (ends[0][a:a + 1] == tile) | (ends[1][a:a + 1] == tile)
            near.append(jnp.where(hit, 1.0, 0.0))
    count = lax.dot_general(jnp.ones((8, shape[1]), jnp.bfloat16), jnp.concatenate(near, axis=0).astype(jnp.bfloat16),
                            (((1,), (1,)), ((), ())), preferred_element_type=jnp.float32)
    win_ref[...] = jnp.where(count[0:1] > 0.0, 1, 0)


def placing(place):
    shape = (SUBSETS, ANG_SUB, place.shape[0])
    return pl.pallas_call(
        placing_kernel,
        out_shape=[jax.ShapeDtypeStruct(shape, jnp.int32), jax.ShapeDtypeStruct(shape, jnp.float32),
                   jax.ShapeDtypeStruct((1, SUBSETS * ANG_SUB * TILES), jnp.int32)],
        name="placing",
    )(place.reshape(1, -1))


def shards(volume, block_place, measured, live_rays):
    groups = lax.axis_size("group")
    patches = lax.axis_size("patch")
    rows = ANG_SUB * NTILE // patches // groups
    lo, frac, win = placing(block_place)
    table = ray_table()
    tall = rows * RAYS_TILE % (2 * LANES) == 0
    estimate = volume
    own = None
    for subset in range(SUBSETS):
        base, first = geometry(subset)
        partial = forward(subset, tall, estimate, lo, frac, win, base, first)
        full, own = exchange(subset, tall, partial, live_rays, table, measured, rows, groups, patches)
        estimate, own = backward(subset, tall, estimate, full, own, lo, frac, win, base, first)
    return (estimate, own[None])


def solution(mesh):
    return jax.shard_map(
        shards,
        mesh=mesh,
        in_specs=(
            P(("group", "patch"), None, None),
            P(("group", "patch")),
            P(None, "patch", None),
            P(),
        ),
        out_specs=(P(("group", "patch"), None, None), P("group", "patch", None)),
        check_vma=False,
    )
```

```python
import math

import jax
import jax.numpy as jnp
import numpy as np
from jax import lax
from jax.experimental import pallas as pl
from jax.experimental.pallas import tpu as pltpu
from jax.sharding import PartitionSpec as P

IMG_BLK = 64
BLK_SIDE = 32
RAYS_TILE = 48
NTILE = 64
ANG_SUB = 8
SUBSETS = 2

spread = 1.5
relax = 0.9

SUB = 8
NQ = (BLK_SIDE // SUB) ** 2
R = 16
VOX = BLK_SIDE * BLK_SIDE
RAYS = NTILE * RAYS_TILE
LANES = 128
PAD = 32
CHUNK = 32
MADE = 4
MADE_EARLY = (3, 8)
DEPTH = 2
EARLY = 3
SPAN = 128
TALL = RAYS + SPAN
VMEM_LIMIT = 60 * 1024 * 1024


def angles(subset):
    return [math.pi * (a * SUBSETS + subset) / (ANG_SUB * SUBSETS) for a in range(ANG_SUB)]


def geometry(subset):
    v = np.arange(VOX)
    col = (v % BLK_SIDE) + 0.5 - BLK_SIDE / 2
    row = (v // BLK_SIDE) + 0.5 - BLK_SIDE / 2
    q_of = (v // BLK_SIDE // SUB) * (BLK_SIDE // SUB) + (v % BLK_SIDE) // SUB
    base = np.zeros((ANG_SUB, VOX), np.float64)
    first = np.zeros((ANG_SUB, NQ), np.int64)
    for a, theta in enumerate(angles(subset)):
        off = col * math.cos(theta) + row * math.sin(theta)
        for q in range(NQ):
            mine = q_of == q
            first[a, q] = math.floor(off[mine].min() - spread)
            base[a, mine] = off[mine] - first[a, q]
    return base.astype(np.float32), first.astype(np.int32)


def fill_grid(base_ref, e_scr):
    ray = lax.broadcasted_iota(jnp.int32, (R, VOX), 0).astype(jnp.float32)
    for a in range(ANG_SUB):
        e_scr[a * R:(a + 1) * R, :] = (base_ref[a:a + 1, :] - ray) * (1.0 / spread)


def footprint(t):
    t = t.astype(jnp.bfloat16)
    bump = jnp.maximum(1.0 - t * t, 0.0)
    return bump * bump


TILES = RAYS // SPAN


WIDE = 16


def list_tiles(subset, win_ref, tiles, starts):
    def angle(a, n):
        starts[a] = n
        for i in range(TILES):
            hit = win_ref[0, (subset * ANG_SUB + a) * TILES + i]
            tiles[n] = a * TILES + i
            n = n + hit
        return n

    starts[ANG_SUB] = lax.fori_loop(0, ANG_SUB, angle, 0)


def over_tiles(tiles, starts, body):
    n = starts[ANG_SUB]

    def some(i, c):
        for j in range(WIDE):
            t = jnp.minimum(WIDE * i + j, n - 1)
            body(t, tiles[t])
        return c

    lax.fori_loop(0, (n + WIDE - 1) // WIDE, some, 0)


def over_angle(a, tiles, starts, body):
    def one(t, c):
        body(t, tiles[t] - a * TILES)
        return c

    lax.fori_loop(starts[a], starts[a + 1], one, 0)


def shifted(ref, base, offsets, lane_q):
    fine = [o % 8 for o in offsets]
    coarse = [o // 8 for o in offsets]
    low, high = min(coarse), max(coarse)

    def member(values, value):
        hits = [lane_q == q for q, v in enumerate(values) if v == value]
        mask = hits[0]
        for h in hits[1:]:
            mask = mask | h
        return mask

    rows = None
    for f in sorted(set(fine)):
        part = ref[pl.ds(base + 8 * low + f, SPAN + 8 * (high - low)), :]
        rows = part if rows is None else jnp.where(member(fine, f), part, rows)
    out = None
    for c in sorted(set(coarse)):
        part = rows[8 * (c - low):8 * (c - low) + SPAN]
        out = part if out is None else jnp.where(member(coarse, c), part, out)
    return out


def spread_lanes(x, lane_q):
    rows = [x]
    for half in (8, 4, 2, 1):
        low = lane_q % (2 * half) < half
        turned = [pltpu.roll(x, half * 8, 1) for x in rows]
        rows = ([jnp.where(low, x, y) for x, y in zip(rows, turned)]
                + [jnp.where(low, y, x) for x, y in zip(rows, turned)])
    return [rows[int(format(r, "04b")[::-1], 2)] for r in range(16)]


def sixteenth(base, r, tall):
    return pl.ds(base + 8 * r, 8) if tall else pl.ds(base + r, 8, stride=16)


def aligned(x, m):
    return pl.multiple_of(x, m)


def size_of(ref):
    return min(CHUNK, ref.shape[0] // 2)


def chunk_of(ref, c):
    return ref.at[pl.ds(c * size_of(ref), size_of(ref))]


def forward_kernel(subset, first, tall, lo_ref, frac_ref, win_ref, vol_hbm, grid_hbm, out_ref,
                   vol_ref, grid_ref, tot, acc, tiles, starts, grid_sem, vol_sem):
    size = size_of(vol_ref)
    chunks = vol_ref.shape[0] // size

    def fetch(c):
        return pltpu.make_async_copy(chunk_of(vol_hbm, c), chunk_of(vol_ref, c), vol_sem.at[c])

    grid_copy = pltpu.make_async_copy(grid_hbm, grid_ref, grid_sem)
    grid_copy.start()
    for c in range(min(DEPTH, chunks)):
        fetch(c).start()

    zero = jnp.zeros((2 * SPAN, LANES), jnp.float32)
    list_tiles(subset, win_ref, tiles, starts)

    def clear(t, at):
        acc[pl.ds(aligned(at // TILES * TALL + lax.rem(at, TILES) * SPAN, SPAN), 2 * SPAN), :] = zero

    over_tiles(tiles, starts, clear)
    out_ref[...] = jnp.zeros_like(out_ref)
    grid_copy.wait()

    width = SUB * BLK_SIDE
    group = BLK_SIDE // SUB
    slices = vol_ref.shape[1]
    col_group = (lax.broadcasted_iota(jnp.int32, (group * slices, width), 1) % BLK_SIDE) // SUB
    mine = col_group == lax.broadcasted_iota(jnp.int32, (group * slices, width), 0) // slices
    angle = lax.broadcasted_iota(jnp.int32, (1, LANES), 1) // R
    def chunk(c, carry):
        fetch(c).wait()

        @pl.when(c + DEPTH < chunks)
        def _():
            fetch(c + DEPTH).start()

        for i in range(size):
            block(c * size + i)
        return carry

    def block(b):
        frac = jnp.zeros((1, LANES), jnp.float32)
        for a in range(ANG_SUB):
            frac = jnp.where(angle == a, frac_ref[subset, a, b], frac)
        parts = []
        for g in range(group):
            at = slice(g * width, (g + 1) * width)
            f = footprint(grid_ref[at, :] + frac)
            wide = jnp.where(mine, jnp.tile(vol_ref[b, :, at], (group, 1)), 0.0)
            parts.append(jnp.dot(wide.astype(jnp.bfloat16), f, preferred_element_type=jnp.float32))
        part = jnp.transpose(jnp.concatenate(parts, axis=0))
        for a in range(ANG_SUB):
            at = pl.ds(a * TALL + PAD + lo_ref[subset, a, b], R)
            acc[at, :] += part[a * R:(a + 1) * R, :]

    lax.fori_loop(0, chunks, chunk, 0)
    lane_q = lax.broadcasted_iota(jnp.int32, (1, LANES), 1) // 8

    for a in range(ANG_SUB):
        def merge(t, i, a=a):
            base = aligned(a * TALL + PAD + i * SPAN, 32)
            tot[pl.ds(aligned(t * SPAN, SPAN), SPAN), :] = shifted(
                acc, base, [-int(o) for o in first[a]], lane_q)

        over_angle(a, tiles, starts, merge)

    def fold(t, at):
        rows = [tot[sixteenth(aligned(t * SPAN, SPAN), r, tall), :] for r in range(16)]
        for half in (1, 2, 4, 8):
            low = lane_q % (2 * half) < half
            rows = [jnp.where(low, x, y) + pltpu.roll(jnp.where(low, y, x), half * 8, 1)
                    for x, y in zip(rows[0::2], rows[1::2])]
        out_ref[pl.ds(aligned(at * 8, 8), 8), :] = rows[0]

    over_tiles(tiles, starts, fold)


def backward_kernel(subset, first, tall, lo_ref, frac_ref, win_ref, vol_hbm, made_hbm, base_ref, res_ref, own_ref,
                    out_hbm, last_ref,
                    vol_ref, out_ref, made, e_scr, res, rb, dd, tiles, starts, vol_sem, out_sem, made_sem):
    size = size_of(vol_ref)
    chunks = vol_ref.shape[0] // size

    def fetch(c):
        return pltpu.make_async_copy(chunk_of(vol_hbm, c), chunk_of(vol_ref, c), vol_sem.at[c])

    def emit(c):
        return pltpu.make_async_copy(chunk_of(out_ref, c), chunk_of(out_hbm, c), out_sem.at[c])

    def load(c):
        at = pl.ds(c * MADE, MADE)
        return pltpu.make_async_copy(made_hbm.at[at], made.at[at], made_sem.at[c])

    for c in range(min(DEPTH, chunks)):
        fetch(c).start()
    for c in range(made.shape[0] // MADE):
        load(c).start()
    fill_grid(base_ref, e_scr)
    lane_q = lax.broadcasted_iota(jnp.int32, (1, LANES), 1) // 8
    last_ref[...] = own_ref[...]
    res[...] = res_ref[...].astype(jnp.float32)
    list_tiles(subset, win_ref, tiles, starts)

    def widen(t, at):
        rows = spread_lanes(res[pl.ds(aligned(at * 8, 8), 8), :], lane_q)
        base = aligned(at // TILES * TALL + PAD + lax.rem(at, TILES) * SPAN, 32)
        for r in range(16):
            rb[sixteenth(base, r, tall), :] = rows[r]

    over_tiles(tiles, starts, widen)

    for a in range(ANG_SUB):
        def shift(t, i, a=a):
            base = aligned(a * TALL + PAD + i * SPAN, 32)
            dd[pl.ds(aligned(a * RAYS + i * SPAN, SPAN), SPAN), :] = shifted(
                rb, base, [int(o) for o in first[a]], lane_q)

        over_angle(a, tiles, starts, shift)

    width = SUB * BLK_SIDE
    group = BLK_SIDE // SUB
    lane = lax.broadcasted_iota(jnp.int32, (8, width), 1)
    col_group = (lane % BLK_SIDE) // SUB

    def block(b, ready):
        rows = jnp.concatenate(
            [dd[pl.ds(a * RAYS + lo_ref[subset, a, b], R), :] for a in range(ANG_SUB)], axis=0)
        turned = jnp.transpose(rows)
        ones = jnp.ones((8, ANG_SUB * R), jnp.float32)
        for g in range(group):
            lhs = jnp.concatenate([turned[g * 32:(g + 1) * 32], ones], axis=0).astype(jnp.bfloat16)
            at = slice(g * width, (g + 1) * width)
            if ready:
                f = made[b - made.shape[0], :, at]
            else:
                f = jnp.concatenate([footprint(e_scr[a * R:(a + 1) * R, at] + frac_ref[subset, a, b])
                                     for a in range(ANG_SUB)], axis=0)
            part = jnp.dot(lhs, f, preferred_element_type=jnp.float32)
            back = part[0:8]
            for j in range(1, group):
                back = jnp.where(col_group == j, part[j * 8:(j + 1) * 8], back)
            col_sum = part[32:40]
            out_ref[b, :, at] = jnp.maximum(vol_ref[b, :, at] + relax * back / col_sum, 0.0)

    def chunk(c, carry, ready):
        fetch(c).wait()

        @pl.when(c + DEPTH < chunks)
        def _():
            fetch(c + DEPTH).start()

        for i in range(size):
            block(c * size + i, ready)
        emit(c).start()
        return carry

    lax.fori_loop(0, chunks // 2, lambda c, carry: chunk(c, carry, False), 0)
    for c in range(made.shape[0] // MADE):
        load(c).wait()
    lax.fori_loop(chunks // 2, chunks, lambda c, carry: chunk(c, carry, True), 0)
    for c in range(chunks):
        emit(c).wait()


def ray_sums(shape, big, small, inv, ray):
    side = IMG_BLK * BLK_SIDE
    half = side * 0.5
    count = side // 8
    part = lax.broadcasted_iota(jnp.int32, shape, 1) % 8
    start = (part * count).astype(jnp.float32) + (0.5 - half)
    start = ray - start * small

    def row(i, total):
        w = start - i.astype(jnp.float32) * small
        mid = jnp.clip(jnp.floor(w * inv) + 0.5, 2.5 - half, half - 2.5)
        t0 = mid * big - w
        for t in (t0 - 2 * big, t0 - big, t0, t0 + big, t0 + 2 * big):
            bump = jnp.maximum(1.0 - t * t, 0.0)
            total = total + bump * bump
        return total

    def fold(total):
        for d in (1, 2, 4):
            total = total + jnp.where(
                part // d % 2 == 0, pltpu.roll(total, LANES - d, 1), pltpu.roll(total, d, 1))
        return total

    early = count * EARLY // 8
    first = lax.fori_loop(0, early, row, jnp.zeros(shape, jnp.float32), unroll=4)
    return first, lambda total: fold(lax.fori_loop(early, count, row, total, unroll=4))


def ray_at(line, lane, tall):
    if tall:
        return line // 8 * LANES + lane // 8 * 8 + line % 8
    return line * 16 + lane // 8


def exchange_kernel(subset, tall, part_ref, live_ref, table_ref, frac_ref, meas_ref, base_ref, gathered, own_ref, made_hbm,
                    keep, half, inbox, sums, lines_scr, flat, halves, meas, stage, e_scr, made,
                    meas_sem, keep_sem, pair_send, pair_recv, send_sem, recv_sem, rs_send, rs_recv,
                    out_send, out_recv, back_send, back_recv, made_sem):
    g, p = lax.axis_index("group"), lax.axis_index("patch")
    pairs, groups = inbox.shape[0], inbox.shape[1]
    n = groups * pairs
    lines = stage.shape[0]
    rows = own_ref.shape[0]
    parity, column = lax.rem(p, 2), p // 2
    partner = (g, column * 2 + 1 - parity)
    mesh_id = pl.DeviceIdType.MESH

    def peer(d):
        return lax.rem(column + d // groups, pairs), lax.rem(g + lax.rem(d, groups), groups)

    def source(d):
        return (lax.rem(column + pairs - d // groups, pairs),
                lax.rem(g + groups - lax.rem(d, groups), groups))

    barrier = pltpu.get_barrier_semaphore()
    pl.semaphore_signal(barrier, inc=1, device_id=partner, device_id_type=mesh_id)

    def greet(d, c):
        pc, pg = peer(d)
        pl.semaphore_signal(barrier, inc=1, device_id=(pg, pc * 2 + parity), device_id_type=mesh_id)
        return c

    lax.fori_loop(1, n, greet, 0)
    read = pltpu.make_async_copy(meas_ref.at[subset, pl.ds(g * rows, rows)], meas, meas_sem)
    read.start()
    kept = pltpu.make_async_copy(part_ref.at[:, parity], keep, keep_sem)
    kept.start()
    first_row = (p * groups + g) * rows
    mine = p // pairs
    line = lax.broadcasted_iota(jnp.int32, halves.shape[1:], 0)
    lane = lax.broadcasted_iota(jnp.int32, halves.shape[1:], 1)
    ray = lax.rem(first_row, NTILE) * RAYS_TILE + mine * (lines * 8) + ray_at(line, lane, tall)
    ray = (ray.astype(jnp.float32) + (0.5 - RAYS * 0.5)) * (1.0 / spread)
    a = first_row // NTILE
    early, rest = ray_sums(
        halves.shape[1:], table_ref[subset, 0, a], table_ref[subset, 1, a], table_ref[subset, 2, a], ray)
    fill_grid(base_ref, e_scr)
    pl.semaphore_wait(barrier, n)

    def put(i):
        slot = lax.rem(i, 2)
        return pltpu.make_async_copy(made.at[slot], made_hbm.at[pl.ds(i * MADE, MADE)], made_sem.at[slot])

    def make(i, c):
        @pl.when(i >= 2)
        def _():
            put(i - 2).wait()

        for k in range(MADE):
            b = frac_ref.shape[2] // 2 + i * MADE + k
            for a in range(ANG_SUB):
                made[lax.rem(i, 2), k, a * R:(a + 1) * R, :] = footprint(
                    e_scr[a * R:(a + 1) * R, :] + frac_ref[subset, a, b])
        put(i).start()
        return c

    steps = made_hbm.shape[0] // MADE
    early_steps = min(MADE_EARLY[subset], steps)

    def swap(d):
        pc = lax.rem(column + d, pairs)
        return pltpu.make_async_remote_copy(
            src_ref=part_ref.at[pc, 1 - parity], dst_ref=half.at[pc], send_sem=pair_send.at[d],
            recv_sem=pair_recv.at[d], device_id=partner, device_id_type=mesh_id)

    def to_owner(d):
        pc, pg = peer(d)
        return pltpu.make_async_remote_copy(
            src_ref=sums.at[pc, pg], dst_ref=inbox.at[column, g], send_sem=send_sem.at[d],
            recv_sem=recv_sem.at[d], device_id=(pg, pc * 2 + parity), device_id_type=mesh_id)

    def go_swap(d, c):
        swap(d).start()
        return c

    def go_column(i, c):
        pc = lax.rem(column + i, pairs)
        swap(i).wait_recv()
        sums[pc] = (keep[pc] + half[pc]).astype(sums.dtype)

        def go(d, c):
            to_owner(d).start()
            return c

        return lax.fori_loop(jnp.maximum(i * groups, 1), (i + 1) * groups, go, c)

    lax.fori_loop(0, pairs, go_swap, 0)
    kept.wait()
    lax.fori_loop(0, pairs, go_column, 0)
    halves[mine] = rest(early)
    trade = pltpu.make_async_remote_copy(
        src_ref=halves.at[mine], dst_ref=halves.at[mine], send_sem=rs_send, recv_sem=rs_recv,
        device_id=(g, lax.rem(p + pairs, 2 * pairs)), device_id_type=mesh_id)
    trade.start()

    lax.fori_loop(0, early_steps, make, 0)

    def got(d, c):
        to_owner(d).wait_recv()
        return c

    read.wait()
    wide = lines // rows
    lane_q = lax.broadcasted_iota(jnp.int32, (1, LANES), 1) // 8

    def retile(forth):
        def one(i, c):
            at = pl.ds(aligned(i * 8, 8), 8)
            for r, x in enumerate(spread_lanes(lines_scr[at, :], lane_q)):
                flat[sixteenth(0, r, not forth), :] = x
            out = flat[sixteenth(0, 0, forth), :]
            for r in range(1, 16):
                out = jnp.where(lane_q == r, flat[sixteenth(0, r, forth), :], out)
            lines_scr[at, :] = out
            return c

        if tall:
            lax.fori_loop(0, lines // 8, one, 0)

    for c in range(wide):
        lines_scr[pl.ds(c, rows, stride=wide), :] = meas[:, c * LANES:(c + 1) * LANES]
    retile(True)

    inbox[column, g] = sums[column, g]
    lax.fori_loop(1, n, got, 0)
    total = jnp.zeros(stage.shape, jnp.float32)
    for i in range(pairs):
        for j in range(groups):
            total = total + inbox[i, j].astype(jnp.float32)
    ray = ray_at(lax.broadcasted_iota(jnp.int32, stage.shape, 0),
                 lax.broadcasted_iota(jnp.int32, stage.shape, 1), tall)
    row = ray // RAYS_TILE
    live = jnp.zeros(stage.shape, jnp.int32)
    for r in range(rows):
        live = jnp.where(row == r, live_ref[subset, first_row + r], live)
    trade.wait()
    sums_of = jnp.concatenate([halves[0], halves[1]], axis=0)
    differ = lines_scr[...] - total / jnp.maximum(sums_of, 1.0)
    residual = jnp.where(ray - row * RAYS_TILE < live, differ, 0.0)
    lines_scr[...] = residual
    stage[...] = residual.astype(jnp.bfloat16)

    def to_all(d):
        pc, pg = peer(d)
        return pltpu.make_async_remote_copy(
            src_ref=stage, dst_ref=gathered.at[column, parity, g], send_sem=out_send.at[d],
            recv_sem=out_recv.at[d], device_id=(pg, pc * 2 + parity), device_id_type=mesh_id)

    def share(d):
        pc, pg = source(d)
        return pltpu.make_async_remote_copy(
            src_ref=gathered.at[pc, parity, pg], dst_ref=gathered.at[pc, parity, pg], send_sem=back_send.at[d],
            recv_sem=back_recv.at[d], device_id=partner, device_id_type=mesh_id)

    def go_all(d, c):
        to_all(d).start()
        return c

    def pass_on(d, c):
        to_all(d).wait_recv()
        share(d).start()
        return c

    def finish(d, c):
        share(d).wait()
        return c

    def sent(d, c):
        to_owner(d).wait_send()
        to_all(d).wait_send()
        return c

    def swapped(d, c):
        swap(d).wait_send()
        return c

    lax.fori_loop(1, n, go_all, 0)
    gathered[column, parity, g] = stage[...]
    share(0).start()
    lax.fori_loop(early_steps, steps, make, 0)
    retile(False)
    for c in range(wide):
        own_ref[:, c * LANES:(c + 1) * LANES] = lines_scr[pl.ds(c, rows, stride=wide), :]
    lax.fori_loop(1, n, pass_on, 0)
    lax.fori_loop(0, n, finish, 0)
    lax.fori_loop(1, n, sent, 0)
    lax.fori_loop(0, pairs, swapped, 0)
    for i in range(max(steps - 2, 0), steps):
        put(i).wait()


def exchange(subset, tall, partial, live, table, frac, measured, base, rows, groups, patches):
    pairs = patches // 2
    lines = rows * measured.shape[2] // LANES
    shape = (pairs, 2, groups, lines, LANES)
    n = pairs * groups
    wire = jnp.bfloat16 if subset < SUBSETS - 1 else jnp.float32
    dma = pltpu.SemaphoreType.DMA
    vmem = pl.BlockSpec(memory_space=pltpu.VMEM)
    full, own, made = pl.pallas_call(
        lambda *refs: exchange_kernel(subset, tall, *refs),
        in_specs=[pl.BlockSpec(memory_space=pl.ANY), smem(), smem(), smem(), pl.BlockSpec(memory_space=pl.ANY), vmem],
        out_specs=[vmem, vmem, pl.BlockSpec(memory_space=pl.ANY)],
        out_shape=[jax.ShapeDtypeStruct(shape, jnp.bfloat16),
                   jax.ShapeDtypeStruct((rows, measured.shape[2]), jnp.float32),
                   jax.ShapeDtypeStruct((frac.shape[2] // 2, LANES, VOX), jnp.bfloat16)],
        scratch_shapes=[pltpu.VMEM((pairs, groups, lines, LANES), jnp.float32),
                        pltpu.VMEM((pairs, groups, lines, LANES), jnp.float32),
                        pltpu.VMEM((pairs, groups, lines, LANES), wire),
                        pltpu.VMEM((pairs, groups, lines, LANES), wire),
                        pltpu.VMEM((lines, LANES), jnp.float32),
                        pltpu.VMEM((SPAN, LANES), jnp.float32),
                        pltpu.VMEM((2, lines // 2, LANES), jnp.float32),
                        pltpu.VMEM((rows, measured.shape[2]), jnp.float32),
                        pltpu.VMEM((lines, LANES), jnp.bfloat16),
                        pltpu.VMEM((LANES, VOX), jnp.float32),
                        pltpu.VMEM((2, MADE, LANES, VOX), jnp.bfloat16),
                        dma, dma, dma((pairs,)), dma((pairs,)), dma((n,)), dma((n,)), dma, dma,
                        dma((n,)), dma((n,)), dma((n,)), dma((n,)), dma((2,))],
        compiler_params=pltpu.CompilerParams(collective_id=subset, has_side_effects=True),
        name="exchange",
    )(partial.reshape(shape), live, table, frac, measured, base)
    return full.reshape(partial.shape), own, made


def smem():
    return pl.BlockSpec(memory_space=pltpu.SMEM)


def forward(subset, tall, volume, lo, frac, win, base, first):
    blocks = volume.shape[0]
    lines = ANG_SUB * RAYS // 16
    grid = (np.repeat(base, R, axis=0) - np.tile(np.arange(R), ANG_SUB)[:, None]) * (1.0 / spread)
    vmem = pl.BlockSpec(memory_space=pltpu.VMEM)
    hbm = pl.BlockSpec(memory_space=pl.ANY)
    dma = pltpu.SemaphoreType.DMA
    return pl.pallas_call(
        lambda *refs: forward_kernel(subset, first, tall, *refs),
        in_specs=[smem(), smem(), smem(), hbm, hbm],
        out_specs=vmem,
        out_shape=jax.ShapeDtypeStruct((lines, LANES), jnp.float32),
        scratch_shapes=[pltpu.VMEM(volume.shape, jnp.float32),
                        pltpu.VMEM((VOX, LANES), jnp.float32),
                        pltpu.VMEM((ANG_SUB * RAYS, LANES), jnp.float32),
                        pltpu.VMEM((ANG_SUB * TALL, LANES), jnp.float32),
                        pltpu.SMEM((ANG_SUB * TILES + 1,), jnp.int32),
                        pltpu.SMEM((ANG_SUB + 1,), jnp.int32),
                        dma, dma((blocks // min(CHUNK, blocks // 2),))],
        compiler_params=pltpu.CompilerParams(vmem_limit_bytes=VMEM_LIMIT),
        name="forward",
    )(lo, frac, win, volume, grid.T.astype(np.float32))


def backward(subset, tall, volume, made, residual, own, lo, frac, win, base, first):
    blocks = volume.shape[0]
    vmem = pl.BlockSpec(memory_space=pltpu.VMEM)
    hbm = pl.BlockSpec(memory_space=pl.ANY)
    dma = pltpu.SemaphoreType.DMA
    return pl.pallas_call(
        lambda *refs: backward_kernel(subset, first, tall, *refs),
        in_specs=[smem(), smem(), smem(), hbm, hbm, vmem, vmem, vmem],
        out_specs=[hbm, vmem],
        out_shape=[jax.ShapeDtypeStruct(volume.shape, jnp.float32),
                   jax.ShapeDtypeStruct(own.shape, jnp.float32)],
        scratch_shapes=[pltpu.VMEM(volume.shape, jnp.float32),
                        pltpu.VMEM(volume.shape, jnp.float32),
                        pltpu.VMEM(made.shape, jnp.bfloat16),
                        pltpu.VMEM((ANG_SUB * R, VOX), jnp.float32),
                        pltpu.VMEM(residual.shape, jnp.float32),
                        pltpu.VMEM((ANG_SUB * TALL, LANES), jnp.float32),
                        pltpu.VMEM((ANG_SUB * RAYS, LANES), jnp.float32),
                        pltpu.SMEM((ANG_SUB * TILES + 1,), jnp.int32),
                        pltpu.SMEM((ANG_SUB + 1,), jnp.int32),
                        dma((blocks // min(CHUNK, blocks // 2),)), dma((blocks // min(CHUNK, blocks // 2),)),
                        dma((made.shape[0] // MADE,))],
        compiler_params=pltpu.CompilerParams(vmem_limit_bytes=VMEM_LIMIT),
        name="backward",
    )(lo, frac, win, volume, made, base, residual, own)


def ray_table():
    table = np.zeros((SUBSETS, 3, ANG_SUB), np.float64)
    for subset in range(SUBSETS):
        for a, t in enumerate(angles(subset)):
            small, big = sorted((abs(math.cos(t)), abs(math.sin(t))))
            table[subset, :, a] = big / spread, small / spread, spread / big
    return table.astype(np.float32)


def placing_kernel(place_ref, lo_ref, frac_ref, win_ref):
    half = IMG_BLK * BLK_SIDE * 0.5
    shape = lo_ref.shape[1:]
    place = jnp.broadcast_to(place_ref[...], shape)
    x = (place % IMG_BLK).astype(jnp.float32) * BLK_SIDE + (BLK_SIDE * 0.5 - half)
    y = (place // IMG_BLK).astype(jnp.float32) * BLK_SIDE + (BLK_SIDE * 0.5 - half)
    angle = lax.broadcasted_iota(jnp.int32, shape, 0)
    tile = lax.broadcasted_iota(jnp.int32, (TILES, shape[1]), 0)
    near = []
    for subset in range(SUBSETS):
        cosine = sine = jnp.zeros(shape, jnp.float32)
        for a, theta in enumerate(angles(subset)):
            cosine = jnp.where(angle == a, np.float32(math.cos(theta)), cosine)
            sine = jnp.where(angle == a, np.float32(math.sin(theta)), sine)
        z = x * cosine + y * sine + (RAYS * 0.5 - 0.5)
        low = jnp.floor(z)
        lo = low.astype(jnp.int32)
        lo_ref[subset] = lo
        frac_ref[subset] = (z - low) * (1.0 / spread)
        ends = (lo - PAD) // SPAN, (lo + R + PAD) // SPAN
        for a in range(ANG_SUB):
            hit = (ends[0][a:a + 1] == tile) | (ends[1][a:a + 1] == tile)
            near.append(jnp.where(hit, 1.0, 0.0))
    count = lax.dot_general(jnp.ones((8, shape[1]), jnp.bfloat16), jnp.concatenate(near, axis=0).astype(jnp.bfloat16),
                            (((1,), (1,)), ((), ())), preferred_element_type=jnp.float32)
    win_ref[...] = jnp.where(count[0:1] > 0.0, 1, 0)


def placing(place):
    shape = (SUBSETS, ANG_SUB, place.shape[0])
    return pl.pallas_call(
        placing_kernel,
        out_shape=[jax.ShapeDtypeStruct(shape, jnp.int32), jax.ShapeDtypeStruct(shape, jnp.float32),
                   jax.ShapeDtypeStruct((1, SUBSETS * ANG_SUB * TILES), jnp.int32)],
        name="placing",
    )(place.reshape(1, -1))


def shards(volume, block_place, measured, live_rays):
    groups = lax.axis_size("group")
    patches = lax.axis_size("patch")
    rows = ANG_SUB * NTILE // patches // groups
    lo, frac, win = placing(block_place)
    table = ray_table()
    tall = rows * RAYS_TILE % (2 * LANES) == 0
    estimate = volume
    own = None
    for subset in range(SUBSETS):
        base, first = geometry(subset)
        partial = forward(subset, tall, estimate, lo, frac, win, base, first)
        full, own, made = exchange(
            subset, tall, partial, live_rays, table, frac, measured, base, rows, groups, patches)
        estimate, own = backward(subset, tall, estimate, made, full, own, lo, frac, win, base, first)
    return (estimate, own[None])


def solution(mesh):
    return jax.shard_map(
        shards,
        mesh=mesh,
        in_specs=(
            P(("group", "patch"), None, None),
            P(("group", "patch")),
            P(None, "patch", None),
            P(),
        ),
        out_specs=(P(("group", "patch"), None, None), P("group", "patch", None)),
        check_vma=False,
    )
```

```python
import math

import jax
import jax.numpy as jnp
import numpy as np
from jax import lax
from jax.experimental import pallas as pl
from jax.experimental.pallas import tpu as pltpu
from jax.sharding import PartitionSpec as P

IMG_BLK = 64
BLK_SIDE = 32
RAYS_TILE = 48
NTILE = 64
ANG_SUB = 8
SUBSETS = 2

spread = 1.5
relax = 0.9

SUB = 8
NQ = (BLK_SIDE // SUB) ** 2
R = 16
VOX = BLK_SIDE * BLK_SIDE
RAYS = NTILE * RAYS_TILE
LANES = 128
PAD = 32
CHUNK = 32
MADE = 4
MADE_EARLY = (0, 5)
PARTS = 4
DEPTH = 2
EARLY = 3
SPAN = 128
TALL = RAYS + SPAN
VMEM_LIMIT = 60 * 1024 * 1024


def angles(subset):
    return [math.pi * (a * SUBSETS + subset) / (ANG_SUB * SUBSETS) for a in range(ANG_SUB)]


def geometry(subset):
    v = np.arange(VOX)
    col = (v % BLK_SIDE) + 0.5 - BLK_SIDE / 2
    row = (v // BLK_SIDE) + 0.5 - BLK_SIDE / 2
    q_of = (v // BLK_SIDE // SUB) * (BLK_SIDE // SUB) + (v % BLK_SIDE) // SUB
    base = np.zeros((ANG_SUB, VOX), np.float64)
    first = np.zeros((ANG_SUB, NQ), np.int64)
    for a, theta in enumerate(angles(subset)):
        off = col * math.cos(theta) + row * math.sin(theta)
        for q in range(NQ):
            mine = q_of == q
            first[a, q] = math.floor(off[mine].min() - spread)
            base[a, mine] = off[mine] - first[a, q]
    return base.astype(np.float32), first.astype(np.int32)


def fill_grid(base_ref, e_scr):
    ray = lax.broadcasted_iota(jnp.int32, (R, VOX), 0).astype(jnp.float32)
    for a in range(ANG_SUB):
        e_scr[a * R:(a + 1) * R, :] = (base_ref[a:a + 1, :] - ray) * (1.0 / spread)


def footprint(t):
    t = t.astype(jnp.bfloat16)
    bump = jnp.maximum(1.0 - t * t, 0.0)
    return bump * bump


TILES = RAYS // SPAN


WIDE = 16


def list_tiles(subset, win_ref, tiles, starts):
    def angle(a, n):
        starts[a] = n
        for i in range(TILES):
            hit = win_ref[0, (subset * ANG_SUB + a) * TILES + i]
            tiles[n] = a * TILES + i
            n = n + hit
        return n

    starts[ANG_SUB] = lax.fori_loop(0, ANG_SUB, angle, 0)


def over_tiles(tiles, starts, body):
    n = starts[ANG_SUB]

    def some(i, c):
        for j in range(WIDE):
            t = jnp.minimum(WIDE * i + j, n - 1)
            body(t, tiles[t])
        return c

    lax.fori_loop(0, (n + WIDE - 1) // WIDE, some, 0)


def over_angle(a, tiles, starts, body):
    def one(t, c):
        body(t, tiles[t] - a * TILES)
        return c

    lax.fori_loop(starts[a], starts[a + 1], one, 0)


def shifted(ref, base, offsets, lane_q):
    fine = [o % 8 for o in offsets]
    coarse = [o // 8 for o in offsets]
    low, high = min(coarse), max(coarse)

    def member(values, value):
        hits = [lane_q == q for q, v in enumerate(values) if v == value]
        mask = hits[0]
        for h in hits[1:]:
            mask = mask | h
        return mask

    rows = None
    for f in sorted(set(fine)):
        part = ref[pl.ds(base + 8 * low + f, SPAN + 8 * (high - low)), :]
        rows = part if rows is None else jnp.where(member(fine, f), part, rows)
    out = None
    for c in sorted(set(coarse)):
        part = rows[8 * (c - low):8 * (c - low) + SPAN]
        out = part if out is None else jnp.where(member(coarse, c), part, out)
    return out


def spread_lanes(x, lane_q):
    rows = [x]
    for half in (8, 4, 2, 1):
        low = lane_q % (2 * half) < half
        turned = [pltpu.roll(x, half * 8, 1) for x in rows]
        rows = ([jnp.where(low, x, y) for x, y in zip(rows, turned)]
                + [jnp.where(low, y, x) for x, y in zip(rows, turned)])
    return [rows[int(format(r, "04b")[::-1], 2)] for r in range(16)]


def sixteenth(base, r, tall):
    return pl.ds(base + 8 * r, 8) if tall else pl.ds(base + r, 8, stride=16)


def aligned(x, m):
    return pl.multiple_of(x, m)


def size_of(ref):
    return min(CHUNK, ref.shape[0] // PARTS)


def chunk_of(ref, c):
    return ref.at[pl.ds(c * size_of(ref), size_of(ref))]


def forward_kernel(subset, first, tall, lo_ref, frac_ref, win_ref, vol_hbm, grid_hbm, out_ref,
                   vol_ref, grid_ref, tot, acc, tiles, starts, grid_sem, vol_sem):
    size = size_of(vol_ref)
    chunks = vol_ref.shape[0] // size

    def fetch(c):
        return pltpu.make_async_copy(chunk_of(vol_hbm, c), chunk_of(vol_ref, c), vol_sem.at[c])

    grid_copy = pltpu.make_async_copy(grid_hbm, grid_ref, grid_sem)
    grid_copy.start()
    for c in range(min(DEPTH, chunks)):
        fetch(c).start()

    zero = jnp.zeros((2 * SPAN, LANES), jnp.float32)
    list_tiles(subset, win_ref, tiles, starts)

    def clear(t, at):
        acc[pl.ds(aligned(at // TILES * TALL + lax.rem(at, TILES) * SPAN, SPAN), 2 * SPAN), :] = zero

    over_tiles(tiles, starts, clear)
    out_ref[...] = jnp.zeros_like(out_ref)
    grid_copy.wait()

    width = SUB * BLK_SIDE
    group = BLK_SIDE // SUB
    slices = vol_ref.shape[1]
    col_group = (lax.broadcasted_iota(jnp.int32, (group * slices, width), 1) % BLK_SIDE) // SUB
    mine = col_group == lax.broadcasted_iota(jnp.int32, (group * slices, width), 0) // slices
    angle = lax.broadcasted_iota(jnp.int32, (1, LANES), 1) // R
    def chunk(c, carry):
        fetch(c).wait()

        @pl.when(c + DEPTH < chunks)
        def _():
            fetch(c + DEPTH).start()

        for i in range(size):
            block(c * size + i)
        return carry

    def block(b):
        frac = jnp.zeros((1, LANES), jnp.float32)
        for a in range(ANG_SUB):
            frac = jnp.where(angle == a, frac_ref[subset, a, b], frac)
        parts = []
        for g in range(group):
            at = slice(g * width, (g + 1) * width)
            f = footprint(grid_ref[at, :] + frac)
            wide = jnp.where(mine, jnp.tile(vol_ref[b, :, at], (group, 1)), 0.0)
            parts.append(jnp.dot(wide.astype(jnp.bfloat16), f, preferred_element_type=jnp.float32))
        part = jnp.transpose(jnp.concatenate(parts, axis=0))
        for a in range(ANG_SUB):
            at = pl.ds(a * TALL + PAD + lo_ref[subset, a, b], R)
            acc[at, :] += part[a * R:(a + 1) * R, :]

    lax.fori_loop(0, chunks, chunk, 0)
    lane_q = lax.broadcasted_iota(jnp.int32, (1, LANES), 1) // 8

    for a in range(ANG_SUB):
        def merge(t, i, a=a):
            base = aligned(a * TALL + PAD + i * SPAN, 32)
            tot[pl.ds(aligned(t * SPAN, SPAN), SPAN), :] = shifted(
                acc, base, [-int(o) for o in first[a]], lane_q)

        over_angle(a, tiles, starts, merge)

    def fold(t, at):
        rows = [tot[sixteenth(aligned(t * SPAN, SPAN), r, tall), :] for r in range(16)]
        for half in (1, 2, 4, 8):
            low = lane_q % (2 * half) < half
            rows = [jnp.where(low, x, y) + pltpu.roll(jnp.where(low, y, x), half * 8, 1)
                    for x, y in zip(rows[0::2], rows[1::2])]
        out_ref[pl.ds(aligned(at * 8, 8), 8), :] = rows[0]

    over_tiles(tiles, starts, fold)


def backward_kernel(subset, first, tall, lo_ref, frac_ref, win_ref, vol_hbm, made_hbm, base_ref, res_ref, own_ref,
                    out_hbm, last_ref,
                    vol_ref, out_ref, made, e_scr, res, rb, dd, tiles, starts, vol_sem, out_sem, made_sem):
    size = size_of(vol_ref)
    chunks = vol_ref.shape[0] // size

    def fetch(c):
        return pltpu.make_async_copy(chunk_of(vol_hbm, c), chunk_of(vol_ref, c), vol_sem.at[c])

    def emit(c):
        return pltpu.make_async_copy(chunk_of(out_ref, c), chunk_of(out_hbm, c), out_sem.at[c])

    def load(c):
        at = pl.ds(c * MADE, MADE)
        return pltpu.make_async_copy(made_hbm.at[at], made.at[at], made_sem.at[c])

    for c in range(min(DEPTH, chunks)):
        fetch(c).start()
    for c in range(made.shape[0] // MADE):
        load(c).start()
    fill_grid(base_ref, e_scr)
    lane_q = lax.broadcasted_iota(jnp.int32, (1, LANES), 1) // 8
    last_ref[...] = own_ref[...]
    res[...] = res_ref[...].astype(jnp.float32)
    list_tiles(subset, win_ref, tiles, starts)

    def widen(t, at):
        rows = spread_lanes(res[pl.ds(aligned(at * 8, 8), 8), :], lane_q)
        base = aligned(at // TILES * TALL + PAD + lax.rem(at, TILES) * SPAN, 32)
        for r in range(16):
            rb[sixteenth(base, r, tall), :] = rows[r]

    over_tiles(tiles, starts, widen)

    for a in range(ANG_SUB):
        def shift(t, i, a=a):
            base = aligned(a * TALL + PAD + i * SPAN, 32)
            dd[pl.ds(aligned(a * RAYS + i * SPAN, SPAN), SPAN), :] = shifted(
                rb, base, [int(o) for o in first[a]], lane_q)

        over_angle(a, tiles, starts, shift)

    width = SUB * BLK_SIDE
    group = BLK_SIDE // SUB
    lane = lax.broadcasted_iota(jnp.int32, (8, width), 1)
    col_group = (lane % BLK_SIDE) // SUB

    def block(b, ready):
        rows = jnp.concatenate(
            [dd[pl.ds(a * RAYS + lo_ref[subset, a, b], R), :] for a in range(ANG_SUB)], axis=0)
        turned = jnp.transpose(rows)
        ones = jnp.ones((8, ANG_SUB * R), jnp.float32)
        for g in range(group):
            lhs = jnp.concatenate([turned[g * 32:(g + 1) * 32], ones], axis=0).astype(jnp.bfloat16)
            at = slice(g * width, (g + 1) * width)
            if ready:
                f = made[b - (vol_ref.shape[0] - made.shape[0]), :, at]
            else:
                f = jnp.concatenate([footprint(e_scr[a * R:(a + 1) * R, at] + frac_ref[subset, a, b])
                                     for a in range(ANG_SUB)], axis=0)
            part = jnp.dot(lhs, f, preferred_element_type=jnp.float32)
            back = part[0:8]
            for j in range(1, group):
                back = jnp.where(col_group == j, part[j * 8:(j + 1) * 8], back)
            col_sum = part[32:40]
            out_ref[b, :, at] = jnp.maximum(vol_ref[b, :, at] + relax * back / col_sum, 0.0)

    def chunk(c, carry, ready):
        fetch(c).wait()

        @pl.when(c + DEPTH < chunks)
        def _():
            fetch(c + DEPTH).start()

        for i in range(size):
            block(c * size + i, ready)
        emit(c).start()
        return carry

    plain = chunks - chunks // PARTS
    lax.fori_loop(0, plain, lambda c, carry: chunk(c, carry, False), 0)
    for c in range(made.shape[0] // MADE):
        load(c).wait()
    lax.fori_loop(plain, chunks, lambda c, carry: chunk(c, carry, True), 0)
    for c in range(chunks):
        emit(c).wait()


def ray_sums(shape, big, small, inv, ray):
    side = IMG_BLK * BLK_SIDE
    half = side * 0.5
    count = side // 8
    part = lax.broadcasted_iota(jnp.int32, shape, 1) % 8
    start = (part * count).astype(jnp.float32) + (0.5 - half)
    start = ray - start * small

    def row(i, total):
        w = start - i.astype(jnp.float32) * small
        mid = jnp.clip(jnp.floor(w * inv) + 0.5, 2.5 - half, half - 2.5)
        t0 = mid * big - w
        for t in (t0 - 2 * big, t0 - big, t0, t0 + big, t0 + 2 * big):
            bump = jnp.maximum(1.0 - t * t, 0.0)
            total = total + bump * bump
        return total

    def fold(total):
        for d in (1, 2, 4):
            total = total + jnp.where(
                part // d % 2 == 0, pltpu.roll(total, LANES - d, 1), pltpu.roll(total, d, 1))
        return total

    early = count * EARLY // 8
    first = lax.fori_loop(0, early, row, jnp.zeros(shape, jnp.float32), unroll=4)
    return first, lambda total: fold(lax.fori_loop(early, count, row, total, unroll=4))


def ray_at(line, lane, tall):
    if tall:
        return line // 8 * LANES + lane // 8 * 8 + line % 8
    return line * 16 + lane // 8


def exchange_kernel(subset, tall, part_ref, live_ref, table_ref, frac_ref, meas_ref, base_ref, gathered, own_ref, made_hbm,
                    keep, half, inbox, sums, lines_scr, flat, halves, meas, stage, e_scr, made,
                    meas_sem, keep_sem, pair_send, pair_recv, send_sem, recv_sem, rs_send, rs_recv,
                    out_send, out_recv, back_send, back_recv, made_sem):
    g, p = lax.axis_index("group"), lax.axis_index("patch")
    pairs, groups = inbox.shape[0], inbox.shape[1]
    n = groups * pairs
    lines = stage.shape[0]
    rows = own_ref.shape[0]
    parity, column = lax.rem(p, 2), p // 2
    partner = (g, column * 2 + 1 - parity)
    mesh_id = pl.DeviceIdType.MESH

    def peer(d):
        return lax.rem(column + d // groups, pairs), lax.rem(g + lax.rem(d, groups), groups)

    def source(d):
        return (lax.rem(column + pairs - d // groups, pairs),
                lax.rem(g + groups - lax.rem(d, groups), groups))

    barrier = pltpu.get_barrier_semaphore()
    pl.semaphore_signal(barrier, inc=1, device_id=partner, device_id_type=mesh_id)

    def greet(d, c):
        pc, pg = peer(d)
        pl.semaphore_signal(barrier, inc=1, device_id=(pg, pc * 2 + parity), device_id_type=mesh_id)
        return c

    lax.fori_loop(1, n, greet, 0)
    read = pltpu.make_async_copy(meas_ref.at[subset, pl.ds(g * rows, rows)], meas, meas_sem)
    read.start()
    kept = pltpu.make_async_copy(part_ref.at[:, parity], keep, keep_sem)
    kept.start()
    first_row = (p * groups + g) * rows
    mine = p // pairs
    line = lax.broadcasted_iota(jnp.int32, halves.shape[1:], 0)
    lane = lax.broadcasted_iota(jnp.int32, halves.shape[1:], 1)
    ray = lax.rem(first_row, NTILE) * RAYS_TILE + mine * (lines * 8) + ray_at(line, lane, tall)
    ray = (ray.astype(jnp.float32) + (0.5 - RAYS * 0.5)) * (1.0 / spread)
    a = first_row // NTILE
    early, rest = ray_sums(
        halves.shape[1:], table_ref[subset, 0, a], table_ref[subset, 1, a], table_ref[subset, 2, a], ray)
    fill_grid(base_ref, e_scr)
    pl.semaphore_wait(barrier, n)

    def put(i):
        slot = lax.rem(i, 2)
        return pltpu.make_async_copy(made.at[slot], made_hbm.at[pl.ds(i * MADE, MADE)], made_sem.at[slot])

    def make(i, c):
        @pl.when(i >= 2)
        def _():
            put(i - 2).wait()

        for k in range(MADE):
            b = frac_ref.shape[2] - made_hbm.shape[0] + i * MADE + k
            for a in range(ANG_SUB):
                made[lax.rem(i, 2), k, a * R:(a + 1) * R, :] = footprint(
                    e_scr[a * R:(a + 1) * R, :] + frac_ref[subset, a, b])
        put(i).start()
        return c

    steps = made_hbm.shape[0] // MADE
    early_steps = min(MADE_EARLY[subset], steps)

    def swap(d):
        pc = lax.rem(column + d, pairs)
        return pltpu.make_async_remote_copy(
            src_ref=part_ref.at[pc, 1 - parity], dst_ref=half.at[pc], send_sem=pair_send.at[d],
            recv_sem=pair_recv.at[d], device_id=partner, device_id_type=mesh_id)

    def to_owner(d):
        pc, pg = peer(d)
        return pltpu.make_async_remote_copy(
            src_ref=sums.at[pc, pg], dst_ref=inbox.at[column, g], send_sem=send_sem.at[d],
            recv_sem=recv_sem.at[d], device_id=(pg, pc * 2 + parity), device_id_type=mesh_id)

    def go_swap(d, c):
        swap(d).start()
        return c

    def go_column(i, c):
        pc = lax.rem(column + i, pairs)
        swap(i).wait_recv()
        sums[pc] = (keep[pc] + half[pc]).astype(sums.dtype)

        def go(d, c):
            to_owner(d).start()
            return c

        return lax.fori_loop(jnp.maximum(i * groups, 1), (i + 1) * groups, go, c)

    lax.fori_loop(0, pairs, go_swap, 0)
    kept.wait()
    lax.fori_loop(0, pairs, go_column, 0)
    halves[mine] = rest(early)
    trade = pltpu.make_async_remote_copy(
        src_ref=halves.at[mine], dst_ref=halves.at[mine], send_sem=rs_send, recv_sem=rs_recv,
        device_id=(g, lax.rem(p + pairs, 2 * pairs)), device_id_type=mesh_id)
    trade.start()

    lax.fori_loop(0, early_steps, make, 0)

    def got(d, c):
        to_owner(d).wait_recv()
        return c

    read.wait()
    wide = lines // rows
    lane_q = lax.broadcasted_iota(jnp.int32, (1, LANES), 1) // 8

    def retile(forth):
        def one(i, c):
            at = pl.ds(aligned(i * 8, 8), 8)
            for r, x in enumerate(spread_lanes(lines_scr[at, :], lane_q)):
                flat[sixteenth(0, r, not forth), :] = x
            out = flat[sixteenth(0, 0, forth), :]
            for r in range(1, 16):
                out = jnp.where(lane_q == r, flat[sixteenth(0, r, forth), :], out)
            lines_scr[at, :] = out
            return c

        if tall:
            lax.fori_loop(0, lines // 8, one, 0)

    for c in range(wide):
        lines_scr[pl.ds(c, rows, stride=wide), :] = meas[:, c * LANES:(c + 1) * LANES]
    retile(True)

    inbox[column, g] = sums[column, g]
    lax.fori_loop(1, n, got, 0)
    total = jnp.zeros(stage.shape, jnp.float32)
    for i in range(pairs):
        for j in range(groups):
            total = total + inbox[i, j].astype(jnp.float32)
    ray = ray_at(lax.broadcasted_iota(jnp.int32, stage.shape, 0),
                 lax.broadcasted_iota(jnp.int32, stage.shape, 1), tall)
    row = ray // RAYS_TILE
    live = jnp.zeros(stage.shape, jnp.int32)
    for r in range(rows):
        live = jnp.where(row == r, live_ref[subset, first_row + r], live)
    trade.wait()
    sums_of = jnp.concatenate([halves[0], halves[1]], axis=0)
    differ = lines_scr[...] - total / jnp.maximum(sums_of, 1.0)
    residual = jnp.where(ray - row * RAYS_TILE < live, differ, 0.0)
    lines_scr[...] = residual
    stage[...] = residual.astype(jnp.bfloat16)

    def to_all(d):
        pc, pg = peer(d)
        return pltpu.make_async_remote_copy(
            src_ref=stage, dst_ref=gathered.at[column, parity, g], send_sem=out_send.at[d],
            recv_sem=out_recv.at[d], device_id=(pg, pc * 2 + parity), device_id_type=mesh_id)

    def share(d):
        pc, pg = source(d)
        return pltpu.make_async_remote_copy(
            src_ref=gathered.at[pc, parity, pg], dst_ref=gathered.at[pc, parity, pg], send_sem=back_send.at[d],
            recv_sem=back_recv.at[d], device_id=partner, device_id_type=mesh_id)

    def go_all(d, c):
        to_all(d).start()
        return c

    def pass_on(d, c):
        to_all(d).wait_recv()
        share(d).start()
        return c

    def finish(d, c):
        share(d).wait()
        return c

    def sent(d, c):
        to_owner(d).wait_send()
        to_all(d).wait_send()
        return c

    def swapped(d, c):
        swap(d).wait_send()
        return c

    lax.fori_loop(1, n, go_all, 0)
    gathered[column, parity, g] = stage[...]
    share(0).start()
    lax.fori_loop(early_steps, steps, make, 0)
    retile(False)
    for c in range(wide):
        own_ref[:, c * LANES:(c + 1) * LANES] = lines_scr[pl.ds(c, rows, stride=wide), :]
    lax.fori_loop(1, n, pass_on, 0)
    lax.fori_loop(0, n, finish, 0)
    lax.fori_loop(1, n, sent, 0)
    lax.fori_loop(0, pairs, swapped, 0)
    for i in range(max(steps - 2, 0), steps):
        put(i).wait()


def exchange(subset, tall, partial, live, table, frac, measured, base, rows, groups, patches):
    pairs = patches // 2
    lines = rows * measured.shape[2] // LANES
    shape = (pairs, 2, groups, lines, LANES)
    n = pairs * groups
    wire = jnp.bfloat16 if subset < SUBSETS - 1 else jnp.float32
    dma = pltpu.SemaphoreType.DMA
    vmem = pl.BlockSpec(memory_space=pltpu.VMEM)
    full, own, made = pl.pallas_call(
        lambda *refs: exchange_kernel(subset, tall, *refs),
        in_specs=[pl.BlockSpec(memory_space=pl.ANY), smem(), smem(), smem(), pl.BlockSpec(memory_space=pl.ANY), vmem],
        out_specs=[vmem, vmem, pl.BlockSpec(memory_space=pl.ANY)],
        out_shape=[jax.ShapeDtypeStruct(shape, jnp.bfloat16),
                   jax.ShapeDtypeStruct((rows, measured.shape[2]), jnp.float32),
                   jax.ShapeDtypeStruct((frac.shape[2] // PARTS, LANES, VOX), jnp.bfloat16)],
        scratch_shapes=[pltpu.VMEM((pairs, groups, lines, LANES), jnp.float32),
                        pltpu.VMEM((pairs, groups, lines, LANES), jnp.float32),
                        pltpu.VMEM((pairs, groups, lines, LANES), wire),
                        pltpu.VMEM((pairs, groups, lines, LANES), wire),
                        pltpu.VMEM((lines, LANES), jnp.float32),
                        pltpu.VMEM((SPAN, LANES), jnp.float32),
                        pltpu.VMEM((2, lines // 2, LANES), jnp.float32),
                        pltpu.VMEM((rows, measured.shape[2]), jnp.float32),
                        pltpu.VMEM((lines, LANES), jnp.bfloat16),
                        pltpu.VMEM((LANES, VOX), jnp.float32),
                        pltpu.VMEM((2, MADE, LANES, VOX), jnp.bfloat16),
                        dma, dma, dma((pairs,)), dma((pairs,)), dma((n,)), dma((n,)), dma, dma,
                        dma((n,)), dma((n,)), dma((n,)), dma((n,)), dma((2,))],
        compiler_params=pltpu.CompilerParams(collective_id=subset, has_side_effects=True),
        name="exchange",
    )(partial.reshape(shape), live, table, frac, measured, base)
    return full.reshape(partial.shape), own, made


def smem():
    return pl.BlockSpec(memory_space=pltpu.SMEM)


def forward(subset, tall, volume, lo, frac, win, base, first):
    blocks = volume.shape[0]
    lines = ANG_SUB * RAYS // 16
    grid = (np.repeat(base, R, axis=0) - np.tile(np.arange(R), ANG_SUB)[:, None]) * (1.0 / spread)
    vmem = pl.BlockSpec(memory_space=pltpu.VMEM)
    hbm = pl.BlockSpec(memory_space=pl.ANY)
    dma = pltpu.SemaphoreType.DMA
    return pl.pallas_call(
        lambda *refs: forward_kernel(subset, first, tall, *refs),
        in_specs=[smem(), smem(), smem(), hbm, hbm],
        out_specs=vmem,
        out_shape=jax.ShapeDtypeStruct((lines, LANES), jnp.float32),
        scratch_shapes=[pltpu.VMEM(volume.shape, jnp.float32),
                        pltpu.VMEM((VOX, LANES), jnp.float32),
                        pltpu.VMEM((ANG_SUB * RAYS, LANES), jnp.float32),
                        pltpu.VMEM((ANG_SUB * TALL, LANES), jnp.float32),
                        pltpu.SMEM((ANG_SUB * TILES + 1,), jnp.int32),
                        pltpu.SMEM((ANG_SUB + 1,), jnp.int32),
                        dma, dma((blocks // min(CHUNK, blocks // PARTS),))],
        compiler_params=pltpu.CompilerParams(vmem_limit_bytes=VMEM_LIMIT),
        name="forward",
    )(lo, frac, win, volume, grid.T.astype(np.float32))


def backward(subset, tall, volume, made, residual, own, lo, frac, win, base, first):
    blocks = volume.shape[0]
    vmem = pl.BlockSpec(memory_space=pltpu.VMEM)
    hbm = pl.BlockSpec(memory_space=pl.ANY)
    dma = pltpu.SemaphoreType.DMA
    return pl.pallas_call(
        lambda *refs: backward_kernel(subset, first, tall, *refs),
        in_specs=[smem(), smem(), smem(), hbm, hbm, vmem, vmem, vmem],
        out_specs=[hbm, vmem],
        out_shape=[jax.ShapeDtypeStruct(volume.shape, jnp.float32),
                   jax.ShapeDtypeStruct(own.shape, jnp.float32)],
        scratch_shapes=[pltpu.VMEM(volume.shape, jnp.float32),
                        pltpu.VMEM(volume.shape, jnp.float32),
                        pltpu.VMEM(made.shape, jnp.bfloat16),
                        pltpu.VMEM((ANG_SUB * R, VOX), jnp.float32),
                        pltpu.VMEM(residual.shape, jnp.float32),
                        pltpu.VMEM((ANG_SUB * TALL, LANES), jnp.float32),
                        pltpu.VMEM((ANG_SUB * RAYS, LANES), jnp.float32),
                        pltpu.SMEM((ANG_SUB * TILES + 1,), jnp.int32),
                        pltpu.SMEM((ANG_SUB + 1,), jnp.int32),
                        dma((blocks // min(CHUNK, blocks // PARTS),)), dma((blocks // min(CHUNK, blocks // PARTS),)),
                        dma((made.shape[0] // MADE,))],
        compiler_params=pltpu.CompilerParams(vmem_limit_bytes=VMEM_LIMIT),
        name="backward",
    )(lo, frac, win, volume, made, base, residual, own)


def ray_table():
    table = np.zeros((SUBSETS, 3, ANG_SUB), np.float64)
    for subset in range(SUBSETS):
        for a, t in enumerate(angles(subset)):
            small, big = sorted((abs(math.cos(t)), abs(math.sin(t))))
            table[subset, :, a] = big / spread, small / spread, spread / big
    return table.astype(np.float32)


def placing_kernel(place_ref, lo_ref, frac_ref, win_ref):
    half = IMG_BLK * BLK_SIDE * 0.5
    shape = lo_ref.shape[1:]
    place = jnp.broadcast_to(place_ref[...], shape)
    x = (place % IMG_BLK).astype(jnp.float32) * BLK_SIDE + (BLK_SIDE * 0.5 - half)
    y = (place // IMG_BLK).astype(jnp.float32) * BLK_SIDE + (BLK_SIDE * 0.5 - half)
    angle = lax.broadcasted_iota(jnp.int32, shape, 0)
    tile = lax.broadcasted_iota(jnp.int32, (TILES, shape[1]), 0)
    near = []
    for subset in range(SUBSETS):
        cosine = sine = jnp.zeros(shape, jnp.float32)
        for a, theta in enumerate(angles(subset)):
            cosine = jnp.where(angle == a, np.float32(math.cos(theta)), cosine)
            sine = jnp.where(angle == a, np.float32(math.sin(theta)), sine)
        z = x * cosine + y * sine + (RAYS * 0.5 - 0.5)
        low = jnp.floor(z)
        lo = low.astype(jnp.int32)
        lo_ref[subset] = lo
        frac_ref[subset] = (z - low) * (1.0 / spread)
        ends = (lo - PAD) // SPAN, (lo + R + PAD) // SPAN
        for a in range(ANG_SUB):
            hit = (ends[0][a:a + 1] == tile) | (ends[1][a:a + 1] == tile)
            near.append(jnp.where(hit, 1.0, 0.0))
    count = lax.dot_general(jnp.ones((8, shape[1]), jnp.bfloat16), jnp.concatenate(near, axis=0).astype(jnp.bfloat16),
                            (((1,), (1,)), ((), ())), preferred_element_type=jnp.float32)
    win_ref[...] = jnp.where(count[0:1] > 0.0, 1, 0)


def placing(place):
    shape = (SUBSETS, ANG_SUB, place.shape[0])
    return pl.pallas_call(
        placing_kernel,
        out_shape=[jax.ShapeDtypeStruct(shape, jnp.int32), jax.ShapeDtypeStruct(shape, jnp.float32),
                   jax.ShapeDtypeStruct((1, SUBSETS * ANG_SUB * TILES), jnp.int32)],
        name="placing",
    )(place.reshape(1, -1))


def shards(volume, block_place, measured, live_rays):
    groups = lax.axis_size("group")
    patches = lax.axis_size("patch")
    rows = ANG_SUB * NTILE // patches // groups
    lo, frac, win = placing(block_place)
    table = ray_table()
    tall = rows * RAYS_TILE % (2 * LANES) == 0
    estimate = volume
    own = None
    for subset in range(SUBSETS):
        base, first = geometry(subset)
        partial = forward(subset, tall, estimate, lo, frac, win, base, first)
        full, own, made = exchange(
            subset, tall, partial, live_rays, table, frac, measured, base, rows, groups, patches)
        estimate, own = backward(subset, tall, estimate, made, full, own, lo, frac, win, base, first)
    return (estimate, own[None])


def solution(mesh):
    return jax.shard_map(
        shards,
        mesh=mesh,
        in_specs=(
            P(("group", "patch"), None, None),
            P(("group", "patch")),
            P(None, "patch", None),
            P(),
        ),
        out_specs=(P(("group", "patch"), None, None), P("group", "patch", None)),
        check_vma=False,
    )
```

```python
import math

import jax
import jax.numpy as jnp
import numpy as np
from jax import lax
from jax.experimental import pallas as pl
from jax.experimental.pallas import tpu as pltpu
from jax.sharding import PartitionSpec as P

IMG_BLK = 64
BLK_SIDE = 32
RAYS_TILE = 48
NTILE = 64
ANG_SUB = 8
SUBSETS = 2

spread = 1.5
relax = 0.9

SUB = 8
NQ = (BLK_SIDE // SUB) ** 2
R = 16
VOX = BLK_SIDE * BLK_SIDE
RAYS = NTILE * RAYS_TILE
LANES = 128
PAD = 32
CHUNK = 32
MADE = 4
MADE_EARLY = (0, 5)
PARTS = 4
DEPTH = 2
EARLY = 3
SPAN = 128
TALL = RAYS + SPAN
VMEM_LIMIT = 60 * 1024 * 1024


def angles(subset):
    return [math.pi * (a * SUBSETS + subset) / (ANG_SUB * SUBSETS) for a in range(ANG_SUB)]


def geometry(subset):
    v = np.arange(VOX)
    col = (v % BLK_SIDE) + 0.5 - BLK_SIDE / 2
    row = (v // BLK_SIDE) + 0.5 - BLK_SIDE / 2
    q_of = (v // BLK_SIDE // SUB) * (BLK_SIDE // SUB) + (v % BLK_SIDE) // SUB
    base = np.zeros((ANG_SUB, VOX), np.float64)
    first = np.zeros((ANG_SUB, NQ), np.int64)
    for a, theta in enumerate(angles(subset)):
        off = col * math.cos(theta) + row * math.sin(theta)
        for q in range(NQ):
            mine = q_of == q
            first[a, q] = math.floor(off[mine].min() - spread)
            base[a, mine] = off[mine] - first[a, q]
    return base.astype(np.float32), first.astype(np.int32)


def fill_grid(base_ref, e_scr):
    ray = lax.broadcasted_iota(jnp.int32, (R, VOX), 0).astype(jnp.float32)
    for a in range(ANG_SUB):
        e_scr[a * R:(a + 1) * R, :] = (base_ref[a:a + 1, :] - ray) * (1.0 / spread)


def footprint(t):
    t = t.astype(jnp.bfloat16)
    bump = jnp.maximum(1.0 - t * t, 0.0)
    return bump * bump


TILES = RAYS // SPAN


WIDE = 16


def list_tiles(subset, win_ref, tiles, starts):
    def angle(a, n):
        starts[a] = n
        for i in range(TILES):
            hit = win_ref[0, (subset * ANG_SUB + a) * TILES + i]
            tiles[n] = a * TILES + i
            n = n + hit
        return n

    starts[ANG_SUB] = lax.fori_loop(0, ANG_SUB, angle, 0)


def over_tiles(tiles, starts, body):
    n = starts[ANG_SUB]

    def some(i, c):
        for j in range(WIDE):
            t = jnp.minimum(WIDE * i + j, n - 1)
            body(t, tiles[t])
        return c

    lax.fori_loop(0, (n + WIDE - 1) // WIDE, some, 0)


def over_angle(a, tiles, starts, body):
    def one(t, c):
        body(t, tiles[t] - a * TILES)
        return c

    lax.fori_loop(starts[a], starts[a + 1], one, 0)


def shifted(ref, base, offsets, lane_q):
    fine = [o % 8 for o in offsets]
    coarse = [o // 8 for o in offsets]
    low, high = min(coarse), max(coarse)

    def member(values, value):
        hits = [lane_q == q for q, v in enumerate(values) if v == value]
        mask = hits[0]
        for h in hits[1:]:
            mask = mask | h
        return mask

    rows = None
    for f in sorted(set(fine)):
        part = ref[pl.ds(base + 8 * low + f, SPAN + 8 * (high - low)), :]
        rows = part if rows is None else jnp.where(member(fine, f), part, rows)
    out = None
    for c in sorted(set(coarse)):
        part = rows[8 * (c - low):8 * (c - low) + SPAN]
        out = part if out is None else jnp.where(member(coarse, c), part, out)
    return out


def spread_lanes(x, lane_q):
    rows = [x]
    for half in (8, 4, 2, 1):
        low = lane_q % (2 * half) < half
        turned = [pltpu.roll(x, half * 8, 1) for x in rows]
        rows = ([jnp.where(low, x, y) for x, y in zip(rows, turned)]
                + [jnp.where(low, y, x) for x, y in zip(rows, turned)])
    return [rows[int(format(r, "04b")[::-1], 2)] for r in range(16)]


def sixteenth(base, r, tall):
    return pl.ds(base + 8 * r, 8) if tall else pl.ds(base + r, 8, stride=16)


def aligned(x, m):
    return pl.multiple_of(x, m)


def size_of(ref):
    return min(CHUNK, ref.shape[0] // PARTS)


def chunk_of(ref, c):
    return ref.at[pl.ds(c * size_of(ref), size_of(ref))]


def forward_parts(subset, first, tall, lo_ref, frac_ref, win_ref, vol_ref, grid_ref, out_ref, tot, acc, tiles, starts):
    width = SUB * BLK_SIDE
    group = BLK_SIDE // SUB
    slices = vol_ref.shape[1]
    col_group = (lax.broadcasted_iota(jnp.int32, (group * slices, width), 1) % BLK_SIDE) // SUB
    mine = col_group == lax.broadcasted_iota(jnp.int32, (group * slices, width), 0) // slices
    mine = jnp.where(mine, 1.0, 0.0).astype(jnp.bfloat16)
    angle = lax.broadcasted_iota(jnp.int32, (1, LANES), 1) // R

    def prepare():
        zero = jnp.zeros((2 * SPAN, LANES), jnp.float32)
        list_tiles(subset, win_ref, tiles, starts)

        def clear(t, at):
            acc[pl.ds(aligned(at // TILES * TALL + lax.rem(at, TILES) * SPAN, SPAN), 2 * SPAN), :] = zero

        over_tiles(tiles, starts, clear)
        out_ref[...] = jnp.zeros_like(out_ref)
    def block(b):
        frac = jnp.zeros((1, LANES), jnp.float32)
        for a in range(ANG_SUB):
            frac = jnp.where(angle == a, frac_ref[subset, a, b], frac)
        parts = []
        for g in range(group):
            at = slice(g * width, (g + 1) * width)
            f = footprint(grid_ref[at, :] + frac)
            pair = jnp.concatenate([vol_ref[b, :, at]] * 2, axis=0).astype(jnp.bfloat16)
            wide = jnp.tile(pair, (group // 2, 1)) * mine
            parts.append(jnp.dot(wide, f, preferred_element_type=jnp.float32))
        part = jnp.transpose(jnp.concatenate(parts, axis=0))
        for a in range(ANG_SUB):
            at = pl.ds(a * TALL + PAD + lo_ref[subset, a, b], R)
            acc[at, :] += part[a * R:(a + 1) * R, :]

    def finish():
        lane_q = lax.broadcasted_iota(jnp.int32, (1, LANES), 1) // 8

        for a in range(ANG_SUB):
            def merge(t, i, a=a):
                base = aligned(a * TALL + PAD + i * SPAN, 32)
                tot[pl.ds(aligned(t * SPAN, SPAN), SPAN), :] = shifted(
                    acc, base, [-int(o) for o in first[a]], lane_q)

            over_angle(a, tiles, starts, merge)

        def fold(t, at):
            rows = [tot[sixteenth(aligned(t * SPAN, SPAN), r, tall), :] for r in range(16)]
            for half in (1, 2, 4, 8):
                low = lane_q % (2 * half) < half
                rows = [jnp.where(low, x, y) + pltpu.roll(jnp.where(low, y, x), half * 8, 1)
                        for x, y in zip(rows[0::2], rows[1::2])]
            out_ref[pl.ds(aligned(at * 8, 8), 8), :] = rows[0]

        over_tiles(tiles, starts, fold)

    return prepare, block, finish


def backward_parts(subset, first, tall, lo_ref, frac_ref, win_ref, vol_ref, base_ref, res_ref, out_ref,
                   made, e_scr, res, rb, dd, tiles, starts):
    width = SUB * BLK_SIDE
    group = BLK_SIDE // SUB
    lane = lax.broadcasted_iota(jnp.int32, (8, width), 1)
    col_group = (lane % BLK_SIDE) // SUB


    def prepare():
        fill_grid(base_ref, e_scr)
        lane_q = lax.broadcasted_iota(jnp.int32, (1, LANES), 1) // 8
        res[...] = res_ref[...].astype(jnp.float32)
        list_tiles(subset, win_ref, tiles, starts)

        def widen(t, at):
            rows = spread_lanes(res[pl.ds(aligned(at * 8, 8), 8), :], lane_q)
            base = aligned(at // TILES * TALL + PAD + lax.rem(at, TILES) * SPAN, 32)
            for r in range(16):
                rb[sixteenth(base, r, tall), :] = rows[r]

        over_tiles(tiles, starts, widen)

        for a in range(ANG_SUB):
            def shift(t, i, a=a):
                base = aligned(a * TALL + PAD + i * SPAN, 32)
                dd[pl.ds(aligned(a * RAYS + i * SPAN, SPAN), SPAN), :] = shifted(
                    rb, base, [int(o) for o in first[a]], lane_q)

            over_angle(a, tiles, starts, shift)

    def block(b, ready):
        rows = jnp.concatenate(
            [dd[pl.ds(a * RAYS + lo_ref[subset, a, b], R), :] for a in range(ANG_SUB)], axis=0)
        turned = jnp.transpose(rows)
        ones = jnp.ones((8, ANG_SUB * R), jnp.float32)
        for g in range(group):
            lhs = jnp.concatenate([turned[g * 32:(g + 1) * 32], ones], axis=0).astype(jnp.bfloat16)
            at = slice(g * width, (g + 1) * width)
            if ready:
                f = made[b - (vol_ref.shape[0] - made.shape[0]), :, at]
            else:
                f = jnp.concatenate([footprint(e_scr[a * R:(a + 1) * R, at] + frac_ref[subset, a, b])
                                     for a in range(ANG_SUB)], axis=0)
            part = jnp.dot(lhs, f, preferred_element_type=jnp.float32)
            back = part[0:8]
            for j in range(1, group):
                back = jnp.where(col_group == j, part[j * 8:(j + 1) * 8], back)
            col_sum = part[32:40]
            out_ref[b, :, at] = jnp.maximum(vol_ref[b, :, at] + relax * back / col_sum, 0.0)

    return prepare, block


def sweep_kernel(back, fore, tall, names, *refs):
    ref = dict(zip(names, refs))
    vol = ref["vol"]
    size = size_of(vol)
    chunks = vol.shape[0] // size
    tables = ref["lo"], ref["frac"], ref["win"]

    def fetch(c):
        return pltpu.make_async_copy(chunk_of(ref["vol_hbm"], c), chunk_of(vol, c), ref["vol_sem"].at[c])

    def emit(c):
        return pltpu.make_async_copy(chunk_of(ref["out"], c), chunk_of(ref["out_hbm"], c), ref["out_sem"].at[c])

    def load(c):
        at = pl.ds(c * MADE, MADE)
        return pltpu.make_async_copy(ref["made_hbm"].at[at], ref["made"].at[at], ref["made_sem"].at[c])

    loads = 0 if back is None else ref["made"].shape[0] // MADE
    if fore is not None:
        grid_copy = pltpu.make_async_copy(ref["grid_hbm"], ref["grid"], ref["grid_sem"])
        grid_copy.start()
    for c in range(min(DEPTH, chunks)):
        fetch(c).start()
    for c in range(loads):
        load(c).start()
    if back is not None:
        prepare, update = backward_parts(
            back, geometry(back)[1], tall, *tables, vol, ref["base"], ref["residual"], ref["out"], ref["made"],
            ref["edges"], ref["res"], ref["tall"], ref["flat"], ref["tiles"], ref["starts"])
        prepare()
    if fore is not None:
        prepare, project, finish = forward_parts(
            fore, geometry(fore)[1], tall, *tables, vol if back is None else ref["out"], ref["grid"], ref["part"],
            ref["flat"], ref["tall"], ref["tiles"], ref["starts"])
        prepare()
        grid_copy.wait()
    else:
        ref["last"][...] = ref["own"][...]

    def chunk(c, carry, ready):
        fetch(c).wait()

        @pl.when(c + DEPTH < chunks)
        def _():
            fetch(c + DEPTH).start()

        if back is not None:
            for i in range(size):
                update(c * size + i, ready)
            emit(c).start()
        if fore is not None:
            for i in range(size):
                project(c * size + i)
        return carry

    plain = chunks if back is None else chunks - chunks // PARTS
    lax.fori_loop(0, plain, lambda c, carry: chunk(c, carry, False), 0)
    for c in range(loads):
        load(c).wait()
    if plain < chunks:
        lax.fori_loop(plain, chunks, lambda c, carry: chunk(c, carry, True), 0)
    if fore is not None:
        finish()
    if back is not None:
        for c in range(chunks):
            emit(c).wait()


def ray_sums(shape, big, small, inv, ray):
    side = IMG_BLK * BLK_SIDE
    half = side * 0.5
    count = side // 8
    part = lax.broadcasted_iota(jnp.int32, shape, 1) % 8
    start = (part * count).astype(jnp.float32) + (0.5 - half)
    start = ray - start * small

    def row(i, total):
        w = start - i.astype(jnp.float32) * small
        mid = jnp.clip(jnp.floor(w * inv) + 0.5, 2.5 - half, half - 2.5)
        t0 = mid * big - w
        for t in (t0 - 2 * big, t0 - big, t0, t0 + big, t0 + 2 * big):
            bump = jnp.maximum(1.0 - t * t, 0.0)
            total = total + bump * bump
        return total

    def fold(total):
        for d in (1, 2, 4):
            total = total + jnp.where(
                part // d % 2 == 0, pltpu.roll(total, LANES - d, 1), pltpu.roll(total, d, 1))
        return total

    early = count * EARLY // 8
    first = lax.fori_loop(0, early, row, jnp.zeros(shape, jnp.float32), unroll=4)
    return first, lambda total: fold(lax.fori_loop(early, count, row, total, unroll=4))


def ray_at(line, lane, tall):
    if tall:
        return line // 8 * LANES + lane // 8 * 8 + line % 8
    return line * 16 + lane // 8


def exchange_kernel(subset, tall, part_ref, live_ref, table_ref, frac_ref, meas_ref, base_ref, gathered, own_ref, made_hbm,
                    keep, half, inbox, sums, lines_scr, flat, halves, meas, stage, e_scr, made,
                    meas_sem, keep_sem, pair_send, pair_recv, send_sem, recv_sem, rs_send, rs_recv,
                    out_send, out_recv, back_send, back_recv, made_sem):
    g, p = lax.axis_index("group"), lax.axis_index("patch")
    pairs, groups = inbox.shape[0], inbox.shape[1]
    n = groups * pairs
    lines = stage.shape[0]
    rows = own_ref.shape[0]
    parity, column = lax.rem(p, 2), p // 2
    partner = (g, column * 2 + 1 - parity)
    mesh_id = pl.DeviceIdType.MESH

    def peer(d):
        return lax.rem(column + d // groups, pairs), lax.rem(g + lax.rem(d, groups), groups)

    def source(d):
        return (lax.rem(column + pairs - d // groups, pairs),
                lax.rem(g + groups - lax.rem(d, groups), groups))

    barrier = pltpu.get_barrier_semaphore()
    pl.semaphore_signal(barrier, inc=1, device_id=partner, device_id_type=mesh_id)

    def greet(d, c):
        pc, pg = peer(d)
        pl.semaphore_signal(barrier, inc=1, device_id=(pg, pc * 2 + parity), device_id_type=mesh_id)
        return c

    lax.fori_loop(1, n, greet, 0)
    read = pltpu.make_async_copy(meas_ref.at[subset, pl.ds(g * rows, rows)], meas, meas_sem)
    read.start()
    kept = pltpu.make_async_copy(part_ref.at[:, parity], keep, keep_sem)
    kept.start()
    first_row = (p * groups + g) * rows
    mine = p // pairs
    line = lax.broadcasted_iota(jnp.int32, halves.shape[1:], 0)
    lane = lax.broadcasted_iota(jnp.int32, halves.shape[1:], 1)
    ray = lax.rem(first_row, NTILE) * RAYS_TILE + mine * (lines * 8) + ray_at(line, lane, tall)
    ray = (ray.astype(jnp.float32) + (0.5 - RAYS * 0.5)) * (1.0 / spread)
    a = first_row // NTILE
    early, rest = ray_sums(
        halves.shape[1:], table_ref[subset, 0, a], table_ref[subset, 1, a], table_ref[subset, 2, a], ray)
    fill_grid(base_ref, e_scr)
    pl.semaphore_wait(barrier, n)

    def put(i):
        slot = lax.rem(i, 2)
        return pltpu.make_async_copy(made.at[slot], made_hbm.at[pl.ds(i * MADE, MADE)], made_sem.at[slot])

    def make(i, c):
        @pl.when(i >= 2)
        def _():
            put(i - 2).wait()

        for k in range(MADE):
            b = frac_ref.shape[2] - made_hbm.shape[0] + i * MADE + k
            for a in range(ANG_SUB):
                made[lax.rem(i, 2), k, a * R:(a + 1) * R, :] = footprint(
                    e_scr[a * R:(a + 1) * R, :] + frac_ref[subset, a, b])
        put(i).start()
        return c

    steps = made_hbm.shape[0] // MADE
    early_steps = min(MADE_EARLY[subset], steps)

    def swap(d):
        pc = lax.rem(column + d, pairs)
        return pltpu.make_async_remote_copy(
            src_ref=part_ref.at[pc, 1 - parity], dst_ref=half.at[pc], send_sem=pair_send.at[d],
            recv_sem=pair_recv.at[d], device_id=partner, device_id_type=mesh_id)

    def to_owner(d):
        pc, pg = peer(d)
        return pltpu.make_async_remote_copy(
            src_ref=sums.at[pc, pg], dst_ref=inbox.at[column, g], send_sem=send_sem.at[d],
            recv_sem=recv_sem.at[d], device_id=(pg, pc * 2 + parity), device_id_type=mesh_id)

    def go_swap(d, c):
        swap(d).start()
        return c

    def go_column(i, c):
        pc = lax.rem(column + i, pairs)
        swap(i).wait_recv()
        sums[pc] = (keep[pc] + half[pc]).astype(sums.dtype)

        def go(d, c):
            to_owner(d).start()
            return c

        return lax.fori_loop(jnp.maximum(i * groups, 1), (i + 1) * groups, go, c)

    lax.fori_loop(0, pairs, go_swap, 0)
    kept.wait()
    lax.fori_loop(0, pairs, go_column, 0)
    halves[mine] = rest(early)
    trade = pltpu.make_async_remote_copy(
        src_ref=halves.at[mine], dst_ref=halves.at[mine], send_sem=rs_send, recv_sem=rs_recv,
        device_id=(g, lax.rem(p + pairs, 2 * pairs)), device_id_type=mesh_id)
    trade.start()

    lax.fori_loop(0, early_steps, make, 0)

    def got(d, c):
        to_owner(d).wait_recv()
        return c

    read.wait()
    wide = lines // rows
    lane_q = lax.broadcasted_iota(jnp.int32, (1, LANES), 1) // 8

    def retile(forth):
        def one(i, c):
            at = pl.ds(aligned(i * 8, 8), 8)
            for r, x in enumerate(spread_lanes(lines_scr[at, :], lane_q)):
                flat[sixteenth(0, r, not forth), :] = x
            out = flat[sixteenth(0, 0, forth), :]
            for r in range(1, 16):
                out = jnp.where(lane_q == r, flat[sixteenth(0, r, forth), :], out)
            lines_scr[at, :] = out
            return c

        if tall:
            lax.fori_loop(0, lines // 8, one, 0)

    for c in range(wide):
        lines_scr[pl.ds(c, rows, stride=wide), :] = meas[:, c * LANES:(c + 1) * LANES]
    retile(True)

    inbox[column, g] = sums[column, g]
    lax.fori_loop(1, n, got, 0)
    total = jnp.zeros(stage.shape, jnp.float32)
    for i in range(pairs):
        for j in range(groups):
            total = total + inbox[i, j].astype(jnp.float32)
    ray = ray_at(lax.broadcasted_iota(jnp.int32, stage.shape, 0),
                 lax.broadcasted_iota(jnp.int32, stage.shape, 1), tall)
    row = ray // RAYS_TILE
    live = jnp.zeros(stage.shape, jnp.int32)
    for r in range(rows):
        live = jnp.where(row == r, live_ref[subset, first_row + r], live)
    trade.wait()
    sums_of = jnp.concatenate([halves[0], halves[1]], axis=0)
    differ = lines_scr[...] - total / jnp.maximum(sums_of, 1.0)
    residual = jnp.where(ray - row * RAYS_TILE < live, differ, 0.0)
    lines_scr[...] = residual
    stage[...] = residual.astype(jnp.bfloat16)

    def to_all(d):
        pc, pg = peer(d)
        return pltpu.make_async_remote_copy(
            src_ref=stage, dst_ref=gathered.at[column, parity, g], send_sem=out_send.at[d],
            recv_sem=out_recv.at[d], device_id=(pg, pc * 2 + parity), device_id_type=mesh_id)

    def share(d):
        pc, pg = source(d)
        return pltpu.make_async_remote_copy(
            src_ref=gathered.at[pc, parity, pg], dst_ref=gathered.at[pc, parity, pg], send_sem=back_send.at[d],
            recv_sem=back_recv.at[d], device_id=partner, device_id_type=mesh_id)

    def go_all(d, c):
        to_all(d).start()
        return c

    def pass_on(d, c):
        to_all(d).wait_recv()
        share(d).start()
        return c

    def finish(d, c):
        share(d).wait()
        return c

    def sent(d, c):
        to_owner(d).wait_send()
        to_all(d).wait_send()
        return c

    def swapped(d, c):
        swap(d).wait_send()
        return c

    lax.fori_loop(1, n, go_all, 0)
    gathered[column, parity, g] = stage[...]
    share(0).start()
    lax.fori_loop(early_steps, steps, make, 0)
    retile(False)
    for c in range(wide):
        own_ref[:, c * LANES:(c + 1) * LANES] = lines_scr[pl.ds(c, rows, stride=wide), :]
    lax.fori_loop(1, n, pass_on, 0)
    lax.fori_loop(0, n, finish, 0)
    lax.fori_loop(1, n, sent, 0)
    lax.fori_loop(0, pairs, swapped, 0)
    for i in range(max(steps - 2, 0), steps):
        put(i).wait()


def exchange(subset, tall, partial, live, table, frac, measured, base, rows, groups, patches):
    pairs = patches // 2
    lines = rows * measured.shape[2] // LANES
    shape = (pairs, 2, groups, lines, LANES)
    n = pairs * groups
    wire = jnp.bfloat16 if subset < SUBSETS - 1 else jnp.float32
    dma = pltpu.SemaphoreType.DMA
    vmem = pl.BlockSpec(memory_space=pltpu.VMEM)
    full, own, made = pl.pallas_call(
        lambda *refs: exchange_kernel(subset, tall, *refs),
        in_specs=[pl.BlockSpec(memory_space=pl.ANY), smem(), smem(), smem(), pl.BlockSpec(memory_space=pl.ANY), vmem],
        out_specs=[vmem, vmem, pl.BlockSpec(memory_space=pl.ANY)],
        out_shape=[jax.ShapeDtypeStruct(shape, jnp.bfloat16),
                   jax.ShapeDtypeStruct((rows, measured.shape[2]), jnp.float32),
                   jax.ShapeDtypeStruct((frac.shape[2] // PARTS, LANES, VOX), jnp.bfloat16)],
        scratch_shapes=[pltpu.VMEM((pairs, groups, lines, LANES), jnp.float32),
                        pltpu.VMEM((pairs, groups, lines, LANES), jnp.float32),
                        pltpu.VMEM((pairs, groups, lines, LANES), wire),
                        pltpu.VMEM((pairs, groups, lines, LANES), wire),
                        pltpu.VMEM((lines, LANES), jnp.float32),
                        pltpu.VMEM((SPAN, LANES), jnp.float32),
                        pltpu.VMEM((2, lines // 2, LANES), jnp.float32),
                        pltpu.VMEM((rows, measured.shape[2]), jnp.float32),
                        pltpu.VMEM((lines, LANES), jnp.bfloat16),
                        pltpu.VMEM((LANES, VOX), jnp.float32),
                        pltpu.VMEM((2, MADE, LANES, VOX), jnp.bfloat16),
                        dma, dma, dma((pairs,)), dma((pairs,)), dma((n,)), dma((n,)), dma, dma,
                        dma((n,)), dma((n,)), dma((n,)), dma((n,)), dma((2,))],
        compiler_params=pltpu.CompilerParams(collective_id=subset, has_side_effects=True),
        name="exchange",
    )(partial.reshape(shape), live, table, frac, measured, base)
    return full.reshape(partial.shape), own, made


def smem():
    return pl.BlockSpec(memory_space=pltpu.SMEM)


def sweep(back, fore, tall, volume, lo, frac, win, made=None, residual=None, own=None):
    blocks = volume.shape[0]
    chunks = blocks // min(CHUNK, blocks // PARTS)
    lines = ANG_SUB * RAYS // 16
    vmem = pl.BlockSpec(memory_space=pltpu.VMEM)
    hbm = pl.BlockSpec(memory_space=pl.ANY)
    dma = pltpu.SemaphoreType.DMA
    f32 = jnp.float32
    given = [("lo", smem(), lo), ("frac", smem(), frac), ("win", smem(), win), ("vol_hbm", hbm, volume)]
    made_here = []
    scratch = [("vol", pltpu.VMEM(volume.shape, f32)),
               ("tall", pltpu.VMEM((ANG_SUB * TALL, LANES), f32)),
               ("flat", pltpu.VMEM((ANG_SUB * RAYS, LANES), f32)),
               ("tiles", pltpu.SMEM((ANG_SUB * TILES + 1,), jnp.int32)),
               ("starts", pltpu.SMEM((ANG_SUB + 1,), jnp.int32)),
               ("vol_sem", dma((chunks,)))]
    if fore is not None:
        base = geometry(fore)[0]
        grid = (np.repeat(base, R, axis=0) - np.tile(np.arange(R), ANG_SUB)[:, None]) * (1.0 / spread)
        given.append(("grid_hbm", hbm, grid.T.astype(np.float32)))
        made_here.append(("part", vmem, jax.ShapeDtypeStruct((lines, LANES), f32)))
        scratch += [("grid", pltpu.VMEM((VOX, LANES), f32)), ("grid_sem", dma)]
    if back is not None:
        given += [("made_hbm", hbm, made), ("base", vmem, geometry(back)[0]), ("residual", vmem, residual)]
        made_here.append(("out_hbm", hbm, jax.ShapeDtypeStruct(volume.shape, f32)))
        scratch += [("out", pltpu.VMEM(volume.shape, f32)),
                    ("made", pltpu.VMEM(made.shape, jnp.bfloat16)),
                    ("edges", pltpu.VMEM((ANG_SUB * R, VOX), f32)),
                    ("res", pltpu.VMEM(residual.shape, f32)),
                    ("out_sem", dma((chunks,))), ("made_sem", dma((made.shape[0] // MADE,)))]
    if fore is None:
        given.append(("own", vmem, own))
        made_here.append(("last", vmem, jax.ShapeDtypeStruct(own.shape, f32)))
    names = [x[0] for x in given + made_here + scratch]
    return pl.pallas_call(
        lambda *refs: sweep_kernel(back, fore, tall, names, *refs),
        in_specs=[x[1] for x in given],
        out_specs=[x[1] for x in made_here],
        out_shape=[x[2] for x in made_here],
        scratch_shapes=[x[1] for x in scratch],
        compiler_params=pltpu.CompilerParams(vmem_limit_bytes=VMEM_LIMIT),
        name="sweep",
    )(*[x[2] for x in given])


def ray_table():
    table = np.zeros((SUBSETS, 3, ANG_SUB), np.float64)
    for subset in range(SUBSETS):
        for a, t in enumerate(angles(subset)):
            small, big = sorted((abs(math.cos(t)), abs(math.sin(t))))
            table[subset, :, a] = big / spread, small / spread, spread / big
    return table.astype(np.float32)


def placing_kernel(place_ref, lo_ref, frac_ref, win_ref):
    half = IMG_BLK * BLK_SIDE * 0.5
    shape = lo_ref.shape[1:]
    place = jnp.broadcast_to(place_ref[...], shape)
    x = (place % IMG_BLK).astype(jnp.float32) * BLK_SIDE + (BLK_SIDE * 0.5 - half)
    y = (place // IMG_BLK).astype(jnp.float32) * BLK_SIDE + (BLK_SIDE * 0.5 - half)
    angle = lax.broadcasted_iota(jnp.int32, shape, 0)
    tile = lax.broadcasted_iota(jnp.int32, (TILES, shape[1]), 0)
    near = []
    for subset in range(SUBSETS):
        cosine = sine = jnp.zeros(shape, jnp.float32)
        for a, theta in enumerate(angles(subset)):
            cosine = jnp.where(angle == a, np.float32(math.cos(theta)), cosine)
            sine = jnp.where(angle == a, np.float32(math.sin(theta)), sine)
        z = x * cosine + y * sine + (RAYS * 0.5 - 0.5)
        low = jnp.floor(z)
        lo = low.astype(jnp.int32)
        lo_ref[subset] = lo
        frac_ref[subset] = (z - low) * (1.0 / spread)
        ends = (lo - PAD) // SPAN, (lo + R + PAD) // SPAN
        for a in range(ANG_SUB):
            hit = (ends[0][a:a + 1] == tile) | (ends[1][a:a + 1] == tile)
            near.append(jnp.where(hit, 1.0, 0.0))
    count = lax.dot_general(jnp.ones((8, shape[1]), jnp.bfloat16), jnp.concatenate(near, axis=0).astype(jnp.bfloat16),
                            (((1,), (1,)), ((), ())), preferred_element_type=jnp.float32)
    win_ref[...] = jnp.where(count[0:1] > 0.0, 1, 0)


def placing(place):
    shape = (SUBSETS, ANG_SUB, place.shape[0])
    return pl.pallas_call(
        placing_kernel,
        out_shape=[jax.ShapeDtypeStruct(shape, jnp.int32), jax.ShapeDtypeStruct(shape, jnp.float32),
                   jax.ShapeDtypeStruct((1, SUBSETS * ANG_SUB * TILES), jnp.int32)],
        name="placing",
    )(place.reshape(1, -1))


def shards(volume, block_place, measured, live_rays):
    groups = lax.axis_size("group")
    patches = lax.axis_size("patch")
    rows = ANG_SUB * NTILE // patches // groups
    lo, frac, win = placing(block_place)
    table = ray_table()
    tall = rows * RAYS_TILE % (2 * LANES) == 0
    estimate = volume
    (partial,) = sweep(None, 0, tall, estimate, lo, frac, win)
    for subset in range(SUBSETS):
        full, own, made = exchange(
            subset, tall, partial, live_rays, table, frac, measured, geometry(subset)[0], rows, groups, patches)
        if subset < SUBSETS - 1:
            partial, estimate = sweep(subset, subset + 1, tall, estimate, lo, frac, win, made, full)
        else:
            estimate, own = sweep(subset, None, tall, estimate, lo, frac, win, made, full, own)
    return (estimate, own[None])


def solution(mesh):
    return jax.shard_map(
        shards,
        mesh=mesh,
        in_specs=(
            P(("group", "patch"), None, None),
            P(("group", "patch")),
            P(None, "patch", None),
            P(),
        ),
        out_specs=(P(("group", "patch"), None, None), P("group", "patch", None)),
        check_vma=False,
    )
```

```python
import math

import jax
import jax.numpy as jnp
import numpy as np
from jax import lax
from jax.experimental import pallas as pl
from jax.experimental.pallas import tpu as pltpu
from jax.sharding import PartitionSpec as P

IMG_BLK = 64
BLK_SIDE = 32
RAYS_TILE = 48
NTILE = 64
ANG_SUB = 8
SUBSETS = 2

spread = 1.5
relax = 0.9

SUB = 8
NQ = (BLK_SIDE // SUB) ** 2
R = 16
VOX = BLK_SIDE * BLK_SIDE
RAYS = NTILE * RAYS_TILE
LANES = 128
PAD = 32
CHUNK = 32
MADE = 4
MADE_EARLY = (0, 5)
PARTS = 4
DEPTH = 2
EARLY = 3
SPAN = 128
TALL = RAYS + SPAN
VMEM_LIMIT = 60 * 1024 * 1024


def angles(subset):
    return [math.pi * (a * SUBSETS + subset) / (ANG_SUB * SUBSETS) for a in range(ANG_SUB)]


def geometry(subset):
    v = np.arange(VOX)
    col = (v % BLK_SIDE) + 0.5 - BLK_SIDE / 2
    row = (v // BLK_SIDE) + 0.5 - BLK_SIDE / 2
    q_of = (v // BLK_SIDE // SUB) * (BLK_SIDE // SUB) + (v % BLK_SIDE) // SUB
    base = np.zeros((ANG_SUB, VOX), np.float64)
    first = np.zeros((ANG_SUB, NQ), np.int64)
    for a, theta in enumerate(angles(subset)):
        off = col * math.cos(theta) + row * math.sin(theta)
        for q in range(NQ):
            mine = q_of == q
            first[a, q] = math.floor(off[mine].min() - spread)
            base[a, mine] = off[mine] - first[a, q]
    return base.astype(np.float32), first.astype(np.int32)


def fill_grid(base_ref, e_scr):
    ray = lax.broadcasted_iota(jnp.int32, (R, VOX), 0).astype(jnp.float32)
    for a in range(ANG_SUB):
        e_scr[a * R:(a + 1) * R, :] = (base_ref[a:a + 1, :] - ray) * (1.0 / spread)


def footprint(t):
    t = t.astype(jnp.bfloat16)
    bump = jnp.maximum(1.0 - t * t, 0.0)
    return bump * bump


TILES = RAYS // SPAN


WIDE = 16


def list_tiles(subset, win_ref, tiles, starts):
    def angle(a, n):
        starts[a] = n
        for i in range(TILES):
            hit = win_ref[0, (subset * ANG_SUB + a) * TILES + i]
            tiles[n] = a * TILES + i
            n = n + hit
        return n

    starts[ANG_SUB] = lax.fori_loop(0, ANG_SUB, angle, 0)


def over_tiles(tiles, starts, body):
    n = starts[ANG_SUB]

    def some(i, c):
        for j in range(WIDE):
            t = jnp.minimum(WIDE * i + j, n - 1)
            body(t, tiles[t])
        return c

    lax.fori_loop(0, (n + WIDE - 1) // WIDE, some, 0)


def over_angle(a, tiles, starts, body):
    def one(t, c):
        body(t, tiles[t] - a * TILES)
        return c

    lax.fori_loop(starts[a], starts[a + 1], one, 0)


def shifted(ref, base, offsets, lane_q):
    fine = [o % 8 for o in offsets]
    coarse = [o // 8 for o in offsets]
    low, high = min(coarse), max(coarse)

    def member(values, value):
        hits = [lane_q == q for q, v in enumerate(values) if v == value]
        mask = hits[0]
        for h in hits[1:]:
            mask = mask | h
        return mask

    rows = None
    for f in sorted(set(fine)):
        part = ref[pl.ds(base + 8 * low + f, SPAN + 8 * (high - low)), :]
        rows = part if rows is None else jnp.where(member(fine, f), part, rows)
    out = None
    for c in sorted(set(coarse)):
        part = rows[8 * (c - low):8 * (c - low) + SPAN]
        out = part if out is None else jnp.where(member(coarse, c), part, out)
    return out


def spread_lanes(x, lane_q):
    rows = [x]
    for half in (8, 4, 2, 1):
        low = lane_q % (2 * half) < half
        turned = [pltpu.roll(x, half * 8, 1) for x in rows]
        rows = ([jnp.where(low, x, y) for x, y in zip(rows, turned)]
                + [jnp.where(low, y, x) for x, y in zip(rows, turned)])
    return [rows[int(format(r, "04b")[::-1], 2)] for r in range(16)]


def sixteenth(base, r, tall):
    return pl.ds(base + 8 * r, 8) if tall else pl.ds(base + r, 8, stride=16)


def aligned(x, m):
    return pl.multiple_of(x, m)


def size_of(ref):
    return min(CHUNK, ref.shape[0] // PARTS)


def chunk_of(ref, c):
    return ref.at[pl.ds(c * size_of(ref), size_of(ref))]


def forward_parts(subset, first, tall, lo_ref, frac_ref, win_ref, vol_ref, grid_ref, out_ref, tot, acc, tiles, starts):
    width = SUB * BLK_SIDE
    group = BLK_SIDE // SUB
    slices = vol_ref.shape[1]
    col_group = (lax.broadcasted_iota(jnp.int32, (group * slices, width), 1) % BLK_SIDE) // SUB
    mine = col_group == lax.broadcasted_iota(jnp.int32, (group * slices, width), 0) // slices
    angle = lax.broadcasted_iota(jnp.int32, (1, LANES), 1) // R

    def prepare():
        zero = jnp.zeros((2 * SPAN, LANES), jnp.float32)
        list_tiles(subset, win_ref, tiles, starts)

        def clear(t, at):
            acc[pl.ds(aligned(at // TILES * TALL + lax.rem(at, TILES) * SPAN, SPAN), 2 * SPAN), :] = zero

        over_tiles(tiles, starts, clear)
        out_ref[...] = jnp.zeros_like(out_ref)
    def block(b):
        frac = jnp.zeros((1, LANES), jnp.float32)
        for a in range(ANG_SUB):
            frac = jnp.where(angle == a, frac_ref[subset, a, b], frac)
        parts = []
        for g in range(group):
            at = slice(g * width, (g + 1) * width)
            f = footprint(grid_ref[at, :] + frac)
            wide = jnp.where(mine, jnp.tile(vol_ref[b, :, at], (group, 1)), 0.0)
            parts.append(jnp.dot(wide.astype(jnp.bfloat16), f, preferred_element_type=jnp.float32))
        part = jnp.transpose(jnp.concatenate(parts, axis=0))
        for a in range(ANG_SUB):
            at = pl.ds(a * TALL + PAD + lo_ref[subset, a, b], R)
            acc[at, :] += part[a * R:(a + 1) * R, :]

    def finish():
        lane_q = lax.broadcasted_iota(jnp.int32, (1, LANES), 1) // 8

        for a in range(ANG_SUB):
            def merge(t, i, a=a):
                base = aligned(a * TALL + PAD + i * SPAN, 32)
                tot[pl.ds(aligned(t * SPAN, SPAN), SPAN), :] = shifted(
                    acc, base, [-int(o) for o in first[a]], lane_q)

            over_angle(a, tiles, starts, merge)

        def fold(t, at):
            rows = [tot[sixteenth(aligned(t * SPAN, SPAN), r, tall), :] for r in range(16)]
            for half in (1, 2, 4, 8):
                low = lane_q % (2 * half) < half
                rows = [jnp.where(low, x, y) + pltpu.roll(jnp.where(low, y, x), half * 8, 1)
                        for x, y in zip(rows[0::2], rows[1::2])]
            out_ref[pl.ds(aligned(at * 8, 8), 8), :] = rows[0]

        over_tiles(tiles, starts, fold)

    return prepare, block, finish


def backward_parts(subset, first, tall, lo_ref, frac_ref, win_ref, vol_ref, base_ref, res_ref, out_ref,
                   made, e_scr, res, rb, dd, tiles, starts):
    width = SUB * BLK_SIDE
    group = BLK_SIDE // SUB
    lane = lax.broadcasted_iota(jnp.int32, (8, width), 1)
    col_group = (lane % BLK_SIDE) // SUB


    def prepare():
        fill_grid(base_ref, e_scr)
        lane_q = lax.broadcasted_iota(jnp.int32, (1, LANES), 1) // 8
        res[...] = res_ref[...].astype(jnp.float32)
        list_tiles(subset, win_ref, tiles, starts)

        def widen(t, at):
            rows = spread_lanes(res[pl.ds(aligned(at * 8, 8), 8), :], lane_q)
            base = aligned(at // TILES * TALL + PAD + lax.rem(at, TILES) * SPAN, 32)
            for r in range(16):
                rb[sixteenth(base, r, tall), :] = rows[r]

        over_tiles(tiles, starts, widen)

        for a in range(ANG_SUB):
            def shift(t, i, a=a):
                base = aligned(a * TALL + PAD + i * SPAN, 32)
                dd[pl.ds(aligned(a * RAYS + i * SPAN, SPAN), SPAN), :] = shifted(
                    rb, base, [int(o) for o in first[a]], lane_q)

            over_angle(a, tiles, starts, shift)

    def block(b, ready):
        rows = jnp.concatenate(
            [dd[pl.ds(a * RAYS + lo_ref[subset, a, b], R), :] for a in range(ANG_SUB)], axis=0)
        turned = jnp.transpose(rows)
        ones = jnp.ones((8, ANG_SUB * R), jnp.float32)
        for g in range(group):
            lhs = jnp.concatenate([turned[g * 32:(g + 1) * 32], ones], axis=0).astype(jnp.bfloat16)
            at = slice(g * width, (g + 1) * width)
            if ready:
                f = made[b - (vol_ref.shape[0] - made.shape[0]), :, at]
            else:
                f = jnp.concatenate([footprint(e_scr[a * R:(a + 1) * R, at] + frac_ref[subset, a, b])
                                     for a in range(ANG_SUB)], axis=0)
            part = jnp.dot(lhs, f, preferred_element_type=jnp.float32)
            back = part[0:8]
            for j in range(1, group):
                back = jnp.where(col_group == j, part[j * 8:(j + 1) * 8], back)
            col_sum = part[32:40]
            out_ref[b, :, at] = jnp.maximum(vol_ref[b, :, at] + relax * back / col_sum, 0.0)

    return prepare, block


def sweep_kernel(back, fore, tall, names, *refs):
    ref = dict(zip(names, refs))
    vol = ref["vol"]
    size = size_of(vol)
    chunks = vol.shape[0] // size
    tables = ref["lo"], ref["frac"], ref["win"]

    def fetch(c):
        return pltpu.make_async_copy(chunk_of(ref["vol_hbm"], c), chunk_of(vol, c), ref["vol_sem"].at[c])

    def emit(c):
        return pltpu.make_async_copy(chunk_of(ref["out"], c), chunk_of(ref["out_hbm"], c), ref["out_sem"].at[c])

    def load(c):
        at = pl.ds(c * MADE, MADE)
        return pltpu.make_async_copy(ref["made_hbm"].at[at], ref["made"].at[at], ref["made_sem"].at[c])

    loads = 0 if back is None else ref["made"].shape[0] // MADE
    if fore is not None:
        grid_copy = pltpu.make_async_copy(ref["grid_hbm"], ref["grid"], ref["grid_sem"])
        grid_copy.start()
    for c in range(min(DEPTH, chunks)):
        fetch(c).start()
    for c in range(loads):
        load(c).start()
    if back is not None:
        prepare, update = backward_parts(
            back, geometry(back)[1], tall, *tables, vol, ref["base"], ref["residual"], ref["out"], ref["made"],
            ref["edges"], ref["res"], ref["tall"], ref["flat"], ref["tiles"], ref["starts"])
        prepare()
    if fore is not None:
        prepare, project, finish = forward_parts(
            fore, geometry(fore)[1], tall, *tables, vol if back is None else ref["out"], ref["grid"], ref["part"],
            ref["flat"], ref["tall"], ref["tiles"], ref["starts"])
        prepare()
        grid_copy.wait()
    else:
        ref["last"][...] = ref["own"][...]

    def chunk(c, carry, ready):
        fetch(c).wait()

        @pl.when(c + DEPTH < chunks)
        def _():
            fetch(c + DEPTH).start()

        if back is not None:
            for i in range(size):
                update(c * size + i, ready)
            emit(c).start()
        if fore is not None:
            for i in range(size):
                project(c * size + i)
        return carry

    plain = chunks if back is None else chunks - chunks // PARTS
    lax.fori_loop(0, plain, lambda c, carry: chunk(c, carry, False), 0)
    for c in range(loads):
        load(c).wait()
    if plain < chunks:
        lax.fori_loop(plain, chunks, lambda c, carry: chunk(c, carry, True), 0)
    if fore is not None:
        finish()
    if back is not None:
        for c in range(chunks):
            emit(c).wait()


def ray_sums(shape, big, small, inv, ray):
    side = IMG_BLK * BLK_SIDE
    half = side * 0.5
    count = side // 8
    part = lax.broadcasted_iota(jnp.int32, shape, 1) % 8
    start = (part * count).astype(jnp.float32) + (0.5 - half)
    start = ray - start * small

    def row(i, total):
        w = start - i.astype(jnp.float32) * small
        mid = jnp.clip(jnp.floor(w * inv) + 0.5, 2.5 - half, half - 2.5)
        t0 = mid * big - w
        for t in (t0 - 2 * big, t0 - big, t0, t0 + big, t0 + 2 * big):
            bump = jnp.maximum(1.0 - t * t, 0.0)
            total = total + bump * bump
        return total

    def fold(total):
        for d in (1, 2, 4):
            total = total + jnp.where(
                part // d % 2 == 0, pltpu.roll(total, LANES - d, 1), pltpu.roll(total, d, 1))
        return total

    early = count * EARLY // 8
    first = lax.fori_loop(0, early, row, jnp.zeros(shape, jnp.float32), unroll=4)
    return first, lambda total: fold(lax.fori_loop(early, count, row, total, unroll=4))


def ray_at(line, lane, tall):
    if tall:
        return line // 8 * LANES + lane // 8 * 8 + line % 8
    return line * 16 + lane // 8


def exchange_kernel(subset, tall, part_ref, live_ref, table_ref, frac_ref, meas_ref, base_ref, gathered, own_ref, made_hbm,
                    keep, half, inbox, sums, lines_scr, flat, halves, meas, stage, e_scr, made,
                    meas_sem, keep_sem, pair_send, pair_recv, send_sem, recv_sem, rs_send, rs_recv,
                    out_send, out_recv, back_send, back_recv, made_sem):
    g, p = lax.axis_index("group"), lax.axis_index("patch")
    pairs, groups = inbox.shape[0], inbox.shape[1]
    n = groups * pairs
    lines = stage.shape[0]
    rows = own_ref.shape[0]
    parity, column = lax.rem(p, 2), p // 2
    partner = (g, column * 2 + 1 - parity)
    mesh_id = pl.DeviceIdType.MESH

    def peer(d):
        return lax.rem(column + d // groups, pairs), lax.rem(g + lax.rem(d, groups), groups)

    def source(d):
        return (lax.rem(column + pairs - d // groups, pairs),
                lax.rem(g + groups - lax.rem(d, groups), groups))

    barrier = pltpu.get_barrier_semaphore()
    pl.semaphore_signal(barrier, inc=1, device_id=partner, device_id_type=mesh_id)

    def greet(d, c):
        pc, pg = peer(d)
        pl.semaphore_signal(barrier, inc=1, device_id=(pg, pc * 2 + parity), device_id_type=mesh_id)
        return c

    lax.fori_loop(1, n, greet, 0)
    read = pltpu.make_async_copy(meas_ref.at[subset, pl.ds(g * rows, rows)], meas, meas_sem)
    read.start()
    kept = pltpu.make_async_copy(part_ref.at[:, parity], keep, keep_sem)
    kept.start()
    first_row = (p * groups + g) * rows
    mine = p // pairs
    line = lax.broadcasted_iota(jnp.int32, halves.shape[1:], 0)
    lane = lax.broadcasted_iota(jnp.int32, halves.shape[1:], 1)
    ray = lax.rem(first_row, NTILE) * RAYS_TILE + mine * (lines * 8) + ray_at(line, lane, tall)
    ray = (ray.astype(jnp.float32) + (0.5 - RAYS * 0.5)) * (1.0 / spread)
    a = first_row // NTILE
    early, rest = ray_sums(
        halves.shape[1:], table_ref[subset, 0, a], table_ref[subset, 1, a], table_ref[subset, 2, a], ray)
    fill_grid(base_ref, e_scr)
    pl.semaphore_wait(barrier, n)

    def put(i):
        slot = lax.rem(i, 2)
        return pltpu.make_async_copy(made.at[slot], made_hbm.at[pl.ds(i * MADE, MADE)], made_sem.at[slot])

    def make(i, c):
        @pl.when(i >= 2)
        def _():
            put(i - 2).wait()

        for k in range(MADE):
            b = frac_ref.shape[2] - made_hbm.shape[0] + i * MADE + k
            for a in range(ANG_SUB):
                made[lax.rem(i, 2), k, a * R:(a + 1) * R, :] = footprint(
                    e_scr[a * R:(a + 1) * R, :] + frac_ref[subset, a, b])
        put(i).start()
        return c

    steps = made_hbm.shape[0] // MADE
    early_steps = min(MADE_EARLY[subset], steps)

    def swap(d):
        pc = lax.rem(column + d, pairs)
        return pltpu.make_async_remote_copy(
            src_ref=part_ref.at[pc, 1 - parity], dst_ref=half.at[pc], send_sem=pair_send.at[d],
            recv_sem=pair_recv.at[d], device_id=partner, device_id_type=mesh_id)

    def to_owner(d):
        pc, pg = peer(d)
        return pltpu.make_async_remote_copy(
            src_ref=sums.at[pc, pg], dst_ref=inbox.at[column, g], send_sem=send_sem.at[d],
            recv_sem=recv_sem.at[d], device_id=(pg, pc * 2 + parity), device_id_type=mesh_id)

    def go_swap(d, c):
        swap(d).start()
        return c

    def go_column(i, c):
        pc = lax.rem(column + i, pairs)
        swap(i).wait_recv()
        sums[pc] = (keep[pc] + half[pc]).astype(sums.dtype)

        def go(d, c):
            to_owner(d).start()
            return c

        return lax.fori_loop(jnp.maximum(i * groups, 1), (i + 1) * groups, go, c)

    lax.fori_loop(0, pairs, go_swap, 0)
    kept.wait()
    lax.fori_loop(0, pairs, go_column, 0)
    halves[mine] = rest(early)
    trade = pltpu.make_async_remote_copy(
        src_ref=halves.at[mine], dst_ref=halves.at[mine], send_sem=rs_send, recv_sem=rs_recv,
        device_id=(g, lax.rem(p + pairs, 2 * pairs)), device_id_type=mesh_id)
    trade.start()

    lax.fori_loop(0, early_steps, make, 0)

    def got(d, c):
        to_owner(d).wait_recv()
        return c

    read.wait()
    wide = lines // rows
    lane_q = lax.broadcasted_iota(jnp.int32, (1, LANES), 1) // 8

    def retile(forth):
        def one(i, c):
            at = pl.ds(aligned(i * 8, 8), 8)
            for r, x in enumerate(spread_lanes(lines_scr[at, :], lane_q)):
                flat[sixteenth(0, r, not forth), :] = x
            out = flat[sixteenth(0, 0, forth), :]
            for r in range(1, 16):
                out = jnp.where(lane_q == r, flat[sixteenth(0, r, forth), :], out)
            lines_scr[at, :] = out
            return c

        if tall:
            lax.fori_loop(0, lines // 8, one, 0)

    for c in range(wide):
        lines_scr[pl.ds(c, rows, stride=wide), :] = meas[:, c * LANES:(c + 1) * LANES]
    retile(True)

    inbox[column, g] = sums[column, g]
    lax.fori_loop(1, n, got, 0)
    total = jnp.zeros(stage.shape, jnp.float32)
    for i in range(pairs):
        for j in range(groups):
            total = total + inbox[i, j].astype(jnp.float32)
    ray = ray_at(lax.broadcasted_iota(jnp.int32, stage.shape, 0),
                 lax.broadcasted_iota(jnp.int32, stage.shape, 1), tall)
    row = ray // RAYS_TILE
    live = jnp.zeros(stage.shape, jnp.int32)
    for r in range(rows):
        live = jnp.where(row == r, live_ref[subset, first_row + r], live)
    trade.wait()
    sums_of = jnp.concatenate([halves[0], halves[1]], axis=0)
    differ = lines_scr[...] - total / jnp.maximum(sums_of, 1.0)
    residual = jnp.where(ray - row * RAYS_TILE < live, differ, 0.0)
    lines_scr[...] = residual
    stage[...] = residual.astype(jnp.bfloat16)

    def to_all(d):
        pc, pg = peer(d)
        return pltpu.make_async_remote_copy(
            src_ref=stage, dst_ref=gathered.at[column, parity, g], send_sem=out_send.at[d],
            recv_sem=out_recv.at[d], device_id=(pg, pc * 2 + parity), device_id_type=mesh_id)

    def share(d):
        pc, pg = source(d)
        return pltpu.make_async_remote_copy(
            src_ref=gathered.at[pc, parity, pg], dst_ref=gathered.at[pc, parity, pg], send_sem=back_send.at[d],
            recv_sem=back_recv.at[d], device_id=partner, device_id_type=mesh_id)

    def go_all(d, c):
        to_all(d).start()
        return c

    def pass_on(d, c):
        to_all(d).wait_recv()
        share(d).start()
        return c

    def finish(d, c):
        share(d).wait()
        return c

    def sent(d, c):
        to_owner(d).wait_send()
        to_all(d).wait_send()
        return c

    def swapped(d, c):
        swap(d).wait_send()
        return c

    lax.fori_loop(1, n, go_all, 0)
    gathered[column, parity, g] = stage[...]
    share(0).start()
    lax.fori_loop(early_steps, steps, make, 0)
    retile(False)
    for c in range(wide):
        own_ref[:, c * LANES:(c + 1) * LANES] = lines_scr[pl.ds(c, rows, stride=wide), :]
    lax.fori_loop(1, n, pass_on, 0)
    lax.fori_loop(0, n, finish, 0)
    lax.fori_loop(1, n, sent, 0)
    lax.fori_loop(0, pairs, swapped, 0)
    for i in range(max(steps - 2, 0), steps):
        put(i).wait()


def exchange(subset, tall, partial, live, table, frac, measured, base, rows, groups, patches):
    pairs = patches // 2
    lines = rows * measured.shape[2] // LANES
    shape = (pairs, 2, groups, lines, LANES)
    n = pairs * groups
    wire = jnp.bfloat16 if subset < SUBSETS - 1 else jnp.float32
    dma = pltpu.SemaphoreType.DMA
    vmem = pl.BlockSpec(memory_space=pltpu.VMEM)
    full, own, made = pl.pallas_call(
        lambda *refs: exchange_kernel(subset, tall, *refs),
        in_specs=[pl.BlockSpec(memory_space=pl.ANY), smem(), smem(), smem(), pl.BlockSpec(memory_space=pl.ANY), vmem],
        out_specs=[vmem, vmem, pl.BlockSpec(memory_space=pl.ANY)],
        out_shape=[jax.ShapeDtypeStruct(shape, jnp.bfloat16),
                   jax.ShapeDtypeStruct((rows, measured.shape[2]), jnp.float32),
                   jax.ShapeDtypeStruct((frac.shape[2] // PARTS, LANES, VOX), jnp.bfloat16)],
        scratch_shapes=[pltpu.VMEM((pairs, groups, lines, LANES), jnp.float32),
                        pltpu.VMEM((pairs, groups, lines, LANES), jnp.float32),
                        pltpu.VMEM((pairs, groups, lines, LANES), wire),
                        pltpu.VMEM((pairs, groups, lines, LANES), wire),
                        pltpu.VMEM((lines, LANES), jnp.float32),
                        pltpu.VMEM((SPAN, LANES), jnp.float32),
                        pltpu.VMEM((2, lines // 2, LANES), jnp.float32),
                        pltpu.VMEM((rows, measured.shape[2]), jnp.float32),
                        pltpu.VMEM((lines, LANES), jnp.bfloat16),
                        pltpu.VMEM((LANES, VOX), jnp.float32),
                        pltpu.VMEM((2, MADE, LANES, VOX), jnp.bfloat16),
                        dma, dma, dma((pairs,)), dma((pairs,)), dma((n,)), dma((n,)), dma, dma,
                        dma((n,)), dma((n,)), dma((n,)), dma((n,)), dma((2,))],
        compiler_params=pltpu.CompilerParams(collective_id=subset, has_side_effects=True),
        name="exchange",
    )(partial.reshape(shape), live, table, frac, measured, base)
    return full.reshape(partial.shape), own, made


def smem():
    return pl.BlockSpec(memory_space=pltpu.SMEM)


def sweep(back, fore, tall, volume, lo, frac, win, made=None, residual=None, own=None):
    blocks = volume.shape[0]
    chunks = blocks // min(CHUNK, blocks // PARTS)
    lines = ANG_SUB * RAYS // 16
    vmem = pl.BlockSpec(memory_space=pltpu.VMEM)
    hbm = pl.BlockSpec(memory_space=pl.ANY)
    dma = pltpu.SemaphoreType.DMA
    f32 = jnp.float32
    given = [("lo", smem(), lo), ("frac", smem(), frac), ("win", smem(), win), ("vol_hbm", hbm, volume)]
    made_here = []
    scratch = [("vol", pltpu.VMEM(volume.shape, f32)),
               ("tall", pltpu.VMEM((ANG_SUB * TALL, LANES), f32)),
               ("flat", pltpu.VMEM((ANG_SUB * RAYS, LANES), f32)),
               ("tiles", pltpu.SMEM((ANG_SUB * TILES + 1,), jnp.int32)),
               ("starts", pltpu.SMEM((ANG_SUB + 1,), jnp.int32)),
               ("vol_sem", dma((chunks,)))]
    if fore is not None:
        base = geometry(fore)[0]
        grid = (np.repeat(base, R, axis=0) - np.tile(np.arange(R), ANG_SUB)[:, None]) * (1.0 / spread)
        given.append(("grid_hbm", hbm, grid.T.astype(np.float32)))
        made_here.append(("part", vmem, jax.ShapeDtypeStruct((lines, LANES), f32)))
        scratch += [("grid", pltpu.VMEM((VOX, LANES), f32)), ("grid_sem", dma)]
    if back is not None:
        given += [("made_hbm", hbm, made), ("base", vmem, geometry(back)[0]), ("residual", vmem, residual)]
        made_here.append(("out_hbm", hbm, jax.ShapeDtypeStruct(volume.shape, f32)))
        scratch += [("out", pltpu.VMEM(volume.shape, f32)),
                    ("made", pltpu.VMEM(made.shape, jnp.bfloat16)),
                    ("edges", pltpu.VMEM((ANG_SUB * R, VOX), f32)),
                    ("res", pltpu.VMEM(residual.shape, f32)),
                    ("out_sem", dma((chunks,))), ("made_sem", dma((made.shape[0] // MADE,)))]
    if fore is None:
        given.append(("own", vmem, own))
        made_here.append(("last", vmem, jax.ShapeDtypeStruct(own.shape, f32)))
    names = [x[0] for x in given + made_here + scratch]
    return pl.pallas_call(
        lambda *refs: sweep_kernel(back, fore, tall, names, *refs),
        in_specs=[x[1] for x in given],
        out_specs=[x[1] for x in made_here],
        out_shape=[x[2] for x in made_here],
        scratch_shapes=[x[1] for x in scratch],
        compiler_params=pltpu.CompilerParams(vmem_limit_bytes=VMEM_LIMIT),
        name="sweep",
    )(*[x[2] for x in given])


def ray_table():
    table = np.zeros((SUBSETS, 3, ANG_SUB), np.float64)
    for subset in range(SUBSETS):
        for a, t in enumerate(angles(subset)):
            small, big = sorted((abs(math.cos(t)), abs(math.sin(t))))
            table[subset, :, a] = big / spread, small / spread, spread / big
    return table.astype(np.float32)


def placing_kernel(place_ref, lo_ref, frac_ref, win_ref):
    half = IMG_BLK * BLK_SIDE * 0.5
    shape = lo_ref.shape[1:]
    place = jnp.broadcast_to(place_ref[...], shape)
    x = (place % IMG_BLK).astype(jnp.float32) * BLK_SIDE + (BLK_SIDE * 0.5 - half)
    y = (place // IMG_BLK).astype(jnp.float32) * BLK_SIDE + (BLK_SIDE * 0.5 - half)
    angle = lax.broadcasted_iota(jnp.int32, shape, 0)
    tile = lax.broadcasted_iota(jnp.int32, (TILES, shape[1]), 0)
    near = []
    for subset in range(SUBSETS):
        cosine = sine = jnp.zeros(shape, jnp.float32)
        for a, theta in enumerate(angles(subset)):
            cosine = jnp.where(angle == a, np.float32(math.cos(theta)), cosine)
            sine = jnp.where(angle == a, np.float32(math.sin(theta)), sine)
        z = x * cosine + y * sine + (RAYS * 0.5 - 0.5)
        low = jnp.floor(z)
        lo = low.astype(jnp.int32)
        lo_ref[subset] = lo
        frac_ref[subset] = (z - low) * (1.0 / spread)
        ends = (lo - PAD) // SPAN, (lo + R + PAD) // SPAN
        for a in range(ANG_SUB):
            hit = (ends[0][a:a + 1] == tile) | (ends[1][a:a + 1] == tile)
            near.append(jnp.where(hit, 1.0, 0.0))
    count = lax.dot_general(jnp.ones((8, shape[1]), jnp.bfloat16), jnp.concatenate(near, axis=0).astype(jnp.bfloat16),
                            (((1,), (1,)), ((), ())), preferred_element_type=jnp.float32)
    win_ref[...] = jnp.where(count[0:1] > 0.0, 1, 0)


def placing(place):
    shape = (SUBSETS, ANG_SUB, place.shape[0])
    return pl.pallas_call(
        placing_kernel,
        out_shape=[jax.ShapeDtypeStruct(shape, jnp.int32), jax.ShapeDtypeStruct(shape, jnp.float32),
                   jax.ShapeDtypeStruct((1, SUBSETS * ANG_SUB * TILES), jnp.int32)],
        name="placing",
    )(place.reshape(1, -1))


def shards(volume, block_place, measured, live_rays):
    groups = lax.axis_size("group")
    patches = lax.axis_size("patch")
    rows = ANG_SUB * NTILE // patches // groups
    lo, frac, win = placing(block_place)
    table = ray_table()
    tall = rows * RAYS_TILE % (2 * LANES) == 0
    estimate = volume
    (partial,) = sweep(None, 0, tall, estimate, lo, frac, win)
    for subset in range(SUBSETS):
        full, own, made = exchange(
            subset, tall, partial, live_rays, table, frac, measured, geometry(subset)[0], rows, groups, patches)
        if subset < SUBSETS - 1:
            partial, estimate = sweep(subset, subset + 1, tall, estimate, lo, frac, win, made, full)
        else:
            estimate, own = sweep(subset, None, tall, estimate, lo, frac, win, made, full, own)
    return (estimate, own[None])


def solution(mesh):
    return jax.shard_map(
        shards,
        mesh=mesh,
        in_specs=(
            P(("group", "patch"), None, None),
            P(("group", "patch")),
            P(None, "patch", None),
            P(),
        ),
        out_specs=(P(("group", "patch"), None, None), P("group", "patch", None)),
        check_vma=False,
    )
```

```python
import math

import jax
import jax.numpy as jnp
import numpy as np
from jax import lax
from jax.experimental import pallas as pl
from jax.experimental.pallas import tpu as pltpu
from jax.sharding import PartitionSpec as P

IMG_BLK = 64
BLK_SIDE = 32
RAYS_TILE = 48
NTILE = 64
ANG_SUB = 8
SUBSETS = 2

spread = 1.5
relax = 0.9

SUB = 8
NQ = (BLK_SIDE // SUB) ** 2
R = 16
VOX = BLK_SIDE * BLK_SIDE
RAYS = NTILE * RAYS_TILE
LANES = 128
PAD = 32
CHUNK = 32
MADE = 4
MADE_EARLY = (2, 2)
PARTS = 4
DEPTH = 2
EARLY = 3
SPAN = 128
TALL = RAYS + SPAN
VMEM_LIMIT = 60 * 1024 * 1024


def angles(subset):
    return [math.pi * (a * SUBSETS + subset) / (ANG_SUB * SUBSETS) for a in range(ANG_SUB)]


def geometry(subset):
    v = np.arange(VOX)
    col = (v % BLK_SIDE) + 0.5 - BLK_SIDE / 2
    row = (v // BLK_SIDE) + 0.5 - BLK_SIDE / 2
    q_of = (v // BLK_SIDE // SUB) * (BLK_SIDE // SUB) + (v % BLK_SIDE) // SUB
    base = np.zeros((ANG_SUB, VOX), np.float64)
    first = np.zeros((ANG_SUB, NQ), np.int64)
    for a, theta in enumerate(angles(subset)):
        off = col * math.cos(theta) + row * math.sin(theta)
        for q in range(NQ):
            mine = q_of == q
            first[a, q] = math.floor(off[mine].min() - spread)
            base[a, mine] = off[mine] - first[a, q]
    return base.astype(np.float32), first.astype(np.int32)


def fill_grid(base_ref, e_scr):
    ray = lax.broadcasted_iota(jnp.int32, (R, VOX), 0).astype(jnp.float32)
    for a in range(ANG_SUB):
        e_scr[a * R:(a + 1) * R, :] = (base_ref[a:a + 1, :] - ray) * (1.0 / spread)


def footprint(t):
    t = t.astype(jnp.bfloat16)
    bump = jnp.maximum(1.0 - t * t, 0.0)
    return bump * bump


TILES = RAYS // SPAN


WIDE = 16


def list_tiles(subset, win_ref, tiles, starts):
    def angle(a, n):
        starts[a] = n
        for i in range(TILES):
            hit = win_ref[0, (subset * ANG_SUB + a) * TILES + i]
            tiles[n] = a * TILES + i
            n = n + hit
        return n

    starts[ANG_SUB] = lax.fori_loop(0, ANG_SUB, angle, 0)


def over_tiles(tiles, starts, body):
    n = starts[ANG_SUB]

    def some(i, c):
        for j in range(WIDE):
            t = jnp.minimum(WIDE * i + j, n - 1)
            body(t, tiles[t])
        return c

    lax.fori_loop(0, (n + WIDE - 1) // WIDE, some, 0)


def over_angle(a, tiles, starts, body):
    def one(t, c):
        body(t, tiles[t] - a * TILES)
        return c

    lax.fori_loop(starts[a], starts[a + 1], one, 0)


def shifted(ref, base, offsets, lane_q):
    fine = [o % 8 for o in offsets]
    coarse = [o // 8 for o in offsets]
    low, high = min(coarse), max(coarse)

    def member(values, value):
        hits = [lane_q == q for q, v in enumerate(values) if v == value]
        mask = hits[0]
        for h in hits[1:]:
            mask = mask | h
        return mask

    rows = None
    for f in sorted(set(fine)):
        part = ref[pl.ds(base + 8 * low + f, SPAN + 8 * (high - low)), :]
        rows = part if rows is None else jnp.where(member(fine, f), part, rows)
    out = None
    for c in sorted(set(coarse)):
        part = rows[8 * (c - low):8 * (c - low) + SPAN]
        out = part if out is None else jnp.where(member(coarse, c), part, out)
    return out


def spread_lanes(x, lane_q):
    rows = [x]
    for half in (8, 4, 2, 1):
        low = lane_q % (2 * half) < half
        turned = [pltpu.roll(x, half * 8, 1) for x in rows]
        rows = ([jnp.where(low, x, y) for x, y in zip(rows, turned)]
                + [jnp.where(low, y, x) for x, y in zip(rows, turned)])
    return [rows[int(format(r, "04b")[::-1], 2)] for r in range(16)]


def sixteenth(base, r, tall):
    return pl.ds(base + 8 * r, 8) if tall else pl.ds(base + r, 8, stride=16)


def aligned(x, m):
    return pl.multiple_of(x, m)


def size_of(ref):
    return min(CHUNK, ref.shape[0] // PARTS)


def chunk_of(ref, c):
    return ref.at[pl.ds(c * size_of(ref), size_of(ref))]


def forward_parts(subset, first, tall, lo_ref, frac_ref, win_ref, vol_ref, grid_ref, out_ref, tot, acc, tiles, starts):
    width = SUB * BLK_SIDE
    group = BLK_SIDE // SUB
    slices = vol_ref.shape[1]
    col_group = (lax.broadcasted_iota(jnp.int32, (group * slices, width), 1) % BLK_SIDE) // SUB
    mine = col_group == lax.broadcasted_iota(jnp.int32, (group * slices, width), 0) // slices
    angle = lax.broadcasted_iota(jnp.int32, (1, LANES), 1) // R

    def prepare():
        zero = jnp.zeros((2 * SPAN, LANES), jnp.float32)
        list_tiles(subset, win_ref, tiles, starts)

        def clear(t, at):
            acc[pl.ds(aligned(at // TILES * TALL + lax.rem(at, TILES) * SPAN, SPAN), 2 * SPAN), :] = zero

        over_tiles(tiles, starts, clear)
        out_ref[...] = jnp.zeros_like(out_ref)
    def block(b):
        frac = jnp.zeros((1, LANES), jnp.float32)
        for a in range(ANG_SUB):
            frac = jnp.where(angle == a, frac_ref[subset, a, b], frac)
        parts = []
        for g in range(group):
            at = slice(g * width, (g + 1) * width)
            f = footprint(grid_ref[at, :] + frac)
            wide = jnp.where(mine, jnp.tile(vol_ref[b, :, at], (group, 1)), 0.0)
            parts.append(jnp.dot(wide.astype(jnp.bfloat16), f, preferred_element_type=jnp.float32))
        part = jnp.transpose(jnp.concatenate(parts, axis=0))
        for a in range(ANG_SUB):
            at = pl.ds(a * TALL + PAD + lo_ref[subset, a, b], R)
            acc[at, :] += part[a * R:(a + 1) * R, :]

    def finish():
        lane_q = lax.broadcasted_iota(jnp.int32, (1, LANES), 1) // 8

        for a in range(ANG_SUB):
            def merge(t, i, a=a):
                base = aligned(a * TALL + PAD + i * SPAN, 32)
                tot[pl.ds(aligned(t * SPAN, SPAN), SPAN), :] = shifted(
                    acc, base, [-int(o) for o in first[a]], lane_q)

            over_angle(a, tiles, starts, merge)

        def fold(t, at):
            rows = [tot[sixteenth(aligned(t * SPAN, SPAN), r, tall), :] for r in range(16)]
            for half in (1, 2, 4, 8):
                low = lane_q % (2 * half) < half
                rows = [jnp.where(low, x, y) + pltpu.roll(jnp.where(low, y, x), half * 8, 1)
                        for x, y in zip(rows[0::2], rows[1::2])]
            out_ref[pl.ds(aligned(at * 8, 8), 8), :] = rows[0]

        over_tiles(tiles, starts, fold)

    return prepare, block, finish


def backward_parts(subset, first, tall, lo_ref, frac_ref, win_ref, vol_ref, base_ref, res_ref, out_ref,
                   made, e_scr, res, rb, dd, tiles, starts):
    width = SUB * BLK_SIDE
    group = BLK_SIDE // SUB
    lane = lax.broadcasted_iota(jnp.int32, (8, width), 1)
    col_group = (lane % BLK_SIDE) // SUB


    def prepare():
        fill_grid(base_ref, e_scr)
        lane_q = lax.broadcasted_iota(jnp.int32, (1, LANES), 1) // 8
        res[...] = res_ref[...].astype(jnp.float32)
        list_tiles(subset, win_ref, tiles, starts)

        def widen(t, at):
            rows = spread_lanes(res[pl.ds(aligned(at * 8, 8), 8), :], lane_q)
            base = aligned(at // TILES * TALL + PAD + lax.rem(at, TILES) * SPAN, 32)
            for r in range(16):
                rb[sixteenth(base, r, tall), :] = rows[r]

        over_tiles(tiles, starts, widen)

        for a in range(ANG_SUB):
            def shift(t, i, a=a):
                base = aligned(a * TALL + PAD + i * SPAN, 32)
                dd[pl.ds(aligned(a * RAYS + i * SPAN, SPAN), SPAN), :] = shifted(
                    rb, base, [int(o) for o in first[a]], lane_q)

            over_angle(a, tiles, starts, shift)

    def block(b, ready):
        rows = jnp.concatenate(
            [dd[pl.ds(a * RAYS + lo_ref[subset, a, b], R), :] for a in range(ANG_SUB)], axis=0)
        turned = jnp.transpose(rows)
        ones = jnp.ones((8, ANG_SUB * R), jnp.float32)
        for g in range(group):
            lhs = jnp.concatenate([turned[g * 32:(g + 1) * 32], ones], axis=0).astype(jnp.bfloat16)
            at = slice(g * width, (g + 1) * width)
            if ready:
                f = made[b - (vol_ref.shape[0] - made.shape[0]), :, at]
            else:
                f = jnp.concatenate([footprint(e_scr[a * R:(a + 1) * R, at] + frac_ref[subset, a, b])
                                     for a in range(ANG_SUB)], axis=0)
            part = jnp.dot(lhs, f, preferred_element_type=jnp.float32)
            back = part[0:8]
            for j in range(1, group):
                back = jnp.where(col_group == j, part[j * 8:(j + 1) * 8], back)
            col_sum = part[32:40]
            out_ref[b, :, at] = jnp.maximum(vol_ref[b, :, at] + relax * back / col_sum, 0.0)

    return prepare, block


def sweep_kernel(back, fore, tall, names, *refs):
    ref = dict(zip(names, refs))
    vol = ref["vol"]
    size = size_of(vol)
    chunks = vol.shape[0] // size
    tables = ref["lo"], ref["frac"], ref["win"]

    def fetch(c):
        return pltpu.make_async_copy(chunk_of(ref["vol_hbm"], c), chunk_of(vol, c), ref["vol_sem"].at[c])

    def emit(c):
        return pltpu.make_async_copy(chunk_of(ref["out"], c), chunk_of(ref["out_hbm"], c), ref["out_sem"].at[c])

    def load(c):
        at = pl.ds(c * MADE, MADE)
        return pltpu.make_async_copy(ref["made_hbm"].at[at], ref["made"].at[at], ref["made_sem"].at[c])

    loads = 0 if back is None else ref["made"].shape[0] // MADE
    if fore is not None:
        grid_copy = pltpu.make_async_copy(ref["grid_hbm"], ref["grid"], ref["grid_sem"])
        grid_copy.start()
    for c in range(min(DEPTH, chunks)):
        fetch(c).start()
    for c in range(loads):
        load(c).start()
    if back is not None:
        prepare, update = backward_parts(
            back, geometry(back)[1], tall, *tables, vol, ref["base"], ref["residual"], ref["out"], ref["made"],
            ref["edges"], ref["res"], ref["tall"], ref["flat"], ref["tiles"], ref["starts"])
        prepare()
    if fore is not None:
        prepare, project, finish = forward_parts(
            fore, geometry(fore)[1], tall, *tables, vol if back is None else ref["out"], ref["grid"], ref["part"],
            ref["flat"], ref["tall"], ref["tiles"], ref["starts"])
        prepare()
        grid_copy.wait()
    else:
        ref["last"][...] = ref["own"][...]

    def chunk(c, carry, ready):
        fetch(c).wait()

        @pl.when(c + DEPTH < chunks)
        def _():
            fetch(c + DEPTH).start()

        if back is not None:
            for i in range(size):
                update(c * size + i, ready)
            emit(c).start()
        if fore is not None:
            for i in range(size):
                project(c * size + i)
        return carry

    plain = chunks if back is None else chunks - chunks // PARTS
    lax.fori_loop(0, plain, lambda c, carry: chunk(c, carry, False), 0)
    for c in range(loads):
        load(c).wait()
    if plain < chunks:
        lax.fori_loop(plain, chunks, lambda c, carry: chunk(c, carry, True), 0)
    if fore is not None:
        finish()
    if back is not None:
        for c in range(chunks):
            emit(c).wait()


def ray_sums(shape, big, small, inv, ray):
    side = IMG_BLK * BLK_SIDE
    half = side * 0.5
    count = side // 8
    part = lax.broadcasted_iota(jnp.int32, shape, 1) % 8
    start = (part * count).astype(jnp.float32) + (0.5 - half)
    start = ray - start * small

    def row(i, total):
        w = start - i.astype(jnp.float32) * small
        mid = jnp.clip(jnp.floor(w * inv) + 0.5, 2.5 - half, half - 2.5)
        t0 = mid * big - w
        for t in (t0 - 2 * big, t0 - big, t0, t0 + big, t0 + 2 * big):
            bump = jnp.maximum(1.0 - t * t, 0.0)
            total = total + bump * bump
        return total

    def fold(total):
        for d in (1, 2, 4):
            total = total + jnp.where(
                part // d % 2 == 0, pltpu.roll(total, LANES - d, 1), pltpu.roll(total, d, 1))
        return total

    early = count * EARLY // 8
    first = lax.fori_loop(0, early, row, jnp.zeros(shape, jnp.float32), unroll=4)
    return first, lambda total: fold(lax.fori_loop(early, count, row, total, unroll=4))


def ray_at(line, lane, tall):
    if tall:
        return line // 8 * LANES + lane // 8 * 8 + line % 8
    return line * 16 + lane // 8


def exchange_kernel(subset, tall, part_ref, live_ref, table_ref, frac_ref, meas_ref, base_ref, gathered, own_ref, made_hbm,
                    keep, half, inbox, sums, lines_scr, flat, halves, meas, stage, e_scr, made,
                    meas_sem, keep_sem, pair_send, pair_recv, send_sem, recv_sem, rs_send, rs_recv,
                    out_send, out_recv, back_send, back_recv, made_sem):
    g, p = lax.axis_index("group"), lax.axis_index("patch")
    pairs, groups = inbox.shape[0], inbox.shape[1]
    n = groups * pairs
    lines = stage.shape[0]
    rows = own_ref.shape[0]
    parity, column = lax.rem(p, 2), p // 2
    partner = (g, column * 2 + 1 - parity)
    mesh_id = pl.DeviceIdType.MESH

    def peer(d):
        return lax.rem(column + d // groups, pairs), lax.rem(g + lax.rem(d, groups), groups)

    def source(d):
        return (lax.rem(column + pairs - d // groups, pairs),
                lax.rem(g + groups - lax.rem(d, groups), groups))

    barrier = pltpu.get_barrier_semaphore()
    pl.semaphore_signal(barrier, inc=1, device_id=partner, device_id_type=mesh_id)

    def greet(d, c):
        pc, pg = peer(d)
        pl.semaphore_signal(barrier, inc=1, device_id=(pg, pc * 2 + parity), device_id_type=mesh_id)
        return c

    lax.fori_loop(1, n, greet, 0)
    read = pltpu.make_async_copy(meas_ref.at[subset, pl.ds(g * rows, rows)], meas, meas_sem)
    read.start()
    kept = pltpu.make_async_copy(part_ref.at[:, parity], keep, keep_sem)
    kept.start()
    first_row = (p * groups + g) * rows
    mine = p // pairs
    line = lax.broadcasted_iota(jnp.int32, halves.shape[1:], 0)
    lane = lax.broadcasted_iota(jnp.int32, halves.shape[1:], 1)
    ray = lax.rem(first_row, NTILE) * RAYS_TILE + mine * (lines * 8) + ray_at(line, lane, tall)
    ray = (ray.astype(jnp.float32) + (0.5 - RAYS * 0.5)) * (1.0 / spread)
    a = first_row // NTILE
    early, rest = ray_sums(
        halves.shape[1:], table_ref[subset, 0, a], table_ref[subset, 1, a], table_ref[subset, 2, a], ray)
    fill_grid(base_ref, e_scr)
    pl.semaphore_wait(barrier, n)

    def put(i):
        slot = lax.rem(i, 2)
        return pltpu.make_async_copy(made.at[slot], made_hbm.at[pl.ds(i * MADE, MADE)], made_sem.at[slot])

    def make(i, c):
        @pl.when(i >= 2)
        def _():
            put(i - 2).wait()

        for k in range(MADE):
            b = frac_ref.shape[2] - made_hbm.shape[0] + i * MADE + k
            for a in range(ANG_SUB):
                made[lax.rem(i, 2), k, a * R:(a + 1) * R, :] = footprint(
                    e_scr[a * R:(a + 1) * R, :] + frac_ref[subset, a, b])
        put(i).start()
        return c

    steps = made_hbm.shape[0] // MADE
    early_steps = min(MADE_EARLY[subset], steps)

    def swap(d):
        pc = lax.rem(column + d, pairs)
        return pltpu.make_async_remote_copy(
            src_ref=part_ref.at[pc, 1 - parity], dst_ref=half.at[pc], send_sem=pair_send.at[d],
            recv_sem=pair_recv.at[d], device_id=partner, device_id_type=mesh_id)

    def to_owner(d):
        pc, pg = peer(d)
        return pltpu.make_async_remote_copy(
            src_ref=sums.at[pc, pg], dst_ref=inbox.at[column, g], send_sem=send_sem.at[d],
            recv_sem=recv_sem.at[d], device_id=(pg, pc * 2 + parity), device_id_type=mesh_id)

    def go_swap(d, c):
        swap(d).start()
        return c

    def go_column(i, c):
        pc = lax.rem(column + i, pairs)
        swap(i).wait_recv()
        sums[pc] = (keep[pc] + half[pc]).astype(sums.dtype)

        def go(d, c):
            to_owner(d).start()
            return c

        return lax.fori_loop(jnp.maximum(i * groups, 1), (i + 1) * groups, go, c)

    lax.fori_loop(0, pairs, go_swap, 0)
    kept.wait()
    lax.fori_loop(0, pairs, go_column, 0)
    halves[mine] = rest(early)
    trade = pltpu.make_async_remote_copy(
        src_ref=halves.at[mine], dst_ref=halves.at[mine], send_sem=rs_send, recv_sem=rs_recv,
        device_id=(g, lax.rem(p + pairs, 2 * pairs)), device_id_type=mesh_id)
    trade.start()

    lax.fori_loop(0, early_steps, make, 0)

    def got(d, c):
        to_owner(d).wait_recv()
        return c

    read.wait()
    wide = lines // rows
    lane_q = lax.broadcasted_iota(jnp.int32, (1, LANES), 1) // 8

    def retile(forth):
        def one(i, c):
            at = pl.ds(aligned(i * 8, 8), 8)
            for r, x in enumerate(spread_lanes(lines_scr[at, :], lane_q)):
                flat[sixteenth(0, r, not forth), :] = x
            out = flat[sixteenth(0, 0, forth), :]
            for r in range(1, 16):
                out = jnp.where(lane_q == r, flat[sixteenth(0, r, forth), :], out)
            lines_scr[at, :] = out
            return c

        if tall:
            lax.fori_loop(0, lines // 8, one, 0)

    for c in range(wide):
        lines_scr[pl.ds(c, rows, stride=wide), :] = meas[:, c * LANES:(c + 1) * LANES]
    retile(True)

    inbox[column, g] = sums[column, g]
    lax.fori_loop(1, n, got, 0)
    total = jnp.zeros(stage.shape, jnp.float32)
    for i in range(pairs):
        for j in range(groups):
            total = total + inbox[i, j].astype(jnp.float32)
    ray = ray_at(lax.broadcasted_iota(jnp.int32, stage.shape, 0),
                 lax.broadcasted_iota(jnp.int32, stage.shape, 1), tall)
    row = ray // RAYS_TILE
    live = jnp.zeros(stage.shape, jnp.int32)
    for r in range(rows):
        live = jnp.where(row == r, live_ref[subset, first_row + r], live)
    trade.wait()
    sums_of = jnp.concatenate([halves[0], halves[1]], axis=0)
    differ = lines_scr[...] - total / jnp.maximum(sums_of, 1.0)
    residual = jnp.where(ray - row * RAYS_TILE < live, differ, 0.0)
    lines_scr[...] = residual
    stage[...] = residual.astype(jnp.bfloat16)

    def to_all(d):
        pc, pg = peer(d)
        return pltpu.make_async_remote_copy(
            src_ref=stage, dst_ref=gathered.at[column, parity, g], send_sem=out_send.at[d],
            recv_sem=out_recv.at[d], device_id=(pg, pc * 2 + parity), device_id_type=mesh_id)

    def share(d):
        pc, pg = source(d)
        return pltpu.make_async_remote_copy(
            src_ref=gathered.at[pc, parity, pg], dst_ref=gathered.at[pc, parity, pg], send_sem=back_send.at[d],
            recv_sem=back_recv.at[d], device_id=partner, device_id_type=mesh_id)

    def go_all(d, c):
        to_all(d).start()
        return c

    def pass_on(d, c):
        to_all(d).wait_recv()
        share(d).start()
        return c

    def finish(d, c):
        share(d).wait()
        return c

    def sent(d, c):
        to_owner(d).wait_send()
        to_all(d).wait_send()
        return c

    def swapped(d, c):
        swap(d).wait_send()
        return c

    lax.fori_loop(1, n, go_all, 0)
    gathered[column, parity, g] = stage[...]
    share(0).start()
    lax.fori_loop(early_steps, steps, make, 0)
    retile(False)
    for c in range(wide):
        own_ref[:, c * LANES:(c + 1) * LANES] = lines_scr[pl.ds(c, rows, stride=wide), :]
    lax.fori_loop(1, n, pass_on, 0)
    lax.fori_loop(0, n, finish, 0)
    lax.fori_loop(1, n, sent, 0)
    lax.fori_loop(0, pairs, swapped, 0)
    for i in range(max(steps - 2, 0), steps):
        put(i).wait()


def exchange(subset, tall, partial, live, table, frac, measured, base, rows, groups, patches):
    pairs = patches // 2
    lines = rows * measured.shape[2] // LANES
    shape = (pairs, 2, groups, lines, LANES)
    n = pairs * groups
    wire = jnp.bfloat16 if subset < SUBSETS - 1 else jnp.float32
    dma = pltpu.SemaphoreType.DMA
    vmem = pl.BlockSpec(memory_space=pltpu.VMEM)
    full, own, made = pl.pallas_call(
        lambda *refs: exchange_kernel(subset, tall, *refs),
        in_specs=[pl.BlockSpec(memory_space=pl.ANY), smem(), smem(), smem(), pl.BlockSpec(memory_space=pl.ANY), vmem],
        out_specs=[vmem, vmem, pl.BlockSpec(memory_space=pl.ANY)],
        out_shape=[jax.ShapeDtypeStruct(shape, jnp.bfloat16),
                   jax.ShapeDtypeStruct((rows, measured.shape[2]), jnp.float32),
                   jax.ShapeDtypeStruct((frac.shape[2] // PARTS, LANES, VOX), jnp.bfloat16)],
        scratch_shapes=[pltpu.VMEM((pairs, groups, lines, LANES), jnp.float32),
                        pltpu.VMEM((pairs, groups, lines, LANES), jnp.float32),
                        pltpu.VMEM((pairs, groups, lines, LANES), wire),
                        pltpu.VMEM((pairs, groups, lines, LANES), wire),
                        pltpu.VMEM((lines, LANES), jnp.float32),
                        pltpu.VMEM((SPAN, LANES), jnp.float32),
                        pltpu.VMEM((2, lines // 2, LANES), jnp.float32),
                        pltpu.VMEM((rows, measured.shape[2]), jnp.float32),
                        pltpu.VMEM((lines, LANES), jnp.bfloat16),
                        pltpu.VMEM((LANES, VOX), jnp.float32),
                        pltpu.VMEM((2, MADE, LANES, VOX), jnp.bfloat16),
                        dma, dma, dma((pairs,)), dma((pairs,)), dma((n,)), dma((n,)), dma, dma,
                        dma((n,)), dma((n,)), dma((n,)), dma((n,)), dma((2,))],
        compiler_params=pltpu.CompilerParams(collective_id=subset, has_side_effects=True),
        name="exchange",
    )(partial.reshape(shape), live, table, frac, measured, base)
    return full.reshape(partial.shape), own, made


def smem():
    return pl.BlockSpec(memory_space=pltpu.SMEM)


def sweep(back, fore, tall, volume, lo, frac, win, made=None, residual=None, own=None):
    blocks = volume.shape[0]
    chunks = blocks // min(CHUNK, blocks // PARTS)
    lines = ANG_SUB * RAYS // 16
    vmem = pl.BlockSpec(memory_space=pltpu.VMEM)
    hbm = pl.BlockSpec(memory_space=pl.ANY)
    dma = pltpu.SemaphoreType.DMA
    f32 = jnp.float32
    given = [("lo", smem(), lo), ("frac", smem(), frac), ("win", smem(), win), ("vol_hbm", hbm, volume)]
    made_here = []
    scratch = [("vol", pltpu.VMEM(volume.shape, f32)),
               ("tall", pltpu.VMEM((ANG_SUB * TALL, LANES), f32)),
               ("flat", pltpu.VMEM((ANG_SUB * RAYS, LANES), f32)),
               ("tiles", pltpu.SMEM((ANG_SUB * TILES + 1,), jnp.int32)),
               ("starts", pltpu.SMEM((ANG_SUB + 1,), jnp.int32)),
               ("vol_sem", dma((chunks,)))]
    if fore is not None:
        base = geometry(fore)[0]
        grid = (np.repeat(base, R, axis=0) - np.tile(np.arange(R), ANG_SUB)[:, None]) * (1.0 / spread)
        given.append(("grid_hbm", hbm, grid.T.astype(np.float32)))
        made_here.append(("part", vmem, jax.ShapeDtypeStruct((lines, LANES), f32)))
        scratch += [("grid", pltpu.VMEM((VOX, LANES), f32)), ("grid_sem", dma)]
    if back is not None:
        given += [("made_hbm", hbm, made), ("base", vmem, geometry(back)[0]), ("residual", vmem, residual)]
        made_here.append(("out_hbm", hbm, jax.ShapeDtypeStruct(volume.shape, f32)))
        scratch += [("out", pltpu.VMEM(volume.shape, f32)),
                    ("made", pltpu.VMEM(made.shape, jnp.bfloat16)),
                    ("edges", pltpu.VMEM((ANG_SUB * R, VOX), f32)),
                    ("res", pltpu.VMEM(residual.shape, f32)),
                    ("out_sem", dma((chunks,))), ("made_sem", dma((made.shape[0] // MADE,)))]
    if fore is None:
        given.append(("own", vmem, own))
        made_here.append(("last", vmem, jax.ShapeDtypeStruct(own.shape, f32)))
    names = [x[0] for x in given + made_here + scratch]
    return pl.pallas_call(
        lambda *refs: sweep_kernel(back, fore, tall, names, *refs),
        in_specs=[x[1] for x in given],
        out_specs=[x[1] for x in made_here],
        out_shape=[x[2] for x in made_here],
        scratch_shapes=[x[1] for x in scratch],
        compiler_params=pltpu.CompilerParams(vmem_limit_bytes=VMEM_LIMIT),
        name="sweep",
    )(*[x[2] for x in given])


def ray_table():
    table = np.zeros((SUBSETS, 3, ANG_SUB), np.float64)
    for subset in range(SUBSETS):
        for a, t in enumerate(angles(subset)):
            small, big = sorted((abs(math.cos(t)), abs(math.sin(t))))
            table[subset, :, a] = big / spread, small / spread, spread / big
    return table.astype(np.float32)


def placing_kernel(place_ref, lo_ref, frac_ref, win_ref):
    half = IMG_BLK * BLK_SIDE * 0.5
    shape = lo_ref.shape[1:]
    place = jnp.broadcast_to(place_ref[...], shape)
    x = (place % IMG_BLK).astype(jnp.float32) * BLK_SIDE + (BLK_SIDE * 0.5 - half)
    y = (place // IMG_BLK).astype(jnp.float32) * BLK_SIDE + (BLK_SIDE * 0.5 - half)
    angle = lax.broadcasted_iota(jnp.int32, shape, 0)
    tile = lax.broadcasted_iota(jnp.int32, (TILES, shape[1]), 0)
    near = []
    for subset in range(SUBSETS):
        cosine = sine = jnp.zeros(shape, jnp.float32)
        for a, theta in enumerate(angles(subset)):
            cosine = jnp.where(angle == a, np.float32(math.cos(theta)), cosine)
            sine = jnp.where(angle == a, np.float32(math.sin(theta)), sine)
        z = x * cosine + y * sine + (RAYS * 0.5 - 0.5)
        low = jnp.floor(z)
        lo = low.astype(jnp.int32)
        lo_ref[subset] = lo
        frac_ref[subset] = (z - low) * (1.0 / spread)
        ends = (lo - PAD) // SPAN, (lo + R + PAD) // SPAN
        for a in range(ANG_SUB):
            hit = (ends[0][a:a + 1] == tile) | (ends[1][a:a + 1] == tile)
            near.append(jnp.where(hit, 1.0, 0.0))
    count = lax.dot_general(jnp.ones((8, shape[1]), jnp.bfloat16), jnp.concatenate(near, axis=0).astype(jnp.bfloat16),
                            (((1,), (1,)), ((), ())), preferred_element_type=jnp.float32)
    win_ref[...] = jnp.where(count[0:1] > 0.0, 1, 0)


def placing(place):
    shape = (SUBSETS, ANG_SUB, place.shape[0])
    return pl.pallas_call(
        placing_kernel,
        out_shape=[jax.ShapeDtypeStruct(shape, jnp.int32), jax.ShapeDtypeStruct(shape, jnp.float32),
                   jax.ShapeDtypeStruct((1, SUBSETS * ANG_SUB * TILES), jnp.int32)],
        name="placing",
    )(place.reshape(1, -1))


def shards(volume, block_place, measured, live_rays):
    groups = lax.axis_size("group")
    patches = lax.axis_size("patch")
    rows = ANG_SUB * NTILE // patches // groups
    lo, frac, win = placing(block_place)
    table = ray_table()
    tall = rows * RAYS_TILE % (2 * LANES) == 0
    estimate = volume
    (partial,) = sweep(None, 0, tall, estimate, lo, frac, win)
    for subset in range(SUBSETS):
        full, own, made = exchange(
            subset, tall, partial, live_rays, table, frac, measured, geometry(subset)[0], rows, groups, patches)
        if subset < SUBSETS - 1:
            partial, estimate = sweep(subset, subset + 1, tall, estimate, lo, frac, win, made, full)
        else:
            estimate, own = sweep(subset, None, tall, estimate, lo, frac, win, made, full, own)
    return (estimate, own[None])


def solution(mesh):
    return jax.shard_map(
        shards,
        mesh=mesh,
        in_specs=(
            P(("group", "patch"), None, None),
            P(("group", "patch")),
            P(None, "patch", None),
            P(),
        ),
        out_specs=(P(("group", "patch"), None, None), P("group", "patch", None)),
        check_vma=False,
    )
```
